32 devices in a mesh: dp: 8 (over y, x, core), fsdp: 4 (over z).
Axes of the slice: x: 2, y: 2, z: 4, core: 2. Of those that a mesh axis runs over, the one named last changes fastest.
Arguments:
- tokens: bfloat16 [32, 1024, 2048], P(('dp', 'fsdp')), may hold values from -6 to 6
- cotangent: bfloat16 [32, 1024, 2048], P(('dp', 'fsdp')), may hold values from -6 to 6
- doc_starts: int32 [32, 4], P(('dp', 'fsdp')), may hold values from 0 to 896, as said below
- active_len: int32 [32, 4], P(('dp', 'fsdp')), may hold values from 0 to 128, as said below
- ln1_gain: bfloat16 [2048], P(('dp', 'fsdp')), may hold values from 0.5 to 1.5
- ln1_bias: bfloat16 [2048], P(('dp', 'fsdp')), may hold values from -1 to 1
- q_weight: bfloat16 [2048, 2048], P(('dp', 'fsdp')), may hold values from -0.125 to 0.125
- q_bias: bfloat16 [2048], P(('dp', 'fsdp')), may hold values from -1.5 to 1.5
- k_weight: bfloat16 [2048, 2048], P(('dp', 'fsdp')), may hold values from -0.125 to 0.125
- v_weight: bfloat16 [2048, 2048], P(('dp', 'fsdp')), may hold values from -0.125 to 0.125
- v_bias: bfloat16 [2048], P(('dp', 'fsdp')), may hold values from -1.5 to 1.5
- o_weight: bfloat16 [2048, 2048], P(('dp', 'fsdp')), may hold values from -0.5 to 0.5
- o_bias: bfloat16 [2048], P(('dp', 'fsdp')), may hold values from -1.5 to 1.5
- ln2_gain: bfloat16 [2048], P(('dp', 'fsdp')), may hold values from 0.5 to 1.5
- ln2_bias: bfloat16 [2048], P(('dp', 'fsdp')), may hold values from -1 to 1
- up_weight: bfloat16 [2048, 8192], P(('dp', 'fsdp')), may hold values from -0.125 to 0.125
- up_bias: bfloat16 [8192], P(('dp', 'fsdp')), may hold values from -1.5 to 1.5
- down_weight: bfloat16 [8192, 2048], P(('dp', 'fsdp')), may hold values from -0.09375 to 0.09375
- down_bias: bfloat16 [2048], P(('dp', 'fsdp')), may hold values from -1.5 to 1.5
Outputs:
- layer_out: bfloat16 [32, 1024, 2048], P(('dp', 'fsdp'))
- input_grad: bfloat16 [32, 1024, 2048], P(('dp', 'fsdp'))
- grad_ln1_gain: float32 [2048], P(('dp', 'fsdp'))
- grad_ln1_bias: float32 [2048], P(('dp', 'fsdp'))
- grad_q_weight: float32 [2048, 2048], P(('dp', 'fsdp'))
- grad_q_bias: float32 [2048], P(('dp', 'fsdp'))
- grad_k_weight: float32 [2048, 2048], P(('dp', 'fsdp'))
- grad_v_weight: float32 [2048, 2048], P(('dp', 'fsdp'))
- grad_v_bias: float32 [2048], P(('dp', 'fsdp'))
- grad_o_weight: float32 [2048, 2048], P(('dp', 'fsdp'))
- grad_o_bias: float32 [2048], P(('dp', 'fsdp'))
- grad_ln2_gain: float32 [2048], P(('dp', 'fsdp'))
- grad_ln2_bias: float32 [2048], P(('dp', 'fsdp'))
- grad_up_weight: float32 [2048, 8192], P(('dp', 'fsdp'))
- grad_up_bias: float32 [8192], P(('dp', 'fsdp'))
- grad_down_weight: float32 [8192, 2048], P(('dp', 'fsdp'))
- grad_down_bias: float32 [2048], P(('dp', 'fsdp'))
The draws below stay inside these ranges and needn't reach their ends.
Inputs may be any that keep to these rules, and one draw needn't show every extreme that they name: `doc_starts`: each row holds 4 documents; starts rise from 0 at the first, every document spans 128 tokens or more, and the last ends at 1024; some row's last document starts at 896. `active_len`: 0 marks a document that exited before this layer; an active document has 64 or more active tokens, never more than its length. Over the rows with the same row index on the devices of one fsdp group, exactly 3 * 4 of the 4 * 4 documents are active.
All inputs are finite; a program needn't handle non-finite values.
Results may differ from the reference program's by a relative error of at most 0.013.
Values may be sent and summed in bfloat16 or wider, within the bound.
No kernel may reach another device: no remote copies, remote signals or barrier semaphores. Data moves between devices by JAX's collectives and lax.ppermute only.
A program may use at most 448 MiB of HBM per device.

```python
import jax
import jax.numpy as jnp
from jax import lax

D = 2048
HEADS = 32
HD = 64
FF = 8192
SLOT = 128
DOCS = 4
RECV = 3
ROWS_DEV = 1
ROW_LEN = 1024
ROWS = 32
N_DP = 8
N_FSDP = 4


def arrange(grid_values):
    shaped = grid_values.reshape(N_DP, ROWS_DEV, N_FSDP, DOCS).transpose(0, 2, 1, 3)
    return shaped.reshape(N_DP * N_FSDP * ROWS_DEV, DOCS).astype(jnp.int32)


def document_layout(key):
    group_count = N_DP * ROWS_DEV
    member_count = N_FSDP * DOCS
    key_cut, key_rank, key_span = jax.random.split(jax.random.fold_in(key, 11), 3)
    cuts = jnp.sort(jax.random.randint(key_cut, (group_count, N_FSDP, DOCS - 1), 0, DOCS * SLOT + 1), axis=-1)
    cuts = cuts.at[0, 0, DOCS - 2].set(DOCS * SLOT)
    edges = jnp.concatenate([jnp.zeros((group_count, N_FSDP, 1), jnp.int32), cuts.astype(jnp.int32), jnp.full((group_count, N_FSDP, 1), DOCS * SLOT, jnp.int32)], axis=-1)
    lengths = SLOT + edges[:, :, 1:] - edges[:, :, :-1]
    starts = jnp.cumsum(lengths, axis=-1) - lengths
    ranking = jax.vmap(lambda sub_key: jax.random.permutation(sub_key, member_count))(jax.random.split(key_rank, group_count))
    ranking = ranking.reshape(group_count, N_FSDP, DOCS)
    prefix = jax.random.randint(key_span, (group_count, N_FSDP, DOCS), SLOT // 2, SLOT + 1)
    prefix = jnp.where(ranking == 0, SLOT, prefix)
    prefix = jnp.where(ranking < N_FSDP * RECV, prefix, 0)
    return (arrange(starts), arrange(prefix))


def draw_doc_starts(key, part):
    return document_layout(key)[0]


def draw_active_len(key, part):
    return document_layout(key)[1]


def spiked(values, rng, source, target, blocks, factor):
    def block_of(dim):
        return (jnp.arange(values.shape[dim]) // (values.shape[dim] // blocks)).reshape((-1,) + (1,) * (values.ndim - 1 - dim))

    near = jax.random.permutation(rng, blocks)[block_of(target)]
    other_side = (block_of(target) + blocks // 2) % blocks
    return jnp.where((block_of(source) == near) | (block_of(source) == other_side), factor * values, values)


def shard_levels(stream_key, extent, pieces, low, largest):
    def one(dim, parts):
        draws = jax.random.uniform(jax.random.fold_in(jax.random.fold_in(stream_key, 6), dim), (parts,), jnp.float32, low / len(pieces), largest / len(pieces))
        return jnp.repeat(jnp.exp(draws), extent[dim] // parts).reshape((-1,) + (1,) * (len(extent) - dim - 1))

    gain = one(*pieces[0])
    for cut in pieces[1:]:
        gain = gain * one(*cut)
    return gain


def bell_draw(key, dims, deviation, most, shards=(), kind=jnp.bfloat16):
    values = jax.random.normal(key, dims, jnp.float32) * deviation
    if len(shards) > 0:
        values = shard_levels(key, dims, shards, -0.22, 0.18) * values
    return jnp.clip(values, min=-most, max=most).astype(kind)


def bell_draw_with(key, shape, width, bound, cuts, heavy, kind=jnp.bfloat16):
    array = width * jax.random.normal(key, shape, jnp.float32)
    if cuts:
        array = array * shard_levels(key, shape, cuts, -0.22, 0.18)
    return jnp.clip(spiked(array, jax.random.fold_in(key, 3), *heavy), -bound, bound).astype(kind)


def setup_inputs(seed: int = 0) -> dict:
    key_list = jax.random.split(jax.random.key(seed), 20)
    tokens = bell_draw(key_list[0], (ROWS, ROW_LEN, D), 1.0, 6.0, ((0, 32),))
    cotangent = bell_draw_with(key_list[1], (ROWS, ROW_LEN, D), 1.0, 6.0, ((0, 32),), (0, 2, 32, 2.75))
    doc_starts = draw_doc_starts(jax.random.fold_in(key_list[19], 71), 0)
    active_len = draw_active_len(jax.random.fold_in(key_list[19], 71), 0)
    ln1_gain = jnp.clip(1.0 + 0.1 * jax.random.normal(key_list[4], (D,), jnp.float32), 0.5, 1.5).astype(jnp.bfloat16)
    ln1_bias = bell_draw(key_list[5], (D,), 0.2, 1.0, ((0, 32),))
    q_weight = bell_draw(key_list[6], (D, D), D ** -0.5, 0.125, ((0, 32),))
    q_bias = bell_draw(key_list[7], (D,), 0.3, 1.5, ((0, 32),))
    k_weight = bell_draw(key_list[8], (D, D), D ** -0.5, 0.125, ((0, 32),))
    v_weight = bell_draw(key_list[9], (D, D), D ** -0.5, 0.125, ((0, 32),))
    v_bias = bell_draw(key_list[10], (D,), 0.3, 1.5, ((0, 32),))
    o_weight = bell_draw(key_list[11], (D, D), (D // 16) ** -0.5, 0.5, ((0, 32),))
    o_bias = bell_draw(key_list[12], (D,), 0.3, 1.5, ((0, 32),))
    ln2_gain = jnp.clip(1.0 + 0.1 * jax.random.normal(key_list[13], (D,), jnp.float32), 0.5, 1.5).astype(jnp.bfloat16)
    ln2_bias = bell_draw(key_list[14], (D,), 0.2, 1.0, ((0, 32),))
    up_weight = bell_draw(key_list[15], (D, FF), D ** -0.5, 0.125, ((0, 32),))
    up_bias = bell_draw(key_list[16], (FF,), 0.3, 1.5, ((0, 32),))
    down_weight = bell_draw(key_list[17], (FF, D), (FF // 2) ** -0.5, 0.09375, ((0, 32),))
    down_bias = bell_draw(key_list[18], (D,), 0.3, 1.5, ((0, 32),))
    return {"tokens": tokens, "cotangent": cotangent, "doc_starts": doc_starts, "active_len": active_len, "ln1_gain": ln1_gain, "ln1_bias": ln1_bias, "q_weight": q_weight, "q_bias": q_bias, "k_weight": k_weight, "v_weight": v_weight, "v_bias": v_bias, "o_weight": o_weight, "o_bias": o_bias, "ln2_gain": ln2_gain, "ln2_bias": ln2_bias, "up_weight": up_weight, "up_bias": up_bias, "down_weight": down_weight, "down_bias": down_bias}


@jax.custom_vjp
def low(v):
    return lax.optimization_barrier(v.astype(jnp.bfloat16)).astype(jnp.float32)

@jax.custom_vjp
def low_back(v):
    return v

def low_keep(v):
    return (low(v), None)

def low_pass(kept, grad):
    return (grad,)

def back_keep(v):
    return (v, None)

def back_low(kept, grad):
    return (low(grad),)
low.defvjp(low_keep, low_pass)
low_back.defvjp(back_keep, back_low)
EPSILON = 1e-05
MASKED = -1e+30
HIGHEST = lax.Precision.HIGHEST

def matmul(factor_one, factor_two):
    return jnp.dot(factor_one, factor_two, precision=HIGHEST, preferred_element_type=jnp.float32)

def layer_norm(row_values, norm_gain, norm_shift):
    centred = row_values - lax.optimization_barrier(jnp.mean(row_values, axis=-1, keepdims=True))
    variance = lax.optimization_barrier(jnp.mean(centred * centred, axis=-1, keepdims=True))
    return centred * lax.rsqrt(variance + EPSILON) * norm_gain + norm_shift

def layer_forward(params, slots):
    ln1_gain, ln1_bias, q_weight, q_bias, k_weight, v_weight, v_bias, o_weight, o_bias, ln2_gain, ln2_bias, up_weight, up_bias, down_weight, down_bias = params
    slot_count = slots.shape[0]
    flat_rows = slots.reshape(slot_count * SLOT, D)
    normed_one = low(layer_norm(flat_rows, ln1_gain, ln1_bias))
    query = low_back(low(matmul(normed_one, q_weight) + q_bias))
    key_rows = low_back(low(matmul(normed_one, k_weight)))
    value_rows = low_back(low(matmul(normed_one, v_weight) + v_bias))
    head_shape = (slot_count, SLOT, HEADS, HD)
    scores = low_back(jnp.einsum('sqhd,skhd->shqk', query.reshape(head_shape), key_rows.reshape(head_shape), precision=HIGHEST) * 0.125)
    causal = jnp.arange(SLOT)[:, None] >= jnp.arange(SLOT)[None, :]
    scores = jnp.where(causal, scores, MASKED)
    exponent = jnp.exp(scores - lax.optimization_barrier(jnp.max(scores, axis=-1, keepdims=True)))
    probs = low(exponent / lax.optimization_barrier(jnp.sum(exponent, axis=-1, keepdims=True)))
    context = jnp.einsum('shqk,skhd->sqhd', probs, value_rows.reshape(head_shape), precision=HIGHEST)
    context = low_back(low(context.reshape(slot_count * SLOT, D)))
    hidden = flat_rows + low_back(matmul(context, o_weight) + o_bias)
    normed_two = low(layer_norm(hidden, ln2_gain, ln2_bias))
    inner = low_back(matmul(normed_two, up_weight) + up_bias)
    activated = low(jax.nn.gelu(inner, approximate=False))
    result = hidden + matmul(activated, down_weight) + down_bias
    return result.reshape(slot_count, SLOT, D)

def take_slots(source, doc_starts, active_len):
    row_count = source.shape[0]
    offsets = jnp.arange(SLOT, dtype=jnp.int32)
    flat_index = (doc_starts[:, :, None] + offsets[None, None, :]).reshape(row_count, DOCS * SLOT)
    picked = jnp.take_along_axis(source.astype(jnp.float32), flat_index[:, :, None], axis=1)
    inside = (offsets[None, None, :] < active_len[:, :, None]).reshape(row_count, DOCS * SLOT)
    picked = jnp.where(inside[:, :, None], picked, 0.0)
    return picked.reshape(row_count * DOCS, SLOT, D)

def place_back(slot_values, doc_starts, active_len, fallback):
    row_count = fallback.shape[0]
    position = jnp.arange(ROW_LEN, dtype=jnp.int32)
    member = lax.optimization_barrier(jnp.sum((position[None, :, None] >= doc_starts[:, None, :]).astype(jnp.int32), axis=-1)) - 1
    offset = position[None, :] - jnp.take_along_axis(doc_starts, member, axis=1)
    inside = offset < jnp.take_along_axis(active_len, member, axis=1)
    flat_index = member * SLOT + jnp.minimum(offset, SLOT - 1)
    picked = jnp.take_along_axis(slot_values.reshape(row_count, DOCS * SLOT, D), flat_index[:, :, None], axis=1)
    return jnp.where(inside[:, :, None], picked, fallback)

def reference(tokens, cotangent, doc_starts, active_len, ln1_gain, ln1_bias, q_weight, q_bias, k_weight, v_weight, v_bias, o_weight, o_bias, ln2_gain, ln2_bias, up_weight, up_bias, down_weight, down_bias):
    params = tuple((weight_item.astype(jnp.float32) for weight_item in (ln1_gain, ln1_bias, q_weight, q_bias, k_weight, v_weight, v_bias, o_weight, o_bias, ln2_gain, ln2_bias, up_weight, up_bias, down_weight, down_bias)))
    block_slots = 32
    inputs = take_slots(tokens, doc_starts, active_len)
    block_count = inputs.shape[0] // block_slots
    inputs = inputs.reshape(block_count, block_slots, SLOT, D)
    seeds = take_slots(cotangent, doc_starts, active_len).reshape(block_count, block_slots, SLOT, D)

    def one_block(running, block_pair):
        block_in, block_seed = block_pair
        block_out, pull_back = jax.vjp(layer_forward, params, block_in)
        param_grads, slot_grads = pull_back(block_seed)
        return (jax.tree.map(jnp.add, running, param_grads), (block_out, slot_grads))
    zero_grads = tuple((jnp.zeros_like(weight_item) for weight_item in params))
    grads, (slot_outputs, slot_grads) = lax.scan(one_block, zero_grads, (inputs, seeds))
    slot_out = slot_outputs.reshape(-1, SLOT, D).astype(jnp.bfloat16)
    slot_back = slot_grads.reshape(-1, SLOT, D).astype(jnp.bfloat16)
    layer_out = place_back(slot_out, doc_starts, active_len, tokens)
    input_grad = place_back(slot_back, doc_starts, active_len, cotangent)
    return (layer_out, input_grad, grads[0], grads[1], grads[2], grads[3], grads[4], grads[5], grads[6], grads[7], grads[8], grads[9], grads[10], grads[11], grads[12], grads[13], grads[14])
```

```python
import jax
import jax.numpy as jnp
from jax import lax
from jax.sharding import PartitionSpec as P

HEADS = 32
HD = 64
SLOT = 128
TEAM = 4

EPSILON = 1e-05
MASKED = -1e30
ROOT_HALF = 0.7071067811865476
DENSITY_SCALE = 0.3989422804014327
BF = jnp.bfloat16
F32 = jnp.float32
BOTH = ("dp", "fsdp")


def dot(a, b, ca, cb):
    return lax.dot_general(a, b, (((ca,), (cb,)), ((), ())), preferred_element_type=F32)


def smooth_gate(values):
    return values * (0.5 + 0.5 * lax.erf(values * ROOT_HALF))


def smooth_slope(values):
    return (
        0.5
        + 0.5 * lax.erf(values * ROOT_HALF)
        + values * DENSITY_SCALE * jnp.exp(-0.5 * values * values)
    )


def norm_parts(row_block, gain, shift):
    centred = row_block - jnp.mean(row_block, axis=-1, keepdims=True)
    inverse = lax.rsqrt(jnp.mean(centred * centred, axis=-1, keepdims=True) + EPSILON)
    normal = centred * inverse
    return normal, inverse, (normal * gain + shift).astype(BF)


def norm_back(grad_out, normal, inverse, gain):
    scaled = grad_out * gain
    centre = jnp.mean(scaled, axis=-1, keepdims=True)
    projected = jnp.mean(scaled * normal, axis=-1, keepdims=True)
    return inverse * (scaled - centre - normal * projected)


def team_swap(a, flip):
    size = lax.axis_size("dp")
    return lax.ppermute(a, "dp", [(i, i ^ flip) for i in range(size)])


def team_gather(own):
    two = jnp.concatenate([own, team_swap(own, 2)], axis=0)
    return jnp.concatenate([two, team_swap(two, 1)], axis=0)


def team_scatter(partial):
    half = partial.shape[0] // 2
    other = team_swap(partial[half:].astype(BF), 1)
    two = partial[:half] + other.astype(F32)
    quarter = half // 2
    last = team_swap(two[quarter:].astype(BF), 2)
    return two[:quarter] + last.astype(F32)


def by_team(stacked, member):
    odd = (member & 1) == 1
    high = (member & 2) == 2
    a = [jnp.where(odd, stacked[i ^ 1], stacked[i]) for i in range(4)]
    return [jnp.where(high, a[i ^ 2], a[i]) for i in range(4)]


def ring_order(size):
    return list(range(0, size, 2)) + list(range(1, size, 2))[::-1]


def outer_pass(a):
    outer = lax.axis_size("dp") // TEAM
    order = ring_order(outer)
    pairs = []
    for p, o in enumerate(order):
        nxt = order[(p + 1) % outer]
        pairs += [(o * TEAM + t, nxt * TEAM + t) for t in range(TEAM)]
    return lax.ppermute(a, "dp", pairs)


def outer_place(me):
    outer = lax.axis_size("dp") // TEAM
    order = ring_order(outer)
    place = [0] * outer
    for p, o in enumerate(order):
        place[o] = p
    return jnp.asarray(order, jnp.int32), jnp.asarray(place, jnp.int32)[me]


def outer_gather(a, me):
    outer = lax.axis_size("dp") // TEAM
    if outer == 1:
        return a[None]
    if outer == 2:
        b = outer_pass(a)
        first = me == 0
        return jnp.stack([jnp.where(first, a, b), jnp.where(first, b, a)])
    order, place = outer_place(me)
    whole = jnp.zeros((outer,) + a.shape, a.dtype)
    whole = lax.dynamic_update_index_in_dim(whole, a, me, 0)
    moving = a
    for step in range(1, outer):
        moving = outer_pass(moving)
        source = order[(place - step) % outer]
        whole = lax.dynamic_update_index_in_dim(whole, moving, source, 0)
    return whole


def outer_scatter(blocks, me):
    outer = lax.axis_size("dp") // TEAM
    if outer == 1:
        return blocks[0]
    order, place = outer_place(me)
    moving = lax.dynamic_index_in_dim(blocks, order[(place - 1) % outer], 0, False)
    for step in range(1, outer):
        moving = outer_pass(moving)
        mine = lax.dynamic_index_in_dim(blocks, order[(place - 1 - step) % outer], 0, False)
        moving = (moving.astype(F32) + mine.astype(F32)).astype(BF)
    return moving


def deal_columns(shard, member, outer, depth):
    r = shard.shape[0]
    parts = shard.reshape(r, outer, TEAM, depth, -1)
    got = []
    for flip in range(TEAM):
        piece = lax.dynamic_index_in_dim(parts, member ^ flip, 2, False).reshape(r, -1)
        got.append(piece if flip == 0 else team_swap(piece, flip))
    return jnp.concatenate(by_team(got, member), axis=0)


def return_columns(block, member, outer, depth):
    r, c = block.shape[0] // TEAM, block.shape[1]
    parts = block.reshape(TEAM, r, c)
    got = []
    for flip in range(TEAM):
        piece = lax.dynamic_index_in_dim(parts, member ^ flip, 0, False)
        got.append(piece if flip == 0 else team_swap(piece, flip))
    cols = jnp.stack([g.reshape(r, outer, depth, -1) for g in by_team(got, member)], axis=2)
    return cols.reshape(r, -1).astype(F32)


def score_block(query_heads, key_heads):
    scores = jnp.einsum("sqhd,skhd->shqk", query_heads, key_heads, preferred_element_type=F32) * 0.125
    causal = jnp.arange(SLOT)[:, None] >= jnp.arange(SLOT)[None, :]
    return jnp.where(causal, scores, MASKED), causal


def body(
    tokens,
    cotangent,
    doc_starts,
    active_len,
    ln1_gain,
    ln1_bias,
    q_weight,
    q_bias,
    k_weight,
    v_weight,
    v_bias,
    o_weight,
    o_bias,
    ln2_gain,
    ln2_bias,
    up_weight,
    up_bias,
    down_weight,
    down_bias,
):
    depth = lax.axis_size("fsdp")
    devices = lax.axis_size("dp") * depth
    outer = lax.axis_size("dp") // TEAM
    dp = lax.axis_index("dp")
    member, me = dp % TEAM, dp // TEAM
    groups, row_len, width = tokens.shape
    docs = doc_starts.shape[1]
    r = q_weight.shape[0]
    hidden_block = down_weight.shape[0]
    part_width = width // TEAM

    vectors = (ln1_gain, ln1_bias, o_bias, ln2_gain, ln2_bias, down_bias, q_bias, v_bias, up_bias)
    packed = lax.all_gather(jnp.concatenate(vectors), BOTH, axis=0, tiled=False)
    edges = [0]
    for v in vectors:
        edges.append(edges[-1] + v.shape[0])
    pieces = [packed[:, edges[i] : edges[i + 1]] for i in range(len(vectors))]
    gain1, shift1, bias_o, gain2, shift2, bias_down = [p.reshape(-1).astype(F32) for p in pieces[:6]]

    def member_part(p):
        whole = p.reshape(outer, TEAM, depth, -1)
        return lax.dynamic_index_in_dim(whole, member, 1, False).reshape(-1).astype(F32)

    bias_q, bias_v, bias_up = [member_part(p) for p in pieces[6:]]

    position = jnp.arange(row_len, dtype=jnp.int32)
    offset = jnp.arange(SLOT, dtype=jnp.int32)
    wanted = doc_starts[:, :, None] + offset
    live = offset < active_len[:, :, None]
    chosen = (wanted[..., None] == position) & live[..., None]
    chosen = chosen.reshape(groups, docs * SLOT, row_len)
    select = chosen.astype(BF)
    covered = jnp.any(chosen, axis=1)

    def pack(source):
        picked = jnp.einsum("gst,gtd->gsd", select, source, preferred_element_type=F32)
        return picked.reshape(groups * docs * SLOT, width).astype(BF)

    def unpack(slot_rows, fallback):
        blocks = slot_rows.astype(BF).reshape(groups, docs * SLOT, width)
        placed = jnp.einsum("gst,gsd->gtd", select, blocks, preferred_element_type=F32).astype(BF)
        return jnp.where(covered[..., None], placed, fallback)

    x_rows = pack(tokens)
    residual = x_rows.astype(F32)
    normal1, inverse1, a_own = norm_parts(residual, gain1, shift1)
    a_all = team_gather(a_own)

    qkv_deal = jnp.concatenate(
        [deal_columns(w, member, outer, depth) for w in (q_weight, k_weight, v_weight)], axis=1
    )
    up_deal = deal_columns(up_weight, member, outer, depth)

    def depth_gather(a):
        return lax.all_gather(a, "fsdp", axis=0, tiled=True)

    def natural(stacked):
        c = stacked.shape[-1]
        return stacked.reshape(outer, depth, TEAM, r, c).transpose(0, 2, 1, 3, 4).reshape(width, c)

    w_qkv = natural(outer_gather(depth_gather(qkv_deal), me))
    w_o = outer_gather(depth_gather(o_weight), me).reshape(part_width, width)
    w_up = natural(outer_gather(depth_gather(up_deal), me))
    w_down = outer_gather(depth_gather(down_weight), me).reshape(-1, width)

    g_rows = pack(cotangent)
    g_all = team_gather(g_rows)

    rows = a_all.shape[0]
    slots = rows // SLOT
    heads = part_width // HD
    zero = jnp.zeros_like(bias_q)
    qkv = (dot(a_all, w_qkv, 1, 0) + jnp.concatenate([bias_q, zero, bias_v])).astype(BF)
    shape = (slots, SLOT, heads, HD)
    q, k, v = [qkv[:, i * part_width : (i + 1) * part_width].reshape(shape) for i in range(3)]
    scores, causal = score_block(q, k)
    row_max = jnp.max(scores, axis=-1, keepdims=True)
    exponent = jnp.exp(scores - row_max)
    total = jnp.sum(exponent, axis=-1, keepdims=True)
    probs = exponent / total
    probs_low = probs.astype(BF)
    context = jnp.einsum("shqk,skhd->sqhd", probs_low, v, preferred_element_type=F32)
    context = context.reshape(rows, part_width).astype(BF)
    hidden = residual + team_scatter(dot(context, w_o, 1, 0)) + bias_o
    normal2, inverse2, b_own = norm_parts(hidden, gain2, shift2)
    b_all = team_gather(b_own)
    inner = dot(b_all, w_up, 1, 0) + bias_up
    activated = smooth_gate(inner).astype(BF)
    y_rows = hidden + team_scatter(dot(activated, w_down, 1, 0)) + bias_down
    layer_out = unpack(y_rows, tokens)

    def depth_scatter(a):
        return lax.psum_scatter(a, "fsdp", scatter_dimension=0, tiled=True)

    def reduce_rows(grad):
        blocks = grad.astype(BF).reshape(outer, -1, grad.shape[1])
        return depth_scatter(outer_scatter(blocks, me))

    def reduce_natural(grad):
        c = grad.shape[1]
        blocks = grad.astype(BF).reshape(outer, TEAM, depth, r, c).transpose(0, 2, 1, 3, 4)
        return depth_scatter(outer_scatter(blocks.reshape(outer, -1, c), me))

    grad_down = reduce_rows(dot(activated, g_all, 0, 0)).astype(F32)
    d_inner_float = dot(g_all, w_down, 1, 1) * smooth_slope(inner)
    d_inner = d_inner_float.astype(BF)
    d_normed2 = team_scatter(dot(d_inner, w_up, 1, 1))
    grad_up = reduce_natural(dot(b_all, d_inner, 0, 0))
    grad_up = return_columns(grad_up, member, outer, depth)
    g_float = g_rows.astype(F32)
    d_hidden = g_float + norm_back(d_normed2, normal2, inverse2, gain2)
    d_out = d_hidden.astype(BF)
    d_out_all = team_gather(d_out)

    d_context = dot(d_out_all, w_o, 1, 1).astype(BF).reshape(shape)
    grad_o = reduce_rows(dot(context, d_out_all, 0, 0)).astype(F32)
    d_probs = jnp.einsum("sqhd,skhd->shqk", d_context, v, preferred_element_type=F32)
    row_dot = jnp.sum(probs * d_probs, axis=-1, keepdims=True)
    d_scores = (probs * (d_probs - row_dot)).astype(BF)
    d_q = (jnp.einsum("shqk,skhd->sqhd", d_scores, k, preferred_element_type=F32) * 0.125).astype(BF)
    d_k = (jnp.einsum("shqk,sqhd->skhd", d_scores, q, preferred_element_type=F32) * 0.125).astype(BF)
    d_v = jnp.einsum("shqk,sqhd->skhd", probs_low, d_context, preferred_element_type=F32).astype(BF)
    d_qkv = jnp.concatenate([d.reshape(rows, part_width) for d in (d_q, d_k, d_v)], axis=1)
    grad_qkv = reduce_natural(dot(a_all, d_qkv, 0, 0))
    grad_q, grad_k, grad_v = [
        return_columns(grad_qkv[:, i * part_width : (i + 1) * part_width], member, outer, depth)
        for i in range(3)
    ]
    d_normed1 = team_scatter(dot(d_qkv, w_qkv, 1, 1))
    d_input = d_hidden + norm_back(d_normed1, normal1, inverse1, gain1)
    input_grad = unpack(d_input, cotangent)

    qkv_sum = jnp.sum(d_qkv, axis=0, dtype=F32)
    whole_sums = [
        jnp.sum(d_normed1 * normal1, axis=0),
        jnp.sum(d_normed1, axis=0),
        jnp.sum(d_out, axis=0, dtype=F32),
        jnp.sum(d_normed2 * normal2, axis=0),
        jnp.sum(d_normed2, axis=0),
        jnp.sum(g_float, axis=0),
    ]
    part_sums = [
        qkv_sum[:part_width],
        qkv_sum[2 * part_width :],
        jnp.sum(d_inner, axis=0, dtype=F32),
    ]
    is_mine = (jnp.arange(TEAM) == member)[None, :, None, None]

    def widen(s):
        blocks = s.reshape(outer, 1, depth, -1)
        return jnp.where(is_mine, blocks, 0.0).reshape(devices, -1)

    table = jnp.concatenate([s.reshape(devices, -1) for s in whole_sums] + [widen(s) for s in part_sums], axis=1)
    small = lax.psum_scatter(table, BOTH, scatter_dimension=0, tiled=True)[0]
    cuts = [small[edges[i] : edges[i + 1]] for i in range(len(vectors))]
    g_gain1, g_shift1, g_bias_o, g_gain2, g_shift2, g_bias_down, g_bias_q, g_bias_v, g_bias_up = cuts
    return (
        layer_out,
        input_grad,
        g_gain1,
        g_shift1,
        grad_q,
        g_bias_q,
        grad_k,
        grad_v,
        g_bias_v,
        grad_o,
        g_bias_o,
        g_gain2,
        g_shift2,
        grad_up,
        g_bias_up,
        grad_down,
        g_bias_down,
    )


def solution(mesh):
    rows2 = P(BOTH, None)
    rows1 = P(BOTH)
    rows3 = P(BOTH, None, None)
    in_specs = (
        rows3,
        rows3,
        rows2,
        rows2,
        rows1,
        rows1,
        rows2,
        rows1,
        rows2,
        rows2,
        rows1,
        rows2,
        rows1,
        rows1,
        rows1,
        rows2,
        rows1,
        rows2,
        rows1,
    )
    out_specs = (rows3, rows3) + tuple(
        rows2 if kind == "w" else rows1 for kind in "vvwvwwvwvvvwvwv"
    )
    return jax.shard_map(body, mesh=mesh, in_specs=in_specs, out_specs=out_specs, check_vma=False)
```

```python
import functools

import jax
import jax.numpy as jnp
from jax import lax
from jax.experimental import pallas as pl
from jax.experimental.pallas import tpu as pltpu
from jax.sharding import Mesh
from jax.sharding import PartitionSpec as P

HD = 64
SLOT = 128
TEAM = 4
TILE = 256
HASTE = 1000
VMEM = 48 * 2**20

EPSILON = 1e-05
MASKED = -1e30
ROOT_HALF = 0.7071067811865476
DENSITY_SCALE = 0.3989422804014327
BF = jnp.bfloat16
F32 = jnp.float32
ALL = ("outer", "team", "fsdp")
SPREAD = ("outer", "fsdp")


def dot(a, b, ca, cb):
    return lax.dot_general(a, b, (((ca,), (cb,)), ((), ())), preferred_element_type=F32)


def team_swap(a, flip):
    return lax.ppermute(a, "team", [(i, i ^ flip) for i in range(TEAM)])


def ring_order(size):
    return list(range(0, size, 2)) + list(range(1, size, 2))[::-1]


def outer_pass(a):
    outer = lax.axis_size("outer")
    order = ring_order(outer)
    return lax.ppermute(a, "outer", [(o, order[(p + 1) % outer]) for p, o in enumerate(order)])


def outer_place(me):
    outer = lax.axis_size("outer")
    order = ring_order(outer)
    place = [0] * outer
    for p, o in enumerate(order):
        place[o] = p
    return jnp.asarray(order, jnp.int32), jnp.asarray(place, jnp.int32)[me]


def outer_halves(a, me):
    outer = lax.axis_size("outer")
    if outer == 2:
        return [a, outer_pass(a)]
    order, place = outer_place(me)
    whole = jnp.zeros((outer,) + a.shape[1:], a.dtype)
    whole = lax.dynamic_update_slice_in_dim(whole, a, me, 0)
    moving = a
    for step in range(1, outer):
        moving = outer_pass(moving)
        whole = lax.dynamic_update_slice_in_dim(whole, moving, order[(place - step) % outer], 0)
    return [whole[: outer // 2], whole[outer // 2 :]]


def outer_scatter(blocks, me):
    outer = lax.axis_size("outer")
    order, place = outer_place(me)
    moving = lax.dynamic_slice_in_dim(blocks, order[(place - 1) % outer], 1, 0)
    for step in range(1, outer):
        moving = outer_pass(moving)
        mine = lax.dynamic_slice_in_dim(blocks, order[(place - 1 - step) % outer], 1, 0)
        moving = (moving.astype(F32) + mine.astype(F32)).astype(BF)
    return moving


def by_team(stacked, member):
    odd = (member & 1) == 1
    high = (member & 2) == 2
    a = [jnp.where(odd, stacked[i ^ 1], stacked[i]) for i in range(4)]
    return [jnp.where(high, a[i ^ 2], a[i]) for i in range(4)]


def deal_columns(shards, member, outer, depth):
    r = shards[0].shape[0]
    parts = [w.reshape(r, outer, TEAM, depth, -1) for w in shards]
    got = []
    for flip in range(TEAM):
        piece = jnp.concatenate(
            [lax.dynamic_index_in_dim(w, member ^ flip, 2, False).reshape(r, -1) for w in parts], axis=1
        )
        got.append(piece if flip == 0 else team_swap(piece, flip))
    return jnp.concatenate(by_team(got, member), axis=0)


def return_columns(block, member, outer, depth, shares):
    r, c = block.shape[0] // TEAM, block.shape[1] // shares
    parts = block.reshape(TEAM, r, shares * c)
    got = []
    for flip in range(TEAM):
        piece = lax.dynamic_index_in_dim(parts, member ^ flip, 0, False)
        got.append(piece if flip == 0 else team_swap(piece, flip))
    got = by_team(got, member)
    result = []
    for i in range(shares):
        cols = jnp.stack([g[:, i * c : (i + 1) * c].reshape(r, outer, depth, -1) for g in got], axis=2)
        result.append(cols.reshape(r, -1).astype(F32))
    return result


def shift_pass(a, axis, step):
    size = lax.axis_size(axis)
    return lax.ppermute(a, axis, [(i, (i + step) % size) for i in range(size)])


def gather_small(vector, member, me, layer):
    depth = lax.axis_size("fsdp")
    outer = lax.axis_size("outer")
    a = vector[None]
    a = jnp.concatenate([a if s == 0 else shift_pass(a, "fsdp", s) for s in range(depth)])
    a = jnp.concatenate([a if s == 0 else shift_pass(a, "outer", s) for s in range(outer)])
    a = jnp.concatenate([a if f == 0 else team_swap(a, f) for f in range(TEAM)])
    index = jnp.arange(TEAM * outer * depth, dtype=jnp.int32)
    flip, step, drop = index // (outer * depth), index // depth % outer, index % depth
    source = ((me - step) % outer * TEAM + (member ^ flip)) * depth + (layer - drop) % depth
    place = (index[:, None] == source[None, :]).astype(BF)
    return dot(place, a, 1, 0)


def reduce_small(table, member, me, layer):
    depth = lax.axis_size("fsdp")
    outer = lax.axis_size("outer")
    blocks = table.reshape(outer, TEAM, depth, -1)
    total = lax.dynamic_index_in_dim(blocks, member, 1, False)
    for flip in range(1, TEAM):
        total = total + team_swap(lax.dynamic_index_in_dim(blocks, member ^ flip, 1, False), flip)
    blocks = total
    total = lax.dynamic_index_in_dim(blocks, me, 0, False)
    for step in range(1, outer):
        total = total + shift_pass(
            lax.dynamic_index_in_dim(blocks, (me + step) % outer, 0, False), "outer", step
        )
    blocks = total
    total = lax.dynamic_index_in_dim(blocks, layer, 0, False)
    for step in range(1, depth):
        total = total + shift_pass(
            lax.dynamic_index_in_dim(blocks, (layer + step) % depth, 0, False), "fsdp", step
        )
    return total


def params():
    return pltpu.CompilerParams(vmem_limit_bytes=VMEM)


def cost(flops, nbytes, exps=0):
    return pl.CostEstimate(
        flops=flops // HASTE, bytes_accessed=nbytes // HASTE, transcendentals=exps // HASTE
    )


def kernel_call(kernel, prefetch, grid, specs, args, out_specs, out_shape, estimate, hold=()):
    count = len(prefetch) + len(args)

    def run(*refs):
        kernel(*refs[:count], *refs[count + len(hold) :])

    return pl.pallas_call(
        run,
        grid_spec=pltpu.PrefetchScalarGridSpec(
            num_scalar_prefetch=len(prefetch),
            grid=grid,
            in_specs=list(specs) + [pl.BlockSpec(memory_space=pl.ANY)] * len(hold),
            out_specs=out_specs,
        ),
        out_shape=out_shape,
        compiler_params=params(),
        cost_estimate=estimate,
    )(*prefetch, *args, *hold)


def pin(value, *hold):
    def run(*refs):
        del refs

    anywhere = pl.BlockSpec(memory_space=pl.ANY)
    return pl.pallas_call(
        run,
        in_specs=[anywhere] * (1 + len(hold)),
        out_specs=anywhere,
        out_shape=jax.ShapeDtypeStruct(value.shape, value.dtype),
        input_output_aliases={0: 0},
        compiler_params=params(),
        cost_estimate=cost(0, 0),
    )(value, *hold)


def still(shape, first=0):
    return pl.BlockSpec(shape, lambda *_: (first,) + (0,) * (len(shape) - 1))


def in_order(block):
    h, z, t, r, n = block.shape
    rows = [block[o, :, i].reshape(z * r, n) for o in range(h) for i in range(t)]
    return jnp.concatenate(rows, axis=0) if len(rows) > 1 else rows[0]


def half_of(start, which, size):
    at = start if which == 0 else 1 - start
    return pl.ds(pl.multiple_of(at * size, size), size)


def forward_kernel(style, count, spread, cuts, per_cut, start_ref, *refs):
    pieces, weights, rest = refs[:count], refs[count : count + 2 * cuts], refs[count + 2 * cuts :]
    start = start_ref[0]
    load = in_order if spread else (lambda b: b.reshape(-1, b.shape[-1]))
    firsts, seconds = load(weights[0][...]), load(weights[1][...])
    for i in range(1, cuts):
        late = pl.program_id(0) >= i * per_cut
        firsts = jnp.where(late, load(weights[2 * i][...]), firsts)
        seconds = jnp.where(late, load(weights[2 * i + 1][...]), seconds)
    size = firsts.shape[0]
    if style == "bare":
        outs = rest
    else:
        bias, outs = rest[0][...], rest[1:]
    at = 0
    for ref in pieces:
        views = [ref] if len(ref.shape) == 2 else [ref.at[i] for i in range(ref.shape[0])]
        for view in views:
            value = dot(view[:, half_of(start, 0, size)], firsts, 1, 0)
            value = value + dot(view[:, half_of(start, 1, size)], seconds, 1, 0)
            if style == "bare":
                outs[at][...] = value.astype(BF)
            elif style == "plain":
                outs[0][at] = (value + bias).astype(BF)
            else:
                value = value + bias
                phi = 0.5 + 0.5 * lax.erf(value * ROOT_HALF)
                outs[0][at] = (value * phi).astype(BF)
                outs[1][at] = (phi + value * DENSITY_SCALE * jnp.exp(-0.5 * value * value)).astype(BF)
            at += 1


def forward_product(pieces, weights, start, bias=None, style="plain", pick=None, rows=512, hold=()):
    whole = len(weights[0]) == 1
    sample = weights[0][0]
    spread = sample.ndim == 5
    paired = sample.ndim == 4
    cuts = len(weights)
    n = sample.shape[-1] * cuts
    tile = min(n // cuts, TILE)
    per_cut = n // cuts // tile
    stack = pieces[0].ndim == 3
    if stack:
        total = pick[1] if pick else pieces[0].shape[0]
        specs = [still((total,) + pieces[0].shape[1:], pick[0] if pick else 0)]
        k = pieces[0].shape[2]
    else:
        total, k = len(pieces), pieces[0].shape[1]
        specs = [still(p.shape) for p in pieces]
    lead = sample.shape[:-1]
    args = list(pieces)
    for i, pair in enumerate(weights):

        def at(j, s, i=i):
            return (0,) * len(lead) + (jnp.clip(j - i * per_cut, 0, per_cut - 1),)

        if paired:
            z, _, b, _ = sample.shape
            specs += [pl.BlockSpec((z, 1, b, tile), lambda j, s, h=h: (0, h, 0, j)) for h in range(2)]
            args += [pair[0], pair[0]]
        elif whole:
            specs += [pl.BlockSpec((lead[0] // 2, tile), lambda j, s, h=h: (h, j)) for h in range(2)]
            args += [pair[0], pair[0]]
        else:
            specs += [pl.BlockSpec(lead + (tile,), at)] * 2
            args += list(pair)
    if style != "bare":
        specs.append(pl.BlockSpec((1, tile), lambda j, s: (0, j)))
        args.append(bias.reshape(1, n))
    if style == "bare":
        out_specs = [pl.BlockSpec((rows, tile), lambda j, s: (0, j))] * total
        out_shape = [jax.ShapeDtypeStruct((rows, n), BF)] * total
    else:
        copies = 2 if style == "gate" else 1
        out_specs = [pl.BlockSpec((total, rows, tile), lambda j, s: (0, 0, j))] * copies
        out_shape = [jax.ShapeDtypeStruct((total, rows, n), BF)] * copies
    return kernel_call(
        functools.partial(forward_kernel, style, len(pieces), spread, cuts, per_cut),
        [start],
        (n // tile,),
        specs,
        args,
        out_specs,
        out_shape,
        cost(2 * total * rows * k * n, 2 * (total * rows * (k + n) + k * n)),
        hold,
    )


def back_kernel(style, count, shares, per_half, start_ref, *refs):
    pieces, weights, rest = refs[:count], refs[count : count + 2 * shares], refs[count + 2 * shares :]
    late = pl.program_id(0) >= per_half
    chosen = []
    for i in range(shares):
        w0, w1 = weights[2 * i][...], weights[2 * i + 1][...]
        if len(w0.shape) == 5:
            w0, w1 = in_order(w0), in_order(w1)
        elif len(w0.shape) == 4:
            w0, w1 = w0[0, 0], w1[0, 0]
        chosen.append(jnp.where(late, w1, w0))
    views = []
    for ref in pieces:
        views += [ref] if len(ref.shape) == 2 else [ref.at[i] for i in range(ref.shape[0])]
    width = chosen[0].shape[1]
    total = None
    for at, view in enumerate(views):
        value = dot(view[:, :width], chosen[0], 1, 1)
        for i in range(1, shares):
            value = value + dot(view[:, i * width : (i + 1) * width], chosen[i], 1, 1)
        if style == "slope":
            low = (value * rest[0][at].astype(F32)).astype(BF)
            rest[1][at] = low
            part = jnp.sum(low.astype(F32), axis=0, keepdims=True)
            total = part if total is None else total + part
        elif style == "plain":
            rest[0][at] = value.astype(BF)
        else:
            rest[at][...] = value.astype(BF)
    if style == "slope":
        rest[2][...] = total


def back_product(pieces, weights, start, style="plain", slope=None, pick=None, rows=512, hold=()):
    shares = len(weights)
    sample = weights[0][0]
    k = sample.shape[-1]
    half_rows = 1
    for d in sample.shape[:-1]:
        half_rows *= d
    whole = len(weights[0]) == 1
    if whole:
        half_rows //= 2
    n = 2 * half_rows
    tile = min(half_rows, TILE)
    per_half = half_rows // tile
    stack = pieces[0].ndim == 3
    if stack:
        total = pick[1] if pick else pieces[0].shape[0]
        specs = [still((total,) + pieces[0].shape[1:], pick[0] if pick else 0)]
    else:
        total = len(pieces)
        specs = [still(p.shape) for p in pieces]
    if sample.ndim == 4:
        tile = sample.shape[2]
        per_half = sample.shape[0]
        block = (1, 1, tile, k)
    elif sample.ndim == 5:
        h, z, t, r, _ = sample.shape
        group = max(1, tile // (z * r))
        tile = group * z * r
        per_half = half_rows // tile
        each = t // group
        block = (1, z, group, r, k)

        def at(j):
            return (j // each, 0, j % each, 0, 0)
    else:
        block = (tile, k)

        def at(j):
            return (j, 0)

    if sample.ndim == 4:
        first = pl.BlockSpec(block, lambda j, s: (jnp.minimum(j, per_half - 1), 0, 0, 0))
        second = pl.BlockSpec(block, lambda j, s: (jnp.maximum(j - per_half, 0), 1, 0, 0))
    else:
        first = pl.BlockSpec(block, lambda j, s: at(jnp.minimum(j, per_half - 1)))
        second = pl.BlockSpec(block, lambda j, s: at(jnp.maximum(j - per_half, 0) + (per_half if whole else 0)))
    args = list(pieces)
    for w in weights:
        specs += [first, second]
        args += [w[0], w[-1]]

    def column(j, s):
        return lax.rem(s[0] * per_half + j, 2 * per_half)

    stacked = pl.BlockSpec((total, rows, tile), lambda j, s: (0, 0, column(j, s)))
    stack_shape = jax.ShapeDtypeStruct((total, rows, n), BF)
    if style == "slope":
        specs.append(stacked)
        args.append(slope)
        out_specs = [stacked, pl.BlockSpec((1, tile), lambda j, s: (0, column(j, s)))]
        out_shape = [stack_shape, jax.ShapeDtypeStruct((1, n), F32)]
    elif style == "plain":
        out_specs, out_shape = [stacked], [stack_shape]
    else:
        out_specs = [pl.BlockSpec((rows, tile), lambda j, s: (0, column(j, s)))] * total
        out_shape = [jax.ShapeDtypeStruct((rows, n), BF)] * total
    return kernel_call(
        functools.partial(back_kernel, style, len(pieces), shares, per_half),
        [start],
        (2 * per_half,),
        specs,
        args,
        out_specs,
        out_shape,
        cost(2 * total * rows * k * n * shares, 2 * (total * rows * (k * shares + n) + k * n)),
        hold,
    )


def weight_kernel(left_count, right_count, start_ref, *refs):
    lefts, rights, out = refs[:left_count], refs[left_count : left_count + right_count], refs[-1]

    def views(group):
        found = []
        for ref in group:
            found += [ref] if len(ref.shape) == 2 else [ref.at[i] for i in range(ref.shape[0])]
        return found

    total = None
    for a, b in zip(views(lefts), views(rights)):
        part = dot(a[...], b[...], 0, 0)
        total = part if total is None else total + part
    low = total.astype(BF)
    if len(out.shape) == 2:
        out[...] = low
    else:
        h, z, t, r, n = out.shape
        for o in range(h):
            for i in range(t):
                base = (o * t + i) * z * r
                out[o, :, i] = low[base : base + z * r].reshape(z, r, n)


def weight_product(left, right, start, which, spread=None, cut=(0, 1, 1), tile=512, hold=()):
    def spec(group, width, index):
        found = []
        for a in group:
            if a.ndim == 2:
                found.append(pl.BlockSpec((a.shape[0], width), lambda j, s: (0, index(j, s))))
            else:
                found.append(pl.BlockSpec(a.shape[:2] + (width,), lambda j, s: (0, 0, index(j, s))))
        return found

    half = left[0].shape[-1] // (1 if which is None else 2)
    share = right[0].shape[-1] // cut[2]
    n = share * (cut[1] - cut[0])
    tile = min(tile, share)
    skip = cut[0] * (share // tile)
    rows = sum(a.shape[0] if a.ndim == 2 else a.shape[0] * a.shape[1] for a in left)
    specs = spec(left, half, lambda j, s: 0 if which is None else s[0] if which == 0 else 1 - s[0])
    specs += spec(right, tile, lambda j, s: j + skip)
    shape = (half, n) if spread is None else spread + (n,)
    block = shape[:-1] + (tile,)
    return kernel_call(
        functools.partial(weight_kernel, len(left), len(right)),
        [start],
        (n // tile,),
        specs,
        [*left, *right],
        pl.BlockSpec(block, lambda j, s: (0,) * (len(block) - 1) + (j,)),
        jax.ShapeDtypeStruct(shape, BF),
        cost(2 * rows * half * n, 2 * (rows * (half + n) + half * n)),
        hold,
    )


def pair_masks():
    lane = lax.broadcasted_iota(jnp.int32, (1, 2 * HD), 1)
    low = jnp.where(lane < HD, 1.0, 0.0).astype(BF)
    high = jnp.where(lane < HD, 0.0, 1.0).astype(BF)
    return low, high


def pair_probs(q_two, k):
    scores = dot(q_two, k, 1, 1) * 0.125
    row = lax.broadcasted_iota(jnp.int32, scores.shape, 0) & (SLOT - 1)
    column = lax.broadcasted_iota(jnp.int32, scores.shape, 1)
    scores = jnp.where(row >= column, scores, MASKED)
    exponent = jnp.exp(scores - jnp.max(scores, axis=-1, keepdims=True))
    return exponent / jnp.sum(exponent, axis=-1, keepdims=True)


def attend_kernel(q_ref, k_ref, v_ref, context_ref):
    low, high = pair_masks()
    for at in range(0, context_ref.shape[1], 2 * HD):
        q, k, v = [ref[:, at : at + 2 * HD] for ref in (q_ref, k_ref, v_ref)]
        probs = pair_probs(jnp.concatenate([q * low, q * high], axis=0), k).astype(BF)
        context = dot(probs[:SLOT], v * low, 1, 0) + dot(probs[SLOT:], v * high, 1, 0)
        context_ref[:, at : at + 2 * HD] = context.astype(BF)


def attend_back_kernel(q_ref, k_ref, v_ref, grad_ref, out_ref, sum_ref):
    part = grad_ref.shape[1]
    low, high = pair_masks()

    @pl.when(pl.program_id(0) == 0)
    def _():
        sum_ref[...] = jnp.zeros_like(sum_ref)

    for at in range(0, part, 2 * HD):
        q, k, v, grad = [ref[:, at : at + 2 * HD] for ref in (q_ref, k_ref, v_ref, grad_ref)]
        q_two = jnp.concatenate([q * low, q * high], axis=0)
        g_two = jnp.concatenate([grad * low, grad * high], axis=0)
        probs = pair_probs(q_two, k)
        d_probs = dot(g_two, v, 1, 1)
        row_dot = jnp.sum(probs * d_probs, axis=-1, keepdims=True)
        d_scores = (probs * (d_probs - row_dot)).astype(BF)
        d_q = dot(d_scores[:SLOT], k * low, 1, 0) + dot(d_scores[SLOT:], k * high, 1, 0)
        d_k = dot(d_scores, q_two, 0, 0)
        d_v = dot(probs.astype(BF), g_two, 0, 0)
        for i, value in enumerate((d_q * 0.125, d_k * 0.125, d_v)):
            where = slice(i * part + at, i * part + at + 2 * HD)
            value = value.astype(BF)
            out_ref[:, where] = value
            sum_ref[:, where] += jnp.sum(value.astype(F32), axis=0, keepdims=True)


def attend(q, k, v, hold=()):
    rows, part = q.shape
    one = pl.BlockSpec((SLOT, part), lambda i: (i, 0))
    return kernel_call(
        attend_kernel,
        [],
        (rows // SLOT,),
        [one] * 3,
        [q, k, v],
        one,
        jax.ShapeDtypeStruct((rows, part), BF),
        cost(32 * rows * SLOT * part, 8 * rows * part, rows * SLOT * part // HD),
        hold,
    )


def attend_back(q, k, v, grad, first, hold=()):
    rows, part = grad.shape
    one = pl.BlockSpec((SLOT, part), lambda i: (i, 0))
    shifted = pl.BlockSpec((SLOT, part), lambda i: (i + first, 0))
    return kernel_call(
        attend_back_kernel,
        [],
        (rows // SLOT,),
        [shifted] * 3 + [one],
        [q, k, v, grad],
        [pl.BlockSpec((SLOT, 3 * part), lambda i: (i, 0)), still((1, 3 * part))],
        [jax.ShapeDtypeStruct((rows, 3 * part), BF), jax.ShapeDtypeStruct((1, 3 * part), F32)],
        cost(80 * rows * SLOT * part, 14 * rows * part, rows * SLOT * part // HD),
        hold,
    )


def normal_of(values):
    centred = values - jnp.mean(values, axis=-1, keepdims=True)
    inverse = lax.rsqrt(jnp.mean(centred * centred, axis=-1, keepdims=True) + EPSILON)
    return centred * inverse, inverse


def rows_of(refs):
    total = refs[0][...].astype(F32)
    for ref in refs[1:]:
        total = total + ref[...].astype(F32)
    return total


def norm_kernel(x_ref, gain_ref, shift_ref, out_ref):
    normal, _ = normal_of(x_ref[...].astype(F32))
    out_ref[...] = (normal * gain_ref[...] + shift_ref[...]).astype(BF)


def join_norm_kernel(count, *refs):
    bias, gain, shift, hidden_ref, out_ref = refs[count:]
    hidden = rows_of(refs[:count]) + bias[...]
    hidden_ref[...] = hidden
    normal, _ = normal_of(hidden)
    out_ref[...] = (normal * gain[...] + shift[...]).astype(BF)


def join_kernel(count, *refs):
    refs[count + 1][...] = (rows_of(refs[:count]) + refs[count][...]).astype(BF)


def norm_back_kernel(count, *refs):
    source, carry, gain, grad_ref, low_ref, sums = refs[count:]
    grad = rows_of(refs[:count])
    normal, inverse = normal_of(source[...].astype(F32))
    scaled = grad * gain[...]
    centre = jnp.mean(scaled, axis=-1, keepdims=True)
    projected = jnp.mean(scaled * normal, axis=-1, keepdims=True)
    carried = carry[...].astype(F32)
    result = carried + inverse * (scaled - centre - normal * projected)
    grad_ref[...] = result.astype(grad_ref.dtype)
    low = result.astype(BF)
    low_ref[...] = low

    @pl.when(pl.program_id(0) == 0)
    def _():
        sums[...] = jnp.zeros_like(sums)

    for i, value in enumerate((grad * normal, grad, low.astype(F32), carried)):
        sums[i : i + 1] += jnp.sum(value, axis=0, keepdims=True)


def add_kernel(a_ref, b_ref, out_ref):
    out_ref[...] = (a_ref[...].astype(F32) + b_ref[...].astype(F32)).astype(BF)


def add_low(a, b, hold=()):
    width = a.shape[-1]
    flat = [x.reshape(-1, width) for x in (a, b)]
    rows = flat[0].shape[0]
    step = min(rows, 256)
    one = pl.BlockSpec((step, width), lambda i: (i, 0))
    result = kernel_call(
        add_kernel,
        [],
        (rows // step,),
        [one, one],
        flat,
        one,
        jax.ShapeDtypeStruct((rows, width), BF),
        cost(rows * width, 6 * rows * width),
        hold,
    )
    return result.reshape(a.shape)


def row_call(kernel, blocks, vectors, outs, sums=0, step=128, hold=()):
    rows, width = blocks[0].shape
    one = pl.BlockSpec((step, width), lambda i: (i, 0))
    out_specs = [one] * len(outs)
    out_shape = [jax.ShapeDtypeStruct((rows, width), d) for d in outs]
    if sums:
        out_specs.append(still((sums, width)))
        out_shape.append(jax.ShapeDtypeStruct((sums, width), F32))
    return kernel_call(
        kernel,
        [],
        (rows // step,),
        [one] * len(blocks) + [still((1, width))] * len(vectors),
        [*blocks, *[v.reshape(1, width) for v in vectors]],
        out_specs,
        out_shape,
        cost(20 * rows * width, 16 * rows * width),
        hold,
    )


def body(
    tokens,
    cotangent,
    doc_starts,
    active_len,
    ln1_gain,
    ln1_bias,
    q_weight,
    q_bias,
    k_weight,
    v_weight,
    v_bias,
    o_weight,
    o_bias,
    ln2_gain,
    ln2_bias,
    up_weight,
    up_bias,
    down_weight,
    down_bias,
):
    depth = lax.axis_size("fsdp")
    outer = lax.axis_size("outer")
    devices = outer * TEAM * depth
    member, me = lax.axis_index("team"), lax.axis_index("outer")
    layer = lax.axis_index("fsdp")
    start = (me if outer == 2 else jnp.zeros_like(me)).reshape(1)
    groups, row_len, width = tokens.shape
    docs = doc_starts.shape[1]
    r = q_weight.shape[0]
    part_width = width // TEAM
    rows = groups * docs * SLOT

    zero_bias = jnp.zeros((part_width,), F32)

    def depth_gather(a):
        return lax.all_gather(a, "fsdp", axis=0, tiled=True)

    def columns(a, i, n):
        c = a.shape[1] // n
        return a[:, i * c : (i + 1) * c]

    def stored(block):
        return block.reshape(1, depth, TEAM, r, block.shape[1])

    def flat(block):
        return block[None]

    def both_halves(block, *hold):
        return outer_halves(pin(block, *hold) if hold else block, me)

    def flatten(halves):
        return [h.reshape(-1, h.shape[-1]) for h in halves]

    qkv_deal = deal_columns((q_weight, k_weight, v_weight), member, outer, depth)
    block_q, block_k, block_v = [stored(depth_gather(columns(qkv_deal, i, 3))) for i in range(3)]
    w_q, w_k = [both_halves(b) for b in (block_q, block_k)]
    block_o = flat(depth_gather(o_weight))

    vectors = (ln1_gain, ln1_bias, o_bias, ln2_gain, ln2_bias, down_bias, q_bias, v_bias, up_bias)
    packed = gather_small(jnp.concatenate(vectors), member, me, layer)
    edges = [0]
    for v in vectors:
        edges.append(edges[-1] + v.shape[0])
    pieces = [packed[:, edges[i] : edges[i + 1]] for i in range(len(vectors))]
    gain1, shift1, bias_o, gain2, shift2, bias_down = [p.reshape(-1) for p in pieces[:6]]

    def member_part(p):
        whole = p.reshape(outer, TEAM, depth, -1)
        return lax.dynamic_index_in_dim(whole, member, 1, False).reshape(-1)

    bias_q, bias_v, bias_up = [member_part(p) for p in pieces[6:]]

    position = jnp.arange(row_len, dtype=jnp.int32)
    offset = jnp.arange(SLOT, dtype=jnp.int32)
    wanted = doc_starts[:, :, None] + offset
    live = offset < active_len[:, :, None]
    chosen = (wanted[..., None] == position) & live[..., None]
    chosen = chosen.reshape(groups, docs * SLOT, row_len)
    select = chosen.astype(BF)
    covered = jnp.any(chosen, axis=1)

    def pack(source):
        picked = jnp.einsum("gst,gtd->gsd", select, source, preferred_element_type=F32)
        return picked.reshape(rows, width).astype(BF)

    def unpack(slot_rows, fallback):
        blocks = slot_rows.reshape(groups, docs * SLOT, width)
        placed = jnp.einsum("gst,gsd->gtd", select, blocks, preferred_element_type=F32).astype(BF)
        return jnp.where(covered[..., None], placed, fallback)

    class Order:
        last = ()

        def step(self, kernel, *args, hold=(), **kw):
            result = kernel(*args, hold=self.last + tuple(hold), **kw)
            self.last = (jax.tree.leaves(result)[-1],)
            return result

    order = Order()

    def begin(weights):
        return jnp.zeros_like(start) if len(weights[0]) == 1 and outer != 2 else start

    def forward(pieces, weights, *rest, **kw):
        return order.step(forward_product, pieces, weights, begin(weights), *rest, rows=rows, **kw)

    def back(pieces, weights, **kw):
        return order.step(back_product, pieces, weights, begin(weights), rows=rows, **kw)

    def weight_grad(left, right, which, **kw):
        return order.step(weight_product, left, right, start, which, **kw)

    def by_rows(kernel, blocks, *args, **kw):
        return order.step(row_call, kernel, blocks, *args, **kw)

    def add(a, b, **kw):
        return order.step(add_low, a, b, **kw)

    def team_gather(own, *hold):
        across = team_swap(own, 2)
        if hold:
            across = pin(across, *hold)
        return [own, across, team_swap(own, 1), team_swap(across, 1)]

    def send_far(parts):
        return [team_swap(p, 1) for p in parts]

    def join_near(near, far, **kw):
        across = add(near[1], far[1], **kw)
        return [near[0], far[0], team_swap(across, 2), across]

    x_rows = pack(tokens)
    down_pair = jnp.stack([down_weight, outer_pass(down_weight)])[None]
    (a_own,) = by_rows(norm_kernel, [x_rows], [gain1, shift1], [BF], hold=[down_pair])
    up_deal = deal_columns((pin(up_weight, a_own),), member, outer, depth)
    a_all = team_gather(pin(a_own, block_o), w_q[1], w_k[1], up_deal)
    block_up = [stored(depth_gather(columns(up_deal, i, 2))) for i in range(2)]
    if outer == 2:
        w_down = [[depth_gather(down_pair)]]
    else:
        w_down = [[lax.all_gather(down_weight, SPREAD, axis=0, tiled=True)]]
    g_rows = pack(cotangent)
    g_all = team_gather(pin(g_rows, a_all[1]))

    wide = TEAM * rows
    q = forward(a_all, [w_q], bias_q)[0]
    k = forward(a_all, [w_k], zero_bias)[0]
    w_v = both_halves(block_v)
    v = forward(a_all, [w_v], bias_v)[0]
    w_o = flatten(both_halves(block_o))
    q, k, v = [s.reshape(wide, part_width) for s in (q, k, v)]
    context = order.step(attend, q, k, v).reshape(TEAM, rows, part_width)
    o_far = send_far(forward([context], [w_o], style="bare", pick=(1, 2), hold=[g_all[1]]))
    o_near = forward([context], [w_o], style="bare", pick=(0, 2))
    w_up = [both_halves(block_up[0], context)]
    *o_parts, o_across = join_near(o_near, o_far)
    hidden, b_own = by_rows(
        functools.partial(join_norm_kernel, 4),
        [x_rows] + o_parts,
        [bias_o, gain2, shift2],
        [F32, BF],
        hold=[w_up[0][1]],
    )
    w_up.append(both_halves(block_up[1], b_own))
    b_all = team_gather(b_own, w_up[1][1])

    active, slope = forward(b_all, w_up, bias_up, style="gate")

    def depth_scatter(a):
        return lax.psum_scatter(a, "fsdp", scatter_dimension=0, tiled=True)

    def send_away(away, *hold):
        if outer != 2:
            return away
        return outer_pass(pin(away, *hold) if hold else away)

    def settle(sent, mine, **kw):
        c = mine.shape[-1]
        if outer == 2:
            total = add(sent, mine, **kw)
        else:
            both = jnp.concatenate([mine.reshape(outer // 2, -1, c), sent.reshape(outer // 2, -1, c)])
            total = outer_scatter(both, me)
        return depth_scatter(total.reshape(-1, c))

    spread = (outer // 2, depth, TEAM, r)

    def settle_whole(grad):
        return lax.psum_scatter(grad, SPREAD, scatter_dimension=0, tiled=True)

    grad_down = [settle_whole(weight_grad([active], g_all, None, cut=(0, 1, 2)))]
    d_inner, sum_inner = back(g_all, w_down, style="slope", slope=slope)
    n_far = send_far(back([d_inner], w_up, style="bare", pick=(1, 2)))
    n_near = back([d_inner], w_up, style="bare", pick=(0, 2))
    n_parts = join_near(n_near, n_far)[:3]
    up_sent = [send_away(weight_grad(b_all, [d_inner], 1, spread=spread, cut=(0, 1, 2)))]
    grad_down.append(settle_whole(weight_grad([active], g_all, None, cut=(1, 2, 2))))
    up_sent.append(send_away(weight_grad(b_all, [d_inner], 1, spread=spread, cut=(1, 2, 2))))
    up_mine = [weight_grad(b_all, [d_inner], 0, spread=spread, cut=(0, 1, 2))]
    d_hidden, d_out, sums2 = by_rows(
        functools.partial(norm_back_kernel, 3), n_parts + [hidden, g_rows], [gain2], [F32, BF], sums=4
    )
    y_far = send_far(forward([active], w_down, style="bare", pick=(1, 2), hold=[grad_down[0]]))
    y_near = forward([active], w_down, style="bare", pick=(0, 2))
    up_mine.append(weight_grad(b_all, [d_inner], 0, spread=spread, cut=(1, 2, 2)))
    d_out_all = team_gather(d_out, up_sent[0], up_mine[1])

    (d_near,) = back(d_out_all[:2], [w_o])
    grad_up = [settle(up_sent[0], up_mine[0])]
    *y_parts, y_across = join_near(y_near, y_far)
    (d_far,) = back(d_out_all[2:], [w_o], hold=[grad_down[1]])
    q_far, sum_far = order.step(attend_back, q, k, v, d_far.reshape(2 * rows, -1), 2 * rows // SLOT)
    q_far = q_far.reshape(2, rows, -1)
    a_far = send_far(back([q_far], [w_q, w_k, w_v], style="bare"))
    grad_up.append(settle(up_sent[1], up_mine[1]))
    o_sent = send_away(weight_grad([context], d_out_all, 1))
    o_mine = weight_grad([context], d_out_all, 0)
    q_near, sum_near = order.step(attend_back, q, k, v, d_near.reshape(2 * rows, -1), 0, hold=[grad_up[0]])
    q_near = q_near.reshape(2, rows, -1)
    grad_o = settle(o_sent, o_mine)
    a_near = back([q_near], [w_q, w_k, w_v], style="bare")
    a_parts = join_near(a_near, a_far, hold=[y_parts[2]])[:3]
    parts = ((0, 1, 3), (1, 3, 3))
    d_both = [q_near, q_far]
    qkv_sent = [
        send_away(weight_grad(a_all, d_both, 1, spread=spread, cut=parts[0], hold=[grad_up[1]])),
        send_away(weight_grad(a_all, d_both, 1, spread=spread, cut=parts[1], hold=[grad_o])),
    ]
    grad_q = settle(qkv_sent[0], weight_grad(a_all, d_both, 0, spread=spread, cut=parts[0]))
    (y_rows,) = by_rows(functools.partial(join_kernel, 4), [hidden] + y_parts, [bias_down], [BF])
    layer_out = unpack(y_rows, tokens)
    (grad_up,) = return_columns(jnp.concatenate(grad_up, axis=1), member, outer, depth, 1)
    held = [a_parts[2], layer_out, grad_up]
    kv_mine = weight_grad(a_all, d_both, 0, spread=spread, cut=parts[1], hold=held)
    grad_kv = settle(qkv_sent[1], kv_mine)
    _, d_input, sums1 = by_rows(
        functools.partial(norm_back_kernel, 3), a_parts + [x_rows, d_hidden], [gain1], [BF, BF], sums=4
    )
    sum_qkv = sum_far + sum_near
    grad_o = grad_o.astype(F32)
    input_grad = unpack(d_input, cotangent)
    grad_down = jnp.concatenate([g.astype(F32) for g in grad_down], axis=1)
    (grad_q,) = return_columns(grad_q, member, outer, depth, 1)
    grad_k, grad_v = return_columns(grad_kv, member, outer, depth, 2)

    whole_sums = [sums1[0], sums1[1], sums2[2], sums2[0], sums2[1], sums2[3]]
    part_sums = [sum_qkv[0, :part_width], sum_qkv[0, 2 * part_width :], sum_inner[0]]
    is_mine = (jnp.arange(TEAM) == member)[None, :, None, None]

    def widen(s):
        blocks = s.reshape(outer, 1, depth, -1)
        return jnp.where(is_mine, blocks, 0.0).reshape(devices, -1)

    table = jnp.concatenate([s.reshape(devices, -1) for s in whole_sums] + [widen(s) for s in part_sums], axis=1)
    small = reduce_small(table, member, me, layer)
    cuts = [small[edges[i] : edges[i + 1]] for i in range(len(vectors))]
    g_gain1, g_shift1, g_bias_o, g_gain2, g_shift2, g_bias_down, g_bias_q, g_bias_v, g_bias_up = cuts
    return (
        layer_out,
        input_grad,
        g_gain1,
        g_shift1,
        grad_q,
        g_bias_q,
        grad_k,
        grad_v,
        g_bias_v,
        grad_o,
        g_bias_o,
        g_gain2,
        g_shift2,
        grad_up,
        g_bias_up,
        grad_down,
        g_bias_down,
    )


def solution(mesh):
    outer = mesh.shape["dp"] // TEAM
    devices = mesh.devices.reshape(outer, TEAM, mesh.shape["fsdp"])
    fine = Mesh(devices, ALL)
    kinds = {"t": P(ALL, None, None), "w": P(ALL, None), "v": P(ALL)}
    vectors = "vvwvwwvwvvvwvwv"
    in_specs = tuple(kinds[c] for c in "ttww" + vectors)
    out_specs = tuple(kinds[c] for c in "tt" + vectors)
    return jax.shard_map(body, mesh=fine, in_specs=in_specs, out_specs=out_specs, check_vma=False)
```

```python
import functools

import jax
import jax.numpy as jnp
from jax import lax
from jax.experimental import pallas as pl
from jax.experimental.pallas import tpu as pltpu
from jax.sharding import Mesh
from jax.sharding import PartitionSpec as P

HD = 64
SLOT = 128
TEAM = 4
TILE = 256
HASTE = 1000
VMEM = 48 * 2**20

EPSILON = 1e-05
MASKED = -1e30
ROOT_HALF = 0.7071067811865476
DENSITY_SCALE = 0.3989422804014327
BF = jnp.bfloat16
F32 = jnp.float32
ALL = ("outer", "team", "fsdp")
SPREAD = ("outer", "fsdp")


def dot(a, b, ca, cb):
    return lax.dot_general(a, b, (((ca,), (cb,)), ((), ())), preferred_element_type=F32)


def team_swap(a, flip):
    return lax.ppermute(a, "team", [(i, i ^ flip) for i in range(TEAM)])


def ring_order(size):
    return list(range(0, size, 2)) + list(range(1, size, 2))[::-1]


def outer_pass(a):
    outer = lax.axis_size("outer")
    order = ring_order(outer)
    return lax.ppermute(a, "outer", [(o, order[(p + 1) % outer]) for p, o in enumerate(order)])


def outer_place(me):
    outer = lax.axis_size("outer")
    order = ring_order(outer)
    place = [0] * outer
    for p, o in enumerate(order):
        place[o] = p
    return jnp.asarray(order, jnp.int32), jnp.asarray(place, jnp.int32)[me]


def outer_halves(a, me):
    outer = lax.axis_size("outer")
    if outer == 2:
        return [a, outer_pass(a)]
    order, place = outer_place(me)
    whole = jnp.zeros((outer,) + a.shape[1:], a.dtype)
    whole = lax.dynamic_update_slice_in_dim(whole, a, me, 0)
    moving = a
    for step in range(1, outer):
        moving = outer_pass(moving)
        whole = lax.dynamic_update_slice_in_dim(whole, moving, order[(place - step) % outer], 0)
    return [whole[: outer // 2], whole[outer // 2 :]]


def outer_scatter(blocks, me):
    outer = lax.axis_size("outer")
    order, place = outer_place(me)
    moving = lax.dynamic_slice_in_dim(blocks, order[(place - 1) % outer], 1, 0)
    for step in range(1, outer):
        moving = outer_pass(moving)
        mine = lax.dynamic_slice_in_dim(blocks, order[(place - 1 - step) % outer], 1, 0)
        moving = (moving.astype(F32) + mine.astype(F32)).astype(BF)
    return moving


def by_team(stacked, member):
    odd = (member & 1) == 1
    high = (member & 2) == 2
    a = [jnp.where(odd, stacked[i ^ 1], stacked[i]) for i in range(4)]
    return [jnp.where(high, a[i ^ 2], a[i]) for i in range(4)]


def deal_columns(shards, member, outer, depth):
    r = shards[0].shape[0]
    parts = [w.reshape(r, outer, TEAM, depth, -1) for w in shards]
    got = []
    for flip in range(TEAM):
        piece = jnp.concatenate(
            [lax.dynamic_index_in_dim(w, member ^ flip, 2, False).reshape(r, -1) for w in parts], axis=1
        )
        got.append(piece if flip == 0 else team_swap(piece, flip))
    return jnp.concatenate(by_team(got, member), axis=0)


def return_columns(block, member, outer, depth, shares):
    r, c = block.shape[0] // TEAM, block.shape[1] // shares
    parts = block.reshape(TEAM, r, shares * c)
    got = []
    for flip in range(TEAM):
        piece = lax.dynamic_index_in_dim(parts, member ^ flip, 0, False)
        got.append(piece if flip == 0 else team_swap(piece, flip))
    got = by_team(got, member)
    result = []
    for i in range(shares):
        cols = jnp.stack([g[:, i * c : (i + 1) * c].reshape(r, outer, depth, -1) for g in got], axis=2)
        result.append(cols.reshape(r, -1).astype(F32))
    return result


def shift_pass(a, axis, step):
    size = lax.axis_size(axis)
    return lax.ppermute(a, axis, [(i, (i + step) % size) for i in range(size)])


def gather_small(vector, member, me, layer):
    depth = lax.axis_size("fsdp")
    outer = lax.axis_size("outer")
    a = vector[None]
    a = jnp.concatenate([a if s == 0 else shift_pass(a, "fsdp", s) for s in range(depth)])
    a = jnp.concatenate([a if s == 0 else shift_pass(a, "outer", s) for s in range(outer)])
    a = jnp.concatenate([a if f == 0 else team_swap(a, f) for f in range(TEAM)])
    index = jnp.arange(TEAM * outer * depth, dtype=jnp.int32)
    flip, step, drop = index // (outer * depth), index // depth % outer, index % depth
    source = ((me - step) % outer * TEAM + (member ^ flip)) * depth + (layer - drop) % depth
    place = (index[:, None] == source[None, :]).astype(BF)
    return dot(place, a, 1, 0)


def reduce_small(table, member, me, layer):
    depth = lax.axis_size("fsdp")
    outer = lax.axis_size("outer")
    blocks = table.reshape(outer, TEAM, depth, -1)
    total = lax.dynamic_index_in_dim(blocks, member, 1, False)
    for flip in range(1, TEAM):
        total = total + team_swap(lax.dynamic_index_in_dim(blocks, member ^ flip, 1, False), flip)
    blocks = total
    total = lax.dynamic_index_in_dim(blocks, me, 0, False)
    for step in range(1, outer):
        total = total + shift_pass(
            lax.dynamic_index_in_dim(blocks, (me + step) % outer, 0, False), "outer", step
        )
    blocks = total
    total = lax.dynamic_index_in_dim(blocks, layer, 0, False)
    for step in range(1, depth):
        total = total + shift_pass(
            lax.dynamic_index_in_dim(blocks, (layer + step) % depth, 0, False), "fsdp", step
        )
    return total


def params():
    return pltpu.CompilerParams(vmem_limit_bytes=VMEM)


def cost(flops, nbytes, exps=0):
    return pl.CostEstimate(
        flops=flops // HASTE, bytes_accessed=nbytes // HASTE, transcendentals=exps // HASTE
    )


def kernel_call(kernel, prefetch, grid, specs, args, out_specs, out_shape, estimate, hold=()):
    count = len(prefetch) + len(args)

    def run(*refs):
        kernel(*refs[:count], *refs[count + len(hold) :])

    return pl.pallas_call(
        run,
        grid_spec=pltpu.PrefetchScalarGridSpec(
            num_scalar_prefetch=len(prefetch),
            grid=grid,
            in_specs=list(specs) + [pl.BlockSpec(memory_space=pl.ANY)] * len(hold),
            out_specs=out_specs,
        ),
        out_shape=out_shape,
        compiler_params=params(),
        cost_estimate=estimate,
    )(*prefetch, *args, *hold)


def pin(value, *hold):
    def run(*refs):
        del refs

    anywhere = pl.BlockSpec(memory_space=pl.ANY)
    return pl.pallas_call(
        run,
        in_specs=[anywhere] * (1 + len(hold)),
        out_specs=anywhere,
        out_shape=jax.ShapeDtypeStruct(value.shape, value.dtype),
        input_output_aliases={0: 0},
        compiler_params=params(),
        cost_estimate=cost(0, 0),
    )(value, *hold)


def still(shape, first=0):
    return pl.BlockSpec(shape, lambda *_: (first,) + (0,) * (len(shape) - 1))


def in_order(block):
    h, z, t, r, n = block.shape
    rows = [block[o, :, i].reshape(z * r, n) for o in range(h) for i in range(t)]
    return jnp.concatenate(rows, axis=0) if len(rows) > 1 else rows[0]


def half_of(start, which, size):
    at = start if which == 0 else 1 - start
    return pl.ds(pl.multiple_of(at * size, size), size)


def forward_kernel(style, count, spread, cuts, per_cut, start_ref, *refs):
    pieces, weights, rest = refs[:count], refs[count : count + 2 * cuts], refs[count + 2 * cuts :]
    start = start_ref[0]
    load = in_order if spread else (lambda b: b.reshape(-1, b.shape[-1]))
    firsts, seconds = load(weights[0][...]), load(weights[1][...])
    for i in range(1, cuts):
        late = pl.program_id(0) >= i * per_cut
        firsts = jnp.where(late, load(weights[2 * i][...]), firsts)
        seconds = jnp.where(late, load(weights[2 * i + 1][...]), seconds)
    size = firsts.shape[0]
    if style == "bare":
        outs = rest
    else:
        bias, outs = rest[0][...], rest[1:]
    at = 0
    for ref in pieces:
        views = [ref] if len(ref.shape) == 2 else [ref.at[i] for i in range(ref.shape[0])]
        for view in views:
            value = dot(view[:, half_of(start, 0, size)], firsts, 1, 0)
            value = value + dot(view[:, half_of(start, 1, size)], seconds, 1, 0)
            if style == "bare":
                outs[at][...] = value.astype(BF)
            elif style == "plain":
                outs[0][at] = (value + bias).astype(BF)
            else:
                value = value + bias
                phi = 0.5 + 0.5 * lax.erf(value * ROOT_HALF)
                outs[0][at] = (value * phi).astype(BF)
                outs[1][at] = (phi + value * DENSITY_SCALE * jnp.exp(-0.5 * value * value)).astype(BF)
            at += 1


def forward_product(pieces, weights, start, bias=None, style="plain", pick=None, rows=512, hold=()):
    whole = len(weights[0]) == 1
    sample = weights[0][0]
    spread = sample.ndim == 5
    paired = sample.ndim == 4
    cuts = len(weights)
    n = sample.shape[-1] * cuts
    tile = min(n // cuts, TILE)
    per_cut = n // cuts // tile
    stack = pieces[0].ndim == 3
    if stack:
        total = pick[1] if pick else pieces[0].shape[0]
        specs = [still((total,) + pieces[0].shape[1:], pick[0] if pick else 0)]
        k = pieces[0].shape[2]
    else:
        total, k = len(pieces), pieces[0].shape[1]
        specs = [still(p.shape) for p in pieces]
    lead = sample.shape[:-1]
    args = list(pieces)
    for i, pair in enumerate(weights):

        def at(j, s, i=i):
            return (0,) * len(lead) + (jnp.clip(j - i * per_cut, 0, per_cut - 1),)

        if paired:
            z, _, b, _ = sample.shape
            specs += [pl.BlockSpec((z, 1, b, tile), lambda j, s, h=h: (0, h, 0, j)) for h in range(2)]
            args += [pair[0], pair[0]]
        elif whole:
            specs += [pl.BlockSpec((lead[0] // 2, tile), lambda j, s, h=h: (h, j)) for h in range(2)]
            args += [pair[0], pair[0]]
        else:
            specs += [pl.BlockSpec(lead + (tile,), at)] * 2
            args += list(pair)
    if style != "bare":
        specs.append(pl.BlockSpec((1, tile), lambda j, s: (0, j)))
        args.append(bias.reshape(1, n))
    if style == "bare":
        out_specs = [pl.BlockSpec((rows, tile), lambda j, s: (0, j))] * total
        out_shape = [jax.ShapeDtypeStruct((rows, n), BF)] * total
    else:
        copies = 2 if style == "gate" else 1
        out_specs = [pl.BlockSpec((total, rows, tile), lambda j, s: (0, 0, j))] * copies
        out_shape = [jax.ShapeDtypeStruct((total, rows, n), BF)] * copies
    return kernel_call(
        functools.partial(forward_kernel, style, len(pieces), spread, cuts, per_cut),
        [start],
        (n // tile,),
        specs,
        args,
        out_specs,
        out_shape,
        cost(2 * total * rows * k * n, 2 * (total * rows * (k + n) + k * n)),
        hold,
    )


def back_kernel(style, count, shares, per_half, start_ref, *refs):
    pieces, weights, rest = refs[:count], refs[count : count + 2 * shares], refs[count + 2 * shares :]
    late = pl.program_id(0) >= per_half
    chosen = []
    for i in range(shares):
        w0, w1 = weights[2 * i][...], weights[2 * i + 1][...]
        if len(w0.shape) == 5:
            w0, w1 = in_order(w0), in_order(w1)
        elif len(w0.shape) == 4:
            w0, w1 = w0[0, 0], w1[0, 0]
        chosen.append(jnp.where(late, w1, w0))
    views = []
    for ref in pieces:
        views += [ref] if len(ref.shape) == 2 else [ref.at[i] for i in range(ref.shape[0])]
    width = chosen[0].shape[1]
    total = None
    for at, view in enumerate(views):
        value = dot(view[:, :width], chosen[0], 1, 1)
        for i in range(1, shares):
            value = value + dot(view[:, i * width : (i + 1) * width], chosen[i], 1, 1)
        if style == "slope":
            low = (value * rest[0][at].astype(F32)).astype(BF)
            rest[1][at] = low
            part = jnp.sum(low.astype(F32), axis=0, keepdims=True)
            total = part if total is None else total + part
        elif style == "plain":
            rest[0][at] = value.astype(BF)
        else:
            rest[at][...] = value.astype(BF)
    if style == "slope":
        rest[2][...] = total


def back_product(pieces, weights, start, style="plain", slope=None, pick=None, rows=512, hold=()):
    shares = len(weights)
    sample = weights[0][0]
    k = sample.shape[-1]
    half_rows = 1
    for d in sample.shape[:-1]:
        half_rows *= d
    whole = len(weights[0]) == 1
    if whole:
        half_rows //= 2
    n = 2 * half_rows
    tile = min(half_rows, TILE)
    per_half = half_rows // tile
    stack = pieces[0].ndim == 3
    if stack:
        total = pick[1] if pick else pieces[0].shape[0]
        specs = [still((total,) + pieces[0].shape[1:], pick[0] if pick else 0)]
    else:
        total = len(pieces)
        specs = [still(p.shape) for p in pieces]
    if sample.ndim == 4:
        tile = sample.shape[2]
        per_half = sample.shape[0]
        block = (1, 1, tile, k)
    elif sample.ndim == 5:
        h, z, t, r, _ = sample.shape
        group = max(1, tile // (z * r))
        tile = group * z * r
        per_half = half_rows // tile
        each = t // group
        block = (1, z, group, r, k)

        def at(j):
            return (j // each, 0, j % each, 0, 0)
    else:
        block = (tile, k)

        def at(j):
            return (j, 0)

    if sample.ndim == 4:
        first = pl.BlockSpec(block, lambda j, s: (jnp.minimum(j, per_half - 1), 0, 0, 0))
        second = pl.BlockSpec(block, lambda j, s: (jnp.maximum(j - per_half, 0), 1, 0, 0))
    else:
        first = pl.BlockSpec(block, lambda j, s: at(jnp.minimum(j, per_half - 1)))
        second = pl.BlockSpec(block, lambda j, s: at(jnp.maximum(j - per_half, 0) + (per_half if whole else 0)))
    args = list(pieces)
    for w in weights:
        specs += [first, second]
        args += [w[0], w[-1]]

    def column(j, s):
        return lax.rem(s[0] * per_half + j, 2 * per_half)

    stacked = pl.BlockSpec((total, rows, tile), lambda j, s: (0, 0, column(j, s)))
    stack_shape = jax.ShapeDtypeStruct((total, rows, n), BF)
    if style == "slope":
        specs.append(stacked)
        args.append(slope)
        out_specs = [stacked, pl.BlockSpec((1, tile), lambda j, s: (0, column(j, s)))]
        out_shape = [stack_shape, jax.ShapeDtypeStruct((1, n), F32)]
    elif style == "plain":
        out_specs, out_shape = [stacked], [stack_shape]
    else:
        out_specs = [pl.BlockSpec((rows, tile), lambda j, s: (0, column(j, s)))] * total
        out_shape = [jax.ShapeDtypeStruct((rows, n), BF)] * total
    return kernel_call(
        functools.partial(back_kernel, style, len(pieces), shares, per_half),
        [start],
        (2 * per_half,),
        specs,
        args,
        out_specs,
        out_shape,
        cost(2 * total * rows * k * n * shares, 2 * (total * rows * (k * shares + n) + k * n)),
        hold,
    )


def weight_kernel(left_count, right_count, start_ref, *refs):
    lefts, rights, out = refs[:left_count], refs[left_count : left_count + right_count], refs[-1]

    def views(group):
        found = []
        for ref in group:
            found += [ref] if len(ref.shape) == 2 else [ref.at[i] for i in range(ref.shape[0])]
        return found

    total = None
    for a, b in zip(views(lefts), views(rights)):
        part = dot(a[...], b[...], 0, 0)
        total = part if total is None else total + part
    low = total.astype(BF)
    if len(out.shape) == 2:
        out[...] = low
    else:
        h, z, t, r, n = out.shape
        for o in range(h):
            for i in range(t):
                base = (o * t + i) * z * r
                out[o, :, i] = low[base : base + z * r].reshape(z, r, n)


def weight_product(left, right, start, which, spread=None, cut=(0, 1, 1), tile=512, hold=()):
    def spec(group, width, index):
        found = []
        for a in group:
            if a.ndim == 2:
                found.append(pl.BlockSpec((a.shape[0], width), lambda j, s: (0, index(j, s))))
            else:
                found.append(pl.BlockSpec(a.shape[:2] + (width,), lambda j, s: (0, 0, index(j, s))))
        return found

    half = left[0].shape[-1] // (1 if which is None else 2)
    share = right[0].shape[-1] // cut[2]
    n = share * (cut[1] - cut[0])
    tile = min(tile, share)
    skip = cut[0] * (share // tile)
    rows = sum(a.shape[0] if a.ndim == 2 else a.shape[0] * a.shape[1] for a in left)
    specs = spec(left, half, lambda j, s: 0 if which is None else s[0] if which == 0 else 1 - s[0])
    specs += spec(right, tile, lambda j, s: j + skip)
    shape = (half, n) if spread is None else spread + (n,)
    block = shape[:-1] + (tile,)
    return kernel_call(
        functools.partial(weight_kernel, len(left), len(right)),
        [start],
        (n // tile,),
        specs,
        [*left, *right],
        pl.BlockSpec(block, lambda j, s: (0,) * (len(block) - 1) + (j,)),
        jax.ShapeDtypeStruct(shape, BF),
        cost(2 * rows * half * n, 2 * (rows * (half + n) + half * n)),
        hold,
    )


def pair_masks():
    lane = lax.broadcasted_iota(jnp.int32, (1, 2 * HD), 1)
    low = jnp.where(lane < HD, 1.0, 0.0).astype(BF)
    high = jnp.where(lane < HD, 0.0, 1.0).astype(BF)
    return low, high


def pair_probs(q_two, k):
    scores = dot(q_two, k, 1, 1) * 0.125
    row = lax.broadcasted_iota(jnp.int32, scores.shape, 0) & (SLOT - 1)
    column = lax.broadcasted_iota(jnp.int32, scores.shape, 1)
    scores = jnp.where(row >= column, scores, MASKED)
    exponent = jnp.exp(scores - jnp.max(scores, axis=-1, keepdims=True))
    return exponent / jnp.sum(exponent, axis=-1, keepdims=True)


def attend_kernel(q_ref, k_ref, v_ref, context_ref):
    low, high = pair_masks()
    for at in range(0, context_ref.shape[1], 2 * HD):
        q, k, v = [ref[:, at : at + 2 * HD] for ref in (q_ref, k_ref, v_ref)]
        probs = pair_probs(jnp.concatenate([q * low, q * high], axis=0), k).astype(BF)
        context = dot(probs[:SLOT], v * low, 1, 0) + dot(probs[SLOT:], v * high, 1, 0)
        context_ref[:, at : at + 2 * HD] = context.astype(BF)


def attend_back_kernel(q_ref, k_ref, v_ref, grad_ref, out_ref, sum_ref):
    part = grad_ref.shape[1]
    low, high = pair_masks()

    @pl.when(pl.program_id(0) == 0)
    def _():
        sum_ref[...] = jnp.zeros_like(sum_ref)

    for at in range(0, part, 2 * HD):
        q, k, v, grad = [ref[:, at : at + 2 * HD] for ref in (q_ref, k_ref, v_ref, grad_ref)]
        q_two = jnp.concatenate([q * low, q * high], axis=0)
        g_two = jnp.concatenate([grad * low, grad * high], axis=0)
        probs = pair_probs(q_two, k)
        d_probs = dot(g_two, v, 1, 1)
        row_dot = jnp.sum(probs * d_probs, axis=-1, keepdims=True)
        d_scores = (probs * (d_probs - row_dot)).astype(BF)
        d_q = dot(d_scores[:SLOT], k * low, 1, 0) + dot(d_scores[SLOT:], k * high, 1, 0)
        d_k = dot(d_scores, q_two, 0, 0)
        d_v = dot(probs.astype(BF), g_two, 0, 0)
        for i, value in enumerate((d_q * 0.125, d_k * 0.125, d_v)):
            where = slice(i * part + at, i * part + at + 2 * HD)
            value = value.astype(BF)
            out_ref[:, where] = value
            sum_ref[:, where] += jnp.sum(value.astype(F32), axis=0, keepdims=True)


def attend(q, k, v, hold=()):
    rows, part = q.shape
    one = pl.BlockSpec((SLOT, part), lambda i: (i, 0))
    return kernel_call(
        attend_kernel,
        [],
        (rows // SLOT,),
        [one] * 3,
        [q, k, v],
        one,
        jax.ShapeDtypeStruct((rows, part), BF),
        cost(32 * rows * SLOT * part, 8 * rows * part, rows * SLOT * part // HD),
        hold,
    )


def attend_back(q, k, v, grad, first, hold=()):
    rows, part = grad.shape
    one = pl.BlockSpec((SLOT, part), lambda i: (i, 0))
    shifted = pl.BlockSpec((SLOT, part), lambda i: (i + first, 0))
    return kernel_call(
        attend_back_kernel,
        [],
        (rows // SLOT,),
        [shifted] * 3 + [one],
        [q, k, v, grad],
        [pl.BlockSpec((SLOT, 3 * part), lambda i: (i, 0)), still((1, 3 * part))],
        [jax.ShapeDtypeStruct((rows, 3 * part), BF), jax.ShapeDtypeStruct((1, 3 * part), F32)],
        cost(80 * rows * SLOT * part, 14 * rows * part, rows * SLOT * part // HD),
        hold,
    )


def normal_of(values):
    centred = values - jnp.mean(values, axis=-1, keepdims=True)
    inverse = lax.rsqrt(jnp.mean(centred * centred, axis=-1, keepdims=True) + EPSILON)
    return centred * inverse, inverse


def rows_of(refs):
    total = refs[0][...].astype(F32)
    for ref in refs[1:]:
        total = total + ref[...].astype(F32)
    return total


def norm_kernel(x_ref, gain_ref, shift_ref, out_ref):
    normal, _ = normal_of(x_ref[...].astype(F32))
    out_ref[...] = (normal * gain_ref[...] + shift_ref[...]).astype(BF)


def join_norm_kernel(count, *refs):
    bias, gain, shift, hidden_ref, out_ref = refs[count:]
    hidden = rows_of(refs[:count]) + bias[...]
    hidden_ref[...] = hidden
    normal, _ = normal_of(hidden)
    out_ref[...] = (normal * gain[...] + shift[...]).astype(BF)


def join_kernel(count, *refs):
    refs[count + 1][...] = (rows_of(refs[:count]) + refs[count][...]).astype(BF)


def norm_back_kernel(count, *refs):
    source, carry, gain, grad_ref, low_ref, sums = refs[count:]
    grad = rows_of(refs[:count])
    normal, inverse = normal_of(source[...].astype(F32))
    scaled = grad * gain[...]
    centre = jnp.mean(scaled, axis=-1, keepdims=True)
    projected = jnp.mean(scaled * normal, axis=-1, keepdims=True)
    carried = carry[...].astype(F32)
    result = carried + inverse * (scaled - centre - normal * projected)
    grad_ref[...] = result.astype(grad_ref.dtype)
    low = result.astype(BF)
    low_ref[...] = low

    @pl.when(pl.program_id(0) == 0)
    def _():
        sums[...] = jnp.zeros_like(sums)

    for i, value in enumerate((grad * normal, grad, low.astype(F32), carried)):
        sums[i : i + 1] += jnp.sum(value, axis=0, keepdims=True)


def add_kernel(a_ref, b_ref, out_ref):
    out_ref[...] = (a_ref[...].astype(F32) + b_ref[...].astype(F32)).astype(BF)


def add_low(a, b, hold=()):
    width = a.shape[-1]
    flat = [x.reshape(-1, width) for x in (a, b)]
    rows = flat[0].shape[0]
    step = min(rows, 256)
    one = pl.BlockSpec((step, width), lambda i: (i, 0))
    result = kernel_call(
        add_kernel,
        [],
        (rows // step,),
        [one, one],
        flat,
        one,
        jax.ShapeDtypeStruct((rows, width), BF),
        cost(rows * width, 6 * rows * width),
        hold,
    )
    return result.reshape(a.shape)


def row_call(kernel, blocks, vectors, outs, sums=0, step=128, hold=()):
    rows, width = blocks[0].shape
    one = pl.BlockSpec((step, width), lambda i: (i, 0))
    out_specs = [one] * len(outs)
    out_shape = [jax.ShapeDtypeStruct((rows, width), d) for d in outs]
    if sums:
        out_specs.append(still((sums, width)))
        out_shape.append(jax.ShapeDtypeStruct((sums, width), F32))
    return kernel_call(
        kernel,
        [],
        (rows // step,),
        [one] * len(blocks) + [still((1, width))] * len(vectors),
        [*blocks, *[v.reshape(1, width) for v in vectors]],
        out_specs,
        out_shape,
        cost(20 * rows * width, 16 * rows * width),
        hold,
    )


def body(
    tokens,
    cotangent,
    doc_starts,
    active_len,
    ln1_gain,
    ln1_bias,
    q_weight,
    q_bias,
    k_weight,
    v_weight,
    v_bias,
    o_weight,
    o_bias,
    ln2_gain,
    ln2_bias,
    up_weight,
    up_bias,
    down_weight,
    down_bias,
):
    depth = lax.axis_size("fsdp")
    outer = lax.axis_size("outer")
    devices = outer * TEAM * depth
    member, me = lax.axis_index("team"), lax.axis_index("outer")
    layer = lax.axis_index("fsdp")
    start = (me if outer == 2 else jnp.zeros_like(me)).reshape(1)
    groups, row_len, width = tokens.shape
    docs = doc_starts.shape[1]
    r = q_weight.shape[0]
    part_width = width // TEAM
    rows = groups * docs * SLOT

    zero_bias = jnp.zeros((part_width,), F32)

    def depth_gather(a):
        return lax.all_gather(a, "fsdp", axis=0, tiled=True)

    def columns(a, i, n):
        c = a.shape[1] // n
        return a[:, i * c : (i + 1) * c]

    def stored(block):
        return block.reshape(1, depth, TEAM, r, block.shape[1])

    def flat(block):
        return block[None]

    def both_halves(block, *hold):
        return outer_halves(pin(block, *hold) if hold else block, me)

    def flatten(halves):
        return [h.reshape(-1, h.shape[-1]) for h in halves]

    down_other = outer_pass(down_weight)
    deal = deal_columns((q_weight, k_weight, v_weight, up_weight), member, outer, depth)
    qkv_deal, up_deal = deal[:, : 3 * part_width], deal[:, 3 * part_width :]
    block_q, block_k, block_v = [stored(depth_gather(columns(qkv_deal, i, 3))) for i in range(3)]
    w_q, w_k = [both_halves(b) for b in (block_q, block_k)]
    block_o = flat(depth_gather(o_weight))

    vectors = (ln1_gain, ln1_bias, o_bias, ln2_gain, ln2_bias, down_bias, q_bias, v_bias, up_bias)
    packed = gather_small(jnp.concatenate(vectors), member, me, layer)
    edges = [0]
    for v in vectors:
        edges.append(edges[-1] + v.shape[0])
    pieces = [packed[:, edges[i] : edges[i + 1]] for i in range(len(vectors))]
    gain1, shift1, bias_o, gain2, shift2, bias_down = [p.reshape(-1) for p in pieces[:6]]

    def member_part(p):
        whole = p.reshape(outer, TEAM, depth, -1)
        return lax.dynamic_index_in_dim(whole, member, 1, False).reshape(-1)

    bias_q, bias_v, bias_up = [member_part(p) for p in pieces[6:]]

    position = jnp.arange(row_len, dtype=jnp.int32)
    offset = jnp.arange(SLOT, dtype=jnp.int32)
    wanted = doc_starts[:, :, None] + offset
    live = offset < active_len[:, :, None]
    chosen = (wanted[..., None] == position) & live[..., None]
    chosen = chosen.reshape(groups, docs * SLOT, row_len)
    select = chosen.astype(BF)
    covered = jnp.any(chosen, axis=1)

    def pack(source):
        picked = jnp.einsum("gst,gtd->gsd", select, source, preferred_element_type=F32)
        return picked.reshape(rows, width).astype(BF)

    def unpack(slot_rows, fallback):
        blocks = slot_rows.reshape(groups, docs * SLOT, width)
        placed = jnp.einsum("gst,gsd->gtd", select, blocks, preferred_element_type=F32).astype(BF)
        return jnp.where(covered[..., None], placed, fallback)

    class Order:
        last = ()

        def step(self, kernel, *args, hold=(), **kw):
            result = kernel(*args, hold=self.last + tuple(hold), **kw)
            self.last = (jax.tree.leaves(result)[-1],)
            return result

    order = Order()

    def begin(weights):
        return jnp.zeros_like(start) if len(weights[0]) == 1 and outer != 2 else start

    def forward(pieces, weights, *rest, **kw):
        return order.step(forward_product, pieces, weights, begin(weights), *rest, rows=rows, **kw)

    def back(pieces, weights, **kw):
        return order.step(back_product, pieces, weights, begin(weights), rows=rows, **kw)

    def weight_grad(left, right, which, **kw):
        return order.step(weight_product, left, right, start, which, **kw)

    def by_rows(kernel, blocks, *args, **kw):
        return order.step(row_call, kernel, blocks, *args, **kw)

    def add(a, b, **kw):
        return order.step(add_low, a, b, **kw)

    def team_gather(own, *hold):
        across = team_swap(own, 2)
        if hold:
            across = pin(across, *hold)
        return [own, across, team_swap(own, 1), team_swap(across, 1)]

    def send_far(parts):
        return [team_swap(p, 1) for p in parts]

    def join_near(near, far, **kw):
        across = add(near[1], far[1], **kw)
        return [near[0], far[0], team_swap(across, 2), across]

    x_rows = pack(tokens)
    (a_own,) = by_rows(norm_kernel, [x_rows], [gain1, shift1], [BF], hold=[down_other])
    a_own = pin(a_own, block_o)
    a_across = team_swap(a_own, 2)
    w_o = flatten(both_halves(block_o))
    a_across = pin(a_across, w_q[1], w_o[1])
    a_all = [a_own, a_across, team_swap(a_own, 1), team_swap(a_across, 1)]
    down_pair = jnp.stack([down_weight, down_other])[None]
    block_up = [stored(depth_gather(columns(up_deal, i, 2))) for i in range(2)]
    if outer == 2:
        w_down = [[depth_gather(down_pair)]]
    else:
        w_down = [[lax.all_gather(down_weight, SPREAD, axis=0, tiled=True)]]
    g_rows = pack(cotangent)
    g_all = team_gather(pin(g_rows, a_all[1]))

    wide = TEAM * rows
    q = forward(a_all, [w_q], bias_q)[0]
    k = forward(a_all, [w_k], zero_bias)[0]
    w_v = both_halves(block_v, q)
    v = forward(a_all, [w_v], bias_v)[0]
    q, k, v = [s.reshape(wide, part_width) for s in (q, k, v)]
    context = order.step(attend, q, k, v).reshape(TEAM, rows, part_width)
    o_far = send_far(forward([context], [w_o], style="bare", pick=(1, 2), hold=[g_all[1]]))
    o_near = forward([context], [w_o], style="bare", pick=(0, 2))
    w_up = [both_halves(block_up[0], context)]
    *o_parts, o_across = join_near(o_near, o_far)
    hidden, b_own = by_rows(
        functools.partial(join_norm_kernel, 4),
        [x_rows] + o_parts,
        [bias_o, gain2, shift2],
        [F32, BF],
        hold=[w_up[0][1]],
    )
    w_up.append(both_halves(block_up[1], b_own))
    b_all = team_gather(b_own, w_up[1][1])

    active, slope = forward(b_all, w_up, bias_up, style="gate")

    def depth_scatter(a):
        return lax.psum_scatter(a, "fsdp", scatter_dimension=0, tiled=True)

    def send_away(away, *hold):
        if outer != 2:
            return away
        return outer_pass(pin(away, *hold) if hold else away)

    def settle(sent, mine, **kw):
        c = mine.shape[-1]
        if outer == 2:
            total = add(sent, mine, **kw)
        else:
            both = jnp.concatenate([mine.reshape(outer // 2, -1, c), sent.reshape(outer // 2, -1, c)])
            total = outer_scatter(both, me)
        return depth_scatter(total.reshape(-1, c))

    spread = (outer // 2, depth, TEAM, r)

    def settle_whole(grad):
        return lax.psum_scatter(grad, SPREAD, scatter_dimension=0, tiled=True)

    grad_down = [settle_whole(weight_grad([active], g_all, None, cut=(0, 1, 2)))]
    grad_down.append(settle_whole(weight_grad([active], g_all, None, cut=(1, 2, 2))))
    d_inner, sum_inner = back(g_all, w_down, style="slope", slope=slope)
    n_far = send_far(back([d_inner], w_up, style="bare", pick=(1, 2)))
    n_near = back([d_inner], w_up, style="bare", pick=(0, 2))
    n_parts = join_near(n_near, n_far)[:3]
    up_sent = [
        send_away(weight_grad(b_all, [d_inner], 1, spread=spread, cut=(i, i + 1, 2))) for i in range(2)
    ]
    up_mine = [weight_grad(b_all, [d_inner], 0, spread=spread, cut=(i, i + 1, 2)) for i in range(2)]
    d_hidden, d_out, sums2 = by_rows(
        functools.partial(norm_back_kernel, 3), n_parts + [hidden, g_rows], [gain2], [F32, BF], sums=4
    )
    y_far = send_far(forward([active], w_down, style="bare", pick=(1, 2), hold=[grad_down[0]]))
    y_near = forward([active], w_down, style="bare", pick=(0, 2))
    d_out_all = team_gather(d_out, up_sent[0], y_near[1])

    (d_near,) = back(d_out_all[:2], [w_o])
    (d_far,) = back(d_out_all[2:], [w_o])
    grad_up = [settle(up_sent[0], up_mine[0], hold=[grad_down[1]])]
    *y_parts, y_across = join_near(y_near, y_far)
    q_far, sum_far = order.step(attend_back, q, k, v, d_far.reshape(2 * rows, -1), 2 * rows // SLOT)
    q_far = q_far.reshape(2, rows, -1)
    a_far = send_far(back([q_far], [w_q, w_k, w_v], style="bare"))
    grad_up.append(settle(up_sent[1], up_mine[1]))
    o_sent = send_away(weight_grad([context], d_out_all, 1))
    o_mine = weight_grad([context], d_out_all, 0)
    q_near, sum_near = order.step(attend_back, q, k, v, d_near.reshape(2 * rows, -1), 0, hold=[grad_up[0]])
    q_near = q_near.reshape(2, rows, -1)
    grad_o = settle(o_sent, o_mine)
    a_near = back([q_near], [w_q, w_k, w_v], style="bare")
    a_parts = join_near(a_near, a_far, hold=[y_parts[2]])[:3]
    parts = ((0, 1, 3), (1, 3, 3))
    d_both = [q_near, q_far]
    qkv_sent = [
        send_away(weight_grad(a_all, d_both, 1, spread=spread, cut=parts[0], hold=[grad_up[1]])),
        send_away(weight_grad(a_all, d_both, 1, spread=spread, cut=parts[1], hold=[grad_o])),
    ]
    grad_q = settle(qkv_sent[0], weight_grad(a_all, d_both, 0, spread=spread, cut=parts[0]))
    kv_mine = weight_grad(a_all, d_both, 0, spread=spread, cut=parts[1])
    (y_rows,) = by_rows(functools.partial(join_kernel, 4), [hidden] + y_parts, [bias_down], [BF])
    layer_out = unpack(y_rows, tokens)
    _, d_input, sums1 = by_rows(
        functools.partial(norm_back_kernel, 3),
        a_parts + [x_rows, d_hidden],
        [gain1],
        [BF, BF],
        sums=4,
        hold=[layer_out],
    )
    grad_kv = settle(qkv_sent[1], kv_mine)
    sum_qkv = sum_far + sum_near
    grad_o = grad_o.astype(F32)
    input_grad = unpack(d_input, cotangent)
    grad_down = jnp.concatenate([g.astype(F32) for g in grad_down], axis=1)
    (grad_up,) = return_columns(jnp.concatenate(grad_up, axis=1), member, outer, depth, 1)
    (grad_q,) = return_columns(grad_q, member, outer, depth, 1)
    grad_k, grad_v = return_columns(grad_kv, member, outer, depth, 2)

    whole_sums = [sums1[0], sums1[1], sums2[2], sums2[0], sums2[1], sums2[3]]
    part_sums = [sum_qkv[0, :part_width], sum_qkv[0, 2 * part_width :], sum_inner[0]]
    is_mine = (jnp.arange(TEAM) == member)[None, :, None, None]

    def widen(s):
        blocks = s.reshape(outer, 1, depth, -1)
        return jnp.where(is_mine, blocks, 0.0).reshape(devices, -1)

    table = jnp.concatenate([s.reshape(devices, -1) for s in whole_sums] + [widen(s) for s in part_sums], axis=1)
    small = reduce_small(table, member, me, layer)
    cuts = [small[edges[i] : edges[i + 1]] for i in range(len(vectors))]
    g_gain1, g_shift1, g_bias_o, g_gain2, g_shift2, g_bias_down, g_bias_q, g_bias_v, g_bias_up = cuts
    return (
        layer_out,
        input_grad,
        g_gain1,
        g_shift1,
        grad_q,
        g_bias_q,
        grad_k,
        grad_v,
        g_bias_v,
        grad_o,
        g_bias_o,
        g_gain2,
        g_shift2,
        grad_up,
        g_bias_up,
        grad_down,
        g_bias_down,
    )


def solution(mesh):
    outer = mesh.shape["dp"] // TEAM
    devices = mesh.devices.reshape(outer, TEAM, mesh.shape["fsdp"])
    fine = Mesh(devices, ALL)
    kinds = {"t": P(ALL, None, None), "w": P(ALL, None), "v": P(ALL)}
    vectors = "vvwvwwvwvvvwvwv"
    in_specs = tuple(kinds[c] for c in "ttww" + vectors)
    out_specs = tuple(kinds[c] for c in "tt" + vectors)
    return jax.shard_map(body, mesh=fine, in_specs=in_specs, out_specs=out_specs, check_vma=False)
```

```python
import functools

import jax
import jax.numpy as jnp
from jax import lax
from jax.experimental import pallas as pl
from jax.experimental.pallas import tpu as pltpu
from jax.sharding import Mesh
from jax.sharding import PartitionSpec as P

HD = 64
SLOT = 128
TEAM = 4
TILE = 256
HASTE = 1000
VMEM = 48 * 2**20

EPSILON = 1e-05
MASKED = -1e30
ROOT_HALF = 0.7071067811865476
DENSITY_SCALE = 0.3989422804014327
BF = jnp.bfloat16
F32 = jnp.float32
ALL = ("outer", "team", "fsdp")
SPREAD = ("outer", "fsdp")


def dot(a, b, ca, cb):
    return lax.dot_general(a, b, (((ca,), (cb,)), ((), ())), preferred_element_type=F32)


def team_swap(a, flip):
    return lax.ppermute(a, "team", [(i, i ^ flip) for i in range(TEAM)])


def ring_order(size):
    return list(range(0, size, 2)) + list(range(1, size, 2))[::-1]


def outer_pass(a):
    outer = lax.axis_size("outer")
    order = ring_order(outer)
    return lax.ppermute(a, "outer", [(o, order[(p + 1) % outer]) for p, o in enumerate(order)])


def outer_place(me):
    outer = lax.axis_size("outer")
    order = ring_order(outer)
    place = [0] * outer
    for p, o in enumerate(order):
        place[o] = p
    return jnp.asarray(order, jnp.int32), jnp.asarray(place, jnp.int32)[me]


def outer_halves(a, me):
    outer = lax.axis_size("outer")
    if outer == 2:
        return [a, outer_pass(a)]
    order, place = outer_place(me)
    whole = jnp.zeros((outer,) + a.shape[1:], a.dtype)
    whole = lax.dynamic_update_slice_in_dim(whole, a, me, 0)
    moving = a
    for step in range(1, outer):
        moving = outer_pass(moving)
        whole = lax.dynamic_update_slice_in_dim(whole, moving, order[(place - step) % outer], 0)
    return [whole[: outer // 2], whole[outer // 2 :]]


def outer_scatter(blocks, me):
    outer = lax.axis_size("outer")
    order, place = outer_place(me)
    moving = lax.dynamic_slice_in_dim(blocks, order[(place - 1) % outer], 1, 0)
    for step in range(1, outer):
        moving = outer_pass(moving)
        mine = lax.dynamic_slice_in_dim(blocks, order[(place - 1 - step) % outer], 1, 0)
        moving = (moving.astype(F32) + mine.astype(F32)).astype(BF)
    return moving


def by_team(stacked, member):
    odd = (member & 1) == 1
    high = (member & 2) == 2
    a = [jnp.where(odd, stacked[i ^ 1], stacked[i]) for i in range(4)]
    return [jnp.where(high, a[i ^ 2], a[i]) for i in range(4)]


def deal_columns(shards, member, outer, depth):
    r = shards[0].shape[0]
    parts = [w.reshape(r, outer, TEAM, depth, -1) for w in shards]
    got = []
    for flip in range(TEAM):
        piece = jnp.concatenate(
            [lax.dynamic_index_in_dim(w, member ^ flip, 2, False).reshape(r, -1) for w in parts], axis=1
        )
        got.append(piece if flip == 0 else team_swap(piece, flip))
    return jnp.concatenate(by_team(got, member), axis=0)


def return_columns(block, member, outer, depth, shares):
    r, c = block.shape[0] // TEAM, block.shape[1] // shares
    parts = block.reshape(TEAM, r, shares * c)
    got = []
    for flip in range(TEAM):
        piece = lax.dynamic_index_in_dim(parts, member ^ flip, 0, False)
        got.append(piece if flip == 0 else team_swap(piece, flip))
    got = by_team(got, member)
    result = []
    for i in range(shares):
        cols = jnp.stack([g[:, i * c : (i + 1) * c].reshape(r, outer, depth, -1) for g in got], axis=2)
        result.append(cols.reshape(r, -1).astype(F32))
    return result


def shift_pass(a, axis, step):
    size = lax.axis_size(axis)
    return lax.ppermute(a, axis, [(i, (i + step) % size) for i in range(size)])


def gather_small(vector, member, me, layer):
    depth = lax.axis_size("fsdp")
    outer = lax.axis_size("outer")
    a = vector[None]
    a = jnp.concatenate([a if s == 0 else shift_pass(a, "fsdp", s) for s in range(depth)])
    a = jnp.concatenate([a if s == 0 else shift_pass(a, "outer", s) for s in range(outer)])
    a = jnp.concatenate([a if f == 0 else team_swap(a, f) for f in range(TEAM)])
    index = jnp.arange(TEAM * outer * depth, dtype=jnp.int32)
    flip, step, drop = index // (outer * depth), index // depth % outer, index % depth
    source = ((me - step) % outer * TEAM + (member ^ flip)) * depth + (layer - drop) % depth
    place = (index[:, None] == source[None, :]).astype(BF)
    return dot(place, a, 1, 0)


def reduce_small(table, member, me, layer):
    depth = lax.axis_size("fsdp")
    outer = lax.axis_size("outer")
    blocks = table.reshape(outer, TEAM, depth, -1)
    total = lax.dynamic_index_in_dim(blocks, member, 1, False)
    for flip in range(1, TEAM):
        total = total + team_swap(lax.dynamic_index_in_dim(blocks, member ^ flip, 1, False), flip)
    blocks = total
    total = lax.dynamic_index_in_dim(blocks, me, 0, False)
    for step in range(1, outer):
        total = total + shift_pass(
            lax.dynamic_index_in_dim(blocks, (me + step) % outer, 0, False), "outer", step
        )
    blocks = total
    total = lax.dynamic_index_in_dim(blocks, layer, 0, False)
    for step in range(1, depth):
        total = total + shift_pass(
            lax.dynamic_index_in_dim(blocks, (layer + step) % depth, 0, False), "fsdp", step
        )
    return total


def params():
    return pltpu.CompilerParams(vmem_limit_bytes=VMEM)


def cost(flops, nbytes, exps=0):
    return pl.CostEstimate(
        flops=flops // HASTE, bytes_accessed=nbytes // HASTE, transcendentals=exps // HASTE
    )


def kernel_call(kernel, prefetch, grid, specs, args, out_specs, out_shape, estimate, hold=()):
    count = len(prefetch) + len(args)

    def run(*refs):
        kernel(*refs[:count], *refs[count + len(hold) :])

    return pl.pallas_call(
        run,
        grid_spec=pltpu.PrefetchScalarGridSpec(
            num_scalar_prefetch=len(prefetch),
            grid=grid,
            in_specs=list(specs) + [pl.BlockSpec(memory_space=pl.ANY)] * len(hold),
            out_specs=out_specs,
        ),
        out_shape=out_shape,
        compiler_params=params(),
        cost_estimate=estimate,
    )(*prefetch, *args, *hold)


def pin(value, *hold):
    def run(*refs):
        del refs

    anywhere = pl.BlockSpec(memory_space=pl.ANY)
    return pl.pallas_call(
        run,
        in_specs=[anywhere] * (1 + len(hold)),
        out_specs=anywhere,
        out_shape=jax.ShapeDtypeStruct(value.shape, value.dtype),
        input_output_aliases={0: 0},
        compiler_params=params(),
        cost_estimate=cost(0, 0),
    )(value, *hold)


def still(shape, first=0):
    return pl.BlockSpec(shape, lambda *_: (first,) + (0,) * (len(shape) - 1))


def in_order(block):
    h, z, t, r, n = block.shape
    rows = [block[o, :, i].reshape(z * r, n) for o in range(h) for i in range(t)]
    return jnp.concatenate(rows, axis=0) if len(rows) > 1 else rows[0]


def half_of(start, which, size):
    at = start if which == 0 else 1 - start
    return pl.ds(pl.multiple_of(at * size, size), size)


def forward_kernel(style, count, spread, cuts, per_cut, start_ref, *refs):
    pieces, weights, rest = refs[:count], refs[count : count + 2 * cuts], refs[count + 2 * cuts :]
    start = start_ref[0]
    load = in_order if spread else (lambda b: b.reshape(-1, b.shape[-1]))
    firsts, seconds = load(weights[0][...]), load(weights[1][...])
    for i in range(1, cuts):
        late = pl.program_id(0) >= i * per_cut
        firsts = jnp.where(late, load(weights[2 * i][...]), firsts)
        seconds = jnp.where(late, load(weights[2 * i + 1][...]), seconds)
    size = firsts.shape[0]
    if style == "bare":
        outs = rest
    else:
        bias, outs = rest[0][...], rest[1:]
    at = 0
    for ref in pieces:
        views = [ref] if len(ref.shape) == 2 else [ref.at[i] for i in range(ref.shape[0])]
        for view in views:
            value = dot(view[:, half_of(start, 0, size)], firsts, 1, 0)
            value = value + dot(view[:, half_of(start, 1, size)], seconds, 1, 0)
            if style == "bare":
                outs[at][...] = value.astype(BF)
            elif style == "plain":
                outs[0][at] = (value + bias).astype(BF)
            else:
                value = value + bias
                phi = 0.5 + 0.5 * lax.erf(value * ROOT_HALF)
                outs[0][at] = (value * phi).astype(BF)
                outs[1][at] = (phi + value * DENSITY_SCALE * jnp.exp(-0.5 * value * value)).astype(BF)
            at += 1


def forward_product(pieces, weights, start, bias=None, style="plain", pick=None, rows=512, hold=()):
    whole = len(weights[0]) == 1
    sample = weights[0][0]
    spread = sample.ndim == 5
    paired = sample.ndim == 4
    cuts = len(weights)
    n = sample.shape[-1] * cuts
    tile = min(n // cuts, TILE)
    per_cut = n // cuts // tile
    stack = pieces[0].ndim == 3
    if stack:
        total = pick[1] if pick else pieces[0].shape[0]
        specs = [still((total,) + pieces[0].shape[1:], pick[0] if pick else 0)]
        k = pieces[0].shape[2]
    else:
        total, k = len(pieces), pieces[0].shape[1]
        specs = [still(p.shape) for p in pieces]
    lead = sample.shape[:-1]
    args = list(pieces)
    for i, pair in enumerate(weights):

        def at(j, s, i=i):
            return (0,) * len(lead) + (jnp.clip(j - i * per_cut, 0, per_cut - 1),)

        if paired:
            z, _, b, _ = sample.shape
            specs += [pl.BlockSpec((z, 1, b, tile), lambda j, s, h=h: (0, h, 0, j)) for h in range(2)]
            args += [pair[0], pair[0]]
        elif whole:
            specs += [pl.BlockSpec((lead[0] // 2, tile), lambda j, s, h=h: (h, j)) for h in range(2)]
            args += [pair[0], pair[0]]
        else:
            specs += [pl.BlockSpec(lead + (tile,), at)] * 2
            args += list(pair)
    if style != "bare":
        specs.append(pl.BlockSpec((1, tile), lambda j, s: (0, j)))
        args.append(bias.reshape(1, n))
    if style == "bare":
        out_specs = [pl.BlockSpec((rows, tile), lambda j, s: (0, j))] * total
        out_shape = [jax.ShapeDtypeStruct((rows, n), BF)] * total
    else:
        copies = 2 if style == "gate" else 1
        out_specs = [pl.BlockSpec((total, rows, tile), lambda j, s: (0, 0, j))] * copies
        out_shape = [jax.ShapeDtypeStruct((total, rows, n), BF)] * copies
    return kernel_call(
        functools.partial(forward_kernel, style, len(pieces), spread, cuts, per_cut),
        [start],
        (n // tile,),
        specs,
        args,
        out_specs,
        out_shape,
        cost(2 * total * rows * k * n, 2 * (total * rows * (k + n) + k * n)),
        hold,
    )


def back_kernel(style, count, shares, per_half, start_ref, *refs):
    pieces, weights, rest = refs[:count], refs[count : count + 2 * shares], refs[count + 2 * shares :]
    late = pl.program_id(0) >= per_half
    chosen = []
    for i in range(shares):
        w0, w1 = weights[2 * i][...], weights[2 * i + 1][...]
        if len(w0.shape) == 5:
            w0, w1 = in_order(w0), in_order(w1)
        elif len(w0.shape) == 4:
            w0, w1 = w0[0, 0], w1[0, 0]
        chosen.append(jnp.where(late, w1, w0))
    views = []
    for ref in pieces:
        views += [ref] if len(ref.shape) == 2 else [ref.at[i] for i in range(ref.shape[0])]
    width = chosen[0].shape[1]
    total = None
    for at, view in enumerate(views):
        value = dot(view[:, :width], chosen[0], 1, 1)
        for i in range(1, shares):
            value = value + dot(view[:, i * width : (i + 1) * width], chosen[i], 1, 1)
        if style == "slope":
            low = (value * rest[0][at].astype(F32)).astype(BF)
            rest[1][at] = low
            part = jnp.sum(low.astype(F32), axis=0, keepdims=True)
            total = part if total is None else total + part
        elif style == "plain":
            rest[0][at] = value.astype(BF)
        else:
            rest[at][...] = value.astype(BF)
    if style == "slope":
        rest[2][...] = total


def back_product(pieces, weights, start, style="plain", slope=None, pick=None, rows=512, hold=()):
    shares = len(weights)
    sample = weights[0][0]
    k = sample.shape[-1]
    half_rows = 1
    for d in sample.shape[:-1]:
        half_rows *= d
    whole = len(weights[0]) == 1
    if whole:
        half_rows //= 2
    n = 2 * half_rows
    tile = min(half_rows, TILE)
    per_half = half_rows // tile
    stack = pieces[0].ndim == 3
    if stack:
        total = pick[1] if pick else pieces[0].shape[0]
        specs = [still((total,) + pieces[0].shape[1:], pick[0] if pick else 0)]
    else:
        total = len(pieces)
        specs = [still(p.shape) for p in pieces]
    if sample.ndim == 4:
        tile = sample.shape[2]
        per_half = sample.shape[0]
        block = (1, 1, tile, k)
    elif sample.ndim == 5:
        h, z, t, r, _ = sample.shape
        group = max(1, tile // (z * r))
        tile = group * z * r
        per_half = half_rows // tile
        each = t // group
        block = (1, z, group, r, k)

        def at(j):
            return (j // each, 0, j % each, 0, 0)
    else:
        block = (tile, k)

        def at(j):
            return (j, 0)

    if sample.ndim == 4:
        first = pl.BlockSpec(block, lambda j, s: (jnp.minimum(j, per_half - 1), 0, 0, 0))
        second = pl.BlockSpec(block, lambda j, s: (jnp.maximum(j - per_half, 0), 1, 0, 0))
    else:
        first = pl.BlockSpec(block, lambda j, s: at(jnp.minimum(j, per_half - 1)))
        second = pl.BlockSpec(block, lambda j, s: at(jnp.maximum(j - per_half, 0) + (per_half if whole else 0)))
    args = list(pieces)
    for w in weights:
        specs += [first, second]
        args += [w[0], w[-1]]

    def column(j, s):
        return lax.rem(s[0] * per_half + j, 2 * per_half)

    stacked = pl.BlockSpec((total, rows, tile), lambda j, s: (0, 0, column(j, s)))
    stack_shape = jax.ShapeDtypeStruct((total, rows, n), BF)
    if style == "slope":
        specs.append(stacked)
        args.append(slope)
        out_specs = [stacked, pl.BlockSpec((1, tile), lambda j, s: (0, column(j, s)))]
        out_shape = [stack_shape, jax.ShapeDtypeStruct((1, n), F32)]
    elif style == "plain":
        out_specs, out_shape = [stacked], [stack_shape]
    else:
        out_specs = [pl.BlockSpec((rows, tile), lambda j, s: (0, column(j, s)))] * total
        out_shape = [jax.ShapeDtypeStruct((rows, n), BF)] * total
    return kernel_call(
        functools.partial(back_kernel, style, len(pieces), shares, per_half),
        [start],
        (2 * per_half,),
        specs,
        args,
        out_specs,
        out_shape,
        cost(2 * total * rows * k * n * shares, 2 * (total * rows * (k * shares + n) + k * n)),
        hold,
    )


def weight_kernel(left_count, right_count, start_ref, *refs):
    lefts, rights, out = refs[:left_count], refs[left_count : left_count + right_count], refs[-1]

    def views(group):
        found = []
        for ref in group:
            found += [ref] if len(ref.shape) == 2 else [ref.at[i] for i in range(ref.shape[0])]
        return found

    total = None
    for a, b in zip(views(lefts), views(rights)):
        part = dot(a[...], b[...], 0, 0)
        total = part if total is None else total + part
    low = total.astype(BF)
    if len(out.shape) == 2:
        out[...] = low
    else:
        h, z, t, r, n = out.shape
        for o in range(h):
            for i in range(t):
                base = (o * t + i) * z * r
                out[o, :, i] = low[base : base + z * r].reshape(z, r, n)


def weight_product(left, right, start, which, spread=None, cut=(0, 1, 1), tile=512, hold=()):
    def spec(group, width, index):
        found = []
        for a in group:
            if a.ndim == 2:
                found.append(pl.BlockSpec((a.shape[0], width), lambda j, s: (0, index(j, s))))
            else:
                found.append(pl.BlockSpec(a.shape[:2] + (width,), lambda j, s: (0, 0, index(j, s))))
        return found

    half = left[0].shape[-1] // (1 if which is None else 2)
    share = right[0].shape[-1] // cut[2]
    n = share * (cut[1] - cut[0])
    tile = min(tile, share)
    skip = cut[0] * (share // tile)
    rows = sum(a.shape[0] if a.ndim == 2 else a.shape[0] * a.shape[1] for a in left)
    specs = spec(left, half, lambda j, s: 0 if which is None else s[0] if which == 0 else 1 - s[0])
    specs += spec(right, tile, lambda j, s: j + skip)
    shape = (half, n) if spread is None else spread + (n,)
    block = shape[:-1] + (tile,)
    return kernel_call(
        functools.partial(weight_kernel, len(left), len(right)),
        [start],
        (n // tile,),
        specs,
        [*left, *right],
        pl.BlockSpec(block, lambda j, s: (0,) * (len(block) - 1) + (j,)),
        jax.ShapeDtypeStruct(shape, BF),
        cost(2 * rows * half * n, 2 * (rows * (half + n) + half * n)),
        hold,
    )


def pair_masks():
    lane = lax.broadcasted_iota(jnp.int32, (1, 2 * HD), 1)
    low = jnp.where(lane < HD, 1.0, 0.0).astype(BF)
    high = jnp.where(lane < HD, 0.0, 1.0).astype(BF)
    return low, high


def pair_probs(q_two, k):
    scores = dot(q_two, k, 1, 1) * 0.125
    row = lax.broadcasted_iota(jnp.int32, scores.shape, 0) & (SLOT - 1)
    column = lax.broadcasted_iota(jnp.int32, scores.shape, 1)
    scores = jnp.where(row >= column, scores, MASKED)
    exponent = jnp.exp(scores - jnp.max(scores, axis=-1, keepdims=True))
    return exponent / jnp.sum(exponent, axis=-1, keepdims=True)


def attend_kernel(q_ref, k_ref, v_ref, context_ref):
    low, high = pair_masks()
    for at in range(0, context_ref.shape[1], 2 * HD):
        q, k, v = [ref[:, at : at + 2 * HD] for ref in (q_ref, k_ref, v_ref)]
        probs = pair_probs(jnp.concatenate([q * low, q * high], axis=0), k).astype(BF)
        context = dot(probs[:SLOT], v * low, 1, 0) + dot(probs[SLOT:], v * high, 1, 0)
        context_ref[:, at : at + 2 * HD] = context.astype(BF)


def attend_back_kernel(q_ref, k_ref, v_ref, grad_ref, out_ref, sum_ref):
    part = grad_ref.shape[1]
    low, high = pair_masks()

    @pl.when(pl.program_id(0) == 0)
    def _():
        sum_ref[...] = jnp.zeros_like(sum_ref)

    for at in range(0, part, 2 * HD):
        q, k, v, grad = [ref[:, at : at + 2 * HD] for ref in (q_ref, k_ref, v_ref, grad_ref)]
        q_two = jnp.concatenate([q * low, q * high], axis=0)
        g_two = jnp.concatenate([grad * low, grad * high], axis=0)
        probs = pair_probs(q_two, k)
        d_probs = dot(g_two, v, 1, 1)
        row_dot = jnp.sum(probs * d_probs, axis=-1, keepdims=True)
        d_scores = (probs * (d_probs - row_dot)).astype(BF)
        d_q = dot(d_scores[:SLOT], k * low, 1, 0) + dot(d_scores[SLOT:], k * high, 1, 0)
        d_k = dot(d_scores, q_two, 0, 0)
        d_v = dot(probs.astype(BF), g_two, 0, 0)
        for i, value in enumerate((d_q * 0.125, d_k * 0.125, d_v)):
            where = slice(i * part + at, i * part + at + 2 * HD)
            value = value.astype(BF)
            out_ref[:, where] = value
            sum_ref[:, where] += jnp.sum(value.astype(F32), axis=0, keepdims=True)


def attend(q, k, v, hold=()):
    rows, part = q.shape
    one = pl.BlockSpec((SLOT, part), lambda i: (i, 0))
    return kernel_call(
        attend_kernel,
        [],
        (rows // SLOT,),
        [one] * 3,
        [q, k, v],
        one,
        jax.ShapeDtypeStruct((rows, part), BF),
        cost(32 * rows * SLOT * part, 8 * rows * part, rows * SLOT * part // HD),
        hold,
    )


def attend_back(q, k, v, grad, first, hold=()):
    rows, part = grad.shape
    one = pl.BlockSpec((SLOT, part), lambda i: (i, 0))
    shifted = pl.BlockSpec((SLOT, part), lambda i: (i + first, 0))
    return kernel_call(
        attend_back_kernel,
        [],
        (rows // SLOT,),
        [shifted] * 3 + [one],
        [q, k, v, grad],
        [pl.BlockSpec((SLOT, 3 * part), lambda i: (i, 0)), still((1, 3 * part))],
        [jax.ShapeDtypeStruct((rows, 3 * part), BF), jax.ShapeDtypeStruct((1, 3 * part), F32)],
        cost(80 * rows * SLOT * part, 14 * rows * part, rows * SLOT * part // HD),
        hold,
    )


def normal_of(values):
    centred = values - jnp.mean(values, axis=-1, keepdims=True)
    inverse = lax.rsqrt(jnp.mean(centred * centred, axis=-1, keepdims=True) + EPSILON)
    return centred * inverse, inverse


def rows_of(refs):
    total = refs[0][...].astype(F32)
    for ref in refs[1:]:
        total = total + ref[...].astype(F32)
    return total


def norm_kernel(x_ref, gain_ref, shift_ref, out_ref):
    normal, _ = normal_of(x_ref[...].astype(F32))
    out_ref[...] = (normal * gain_ref[...] + shift_ref[...]).astype(BF)


def join_norm_kernel(count, *refs):
    bias, gain, shift, hidden_ref, out_ref = refs[count:]
    hidden = rows_of(refs[:count]) + bias[...]
    hidden_ref[...] = hidden
    normal, _ = normal_of(hidden)
    out_ref[...] = (normal * gain[...] + shift[...]).astype(BF)


def join_kernel(count, *refs):
    refs[count + 1][...] = (rows_of(refs[:count]) + refs[count][...]).astype(BF)


def norm_back_kernel(count, *refs):
    source, carry, gain, grad_ref, low_ref, sums = refs[count:]
    grad = rows_of(refs[:count])
    normal, inverse = normal_of(source[...].astype(F32))
    scaled = grad * gain[...]
    centre = jnp.mean(scaled, axis=-1, keepdims=True)
    projected = jnp.mean(scaled * normal, axis=-1, keepdims=True)
    carried = carry[...].astype(F32)
    result = carried + inverse * (scaled - centre - normal * projected)
    grad_ref[...] = result.astype(grad_ref.dtype)
    low = result.astype(BF)
    low_ref[...] = low

    @pl.when(pl.program_id(0) == 0)
    def _():
        sums[...] = jnp.zeros_like(sums)

    for i, value in enumerate((grad * normal, grad, low.astype(F32), carried)):
        sums[i : i + 1] += jnp.sum(value, axis=0, keepdims=True)


def add_kernel(a_ref, b_ref, out_ref):
    out_ref[...] = (a_ref[...].astype(F32) + b_ref[...].astype(F32)).astype(BF)


def add_low(a, b, hold=()):
    width = a.shape[-1]
    flat = [x.reshape(-1, width) for x in (a, b)]
    rows = flat[0].shape[0]
    step = min(rows, 256)
    one = pl.BlockSpec((step, width), lambda i: (i, 0))
    result = kernel_call(
        add_kernel,
        [],
        (rows // step,),
        [one, one],
        flat,
        one,
        jax.ShapeDtypeStruct((rows, width), BF),
        cost(rows * width, 6 * rows * width),
        hold,
    )
    return result.reshape(a.shape)


def row_call(kernel, blocks, vectors, outs, sums=0, step=128, hold=()):
    rows, width = blocks[0].shape
    one = pl.BlockSpec((step, width), lambda i: (i, 0))
    out_specs = [one] * len(outs)
    out_shape = [jax.ShapeDtypeStruct((rows, width), d) for d in outs]
    if sums:
        out_specs.append(still((sums, width)))
        out_shape.append(jax.ShapeDtypeStruct((sums, width), F32))
    return kernel_call(
        kernel,
        [],
        (rows // step,),
        [one] * len(blocks) + [still((1, width))] * len(vectors),
        [*blocks, *[v.reshape(1, width) for v in vectors]],
        out_specs,
        out_shape,
        cost(20 * rows * width, 16 * rows * width),
        hold,
    )


def body(
    tokens,
    cotangent,
    doc_starts,
    active_len,
    ln1_gain,
    ln1_bias,
    q_weight,
    q_bias,
    k_weight,
    v_weight,
    v_bias,
    o_weight,
    o_bias,
    ln2_gain,
    ln2_bias,
    up_weight,
    up_bias,
    down_weight,
    down_bias,
):
    depth = lax.axis_size("fsdp")
    outer = lax.axis_size("outer")
    devices = outer * TEAM * depth
    member, me = lax.axis_index("team"), lax.axis_index("outer")
    layer = lax.axis_index("fsdp")
    start = (me if outer == 2 else jnp.zeros_like(me)).reshape(1)
    groups, row_len, width = tokens.shape
    docs = doc_starts.shape[1]
    r = q_weight.shape[0]
    part_width = width // TEAM
    rows = groups * docs * SLOT

    zero_bias = jnp.zeros((part_width,), F32)

    def depth_gather(a):
        return lax.all_gather(a, "fsdp", axis=0, tiled=True)

    def columns(a, i, n):
        c = a.shape[1] // n
        return a[:, i * c : (i + 1) * c]

    def stored(block):
        return block.reshape(1, depth, TEAM, r, block.shape[1])

    def flat(block):
        return block[None]

    def both_halves(block, *hold):
        return outer_halves(pin(block, *hold) if hold else block, me)

    def flatten(halves):
        return [h.reshape(-1, h.shape[-1]) for h in halves]

    deal = deal_columns((q_weight, k_weight, v_weight, up_weight), member, outer, depth)
    qkv_deal, up_deal = deal[:, : 3 * part_width], deal[:, 3 * part_width :]
    block_q, block_k, block_v = [stored(depth_gather(columns(qkv_deal, i, 3))) for i in range(3)]
    w_q, w_k = [both_halves(b) for b in (block_q, block_k)]
    block_o = flat(depth_gather(o_weight))

    vectors = (ln1_gain, ln1_bias, o_bias, ln2_gain, ln2_bias, down_bias, q_bias, v_bias, up_bias)
    packed = gather_small(jnp.concatenate(vectors), member, me, layer)
    edges = [0]
    for v in vectors:
        edges.append(edges[-1] + v.shape[0])
    pieces = [packed[:, edges[i] : edges[i + 1]] for i in range(len(vectors))]
    gain1, shift1, bias_o, gain2, shift2, bias_down = [p.reshape(-1) for p in pieces[:6]]

    def member_part(p):
        whole = p.reshape(outer, TEAM, depth, -1)
        return lax.dynamic_index_in_dim(whole, member, 1, False).reshape(-1)

    bias_q, bias_v, bias_up = [member_part(p) for p in pieces[6:]]

    position = jnp.arange(row_len, dtype=jnp.int32)
    offset = jnp.arange(SLOT, dtype=jnp.int32)
    wanted = doc_starts[:, :, None] + offset
    live = offset < active_len[:, :, None]
    chosen = (wanted[..., None] == position) & live[..., None]
    chosen = chosen.reshape(groups, docs * SLOT, row_len)
    select = chosen.astype(BF)
    covered = jnp.any(chosen, axis=1)

    def pack(source):
        picked = jnp.einsum("gst,gtd->gsd", select, source, preferred_element_type=F32)
        return picked.reshape(rows, width).astype(BF)

    def unpack(slot_rows, fallback):
        blocks = slot_rows.reshape(groups, docs * SLOT, width)
        placed = jnp.einsum("gst,gsd->gtd", select, blocks, preferred_element_type=F32).astype(BF)
        return jnp.where(covered[..., None], placed, fallback)

    class Order:
        last = ()

        def step(self, kernel, *args, hold=(), **kw):
            result = kernel(*args, hold=self.last + tuple(hold), **kw)
            self.last = (jax.tree.leaves(result)[-1],)
            return result

    order = Order()

    def begin(weights):
        return jnp.zeros_like(start) if len(weights[0]) == 1 and outer != 2 else start

    def forward(pieces, weights, *rest, **kw):
        return order.step(forward_product, pieces, weights, begin(weights), *rest, rows=rows, **kw)

    def back(pieces, weights, **kw):
        return order.step(back_product, pieces, weights, begin(weights), rows=rows, **kw)

    def weight_grad(left, right, which, **kw):
        return order.step(weight_product, left, right, start, which, **kw)

    def by_rows(kernel, blocks, *args, **kw):
        return order.step(row_call, kernel, blocks, *args, **kw)

    def add(a, b, **kw):
        return order.step(add_low, a, b, **kw)

    def team_gather(own, *hold):
        across = team_swap(own, 2)
        if hold:
            across = pin(across, *hold)
        return [own, across, team_swap(own, 1), team_swap(across, 1)]

    def send_far(parts):
        return [team_swap(p, 1) for p in parts]

    def join_near(near, far, **kw):
        across = add(near[1], far[1], **kw)
        return [near[0], far[0], team_swap(across, 2), across]

    x_rows = pack(tokens)
    (a_own,) = by_rows(norm_kernel, [x_rows], [gain1, shift1], [BF])
    a_own = pin(a_own, block_o)
    a_across = team_swap(a_own, 2)
    w_o = flatten(both_halves(block_o))
    a_across = pin(a_across, w_q[1], w_o[1])
    a_all = [a_own, a_across, team_swap(a_own, 1), team_swap(a_across, 1)]
    block_up = [stored(depth_gather(columns(up_deal, i, 2))) for i in range(2)]
    g_rows = pack(cotangent)
    g_all = team_gather(pin(g_rows, a_all[1]))

    wide = TEAM * rows
    q = forward(a_all, [w_q], bias_q)[0]
    k = forward(a_all, [w_k], zero_bias)[0]
    w_v = both_halves(block_v, q)
    v = forward(a_all, [w_v], bias_v)[0]
    q, k, v = [s.reshape(wide, part_width) for s in (q, k, v)]
    context = order.step(attend, q, k, v, hold=[g_all[1]]).reshape(TEAM, rows, part_width)
    if outer == 2:
        down_pair = jnp.stack([down_weight, outer_pass(pin(down_weight, k))])[None]
        w_down = [[depth_gather(pin(down_pair, context))]]
    else:
        w_down = [[lax.all_gather(down_weight, SPREAD, axis=0, tiled=True)]]
    o_far = send_far(forward([context], [w_o], style="bare", pick=(1, 2)))
    o_near = forward([context], [w_o], style="bare", pick=(0, 2))
    w_up = [both_halves(block_up[0], context)]
    *o_parts, o_across = join_near(o_near, o_far)
    hidden, b_own = by_rows(
        functools.partial(join_norm_kernel, 4),
        [x_rows] + o_parts,
        [bias_o, gain2, shift2],
        [F32, BF],
        hold=[w_up[0][1]],
    )
    w_up.append(both_halves(block_up[1], b_own))
    b_all = team_gather(b_own, w_up[1][1])

    active, slope = forward(b_all, w_up, bias_up, style="gate")

    def depth_scatter(a):
        return lax.psum_scatter(a, "fsdp", scatter_dimension=0, tiled=True)

    def send_away(away, *hold):
        if outer != 2:
            return away
        return outer_pass(pin(away, *hold) if hold else away)

    def settle(sent, mine, **kw):
        c = mine.shape[-1]
        if outer == 2:
            total = add(sent, mine, **kw)
        else:
            both = jnp.concatenate([mine.reshape(outer // 2, -1, c), sent.reshape(outer // 2, -1, c)])
            total = outer_scatter(both, me)
        return depth_scatter(total.reshape(-1, c))

    spread = (outer // 2, depth, TEAM, r)

    def settle_whole(grad):
        return lax.psum_scatter(grad, SPREAD, scatter_dimension=0, tiled=True)

    grad_down = [settle_whole(weight_grad([active], g_all, None, cut=(0, 1, 2)))]
    grad_down.append(settle_whole(weight_grad([active], g_all, None, cut=(1, 2, 2))))
    d_inner, sum_inner = back(g_all, w_down, style="slope", slope=slope)
    n_far = send_far(back([d_inner], w_up, style="bare", pick=(1, 2)))
    n_near = back([d_inner], w_up, style="bare", pick=(0, 2))
    n_parts = join_near(n_near, n_far)[:3]
    up_sent = [
        send_away(weight_grad(b_all, [d_inner], 1, spread=spread, cut=(i, i + 1, 2))) for i in range(2)
    ]
    up_mine = [weight_grad(b_all, [d_inner], 0, spread=spread, cut=(i, i + 1, 2)) for i in range(2)]
    d_hidden, d_out, sums2 = by_rows(
        functools.partial(norm_back_kernel, 3), n_parts + [hidden, g_rows], [gain2], [F32, BF], sums=4
    )
    y_far = send_far(forward([active], w_down, style="bare", pick=(1, 2), hold=[grad_down[0]]))
    y_near = forward([active], w_down, style="bare", pick=(0, 2))
    d_out_all = team_gather(d_out, up_sent[0], y_near[1])

    (d_near,) = back(d_out_all[:2], [w_o])
    (d_far,) = back(d_out_all[2:], [w_o])
    grad_up = [settle(up_sent[0], up_mine[0], hold=[grad_down[1]])]
    *y_parts, y_across = join_near(y_near, y_far)
    q_far, sum_far = order.step(attend_back, q, k, v, d_far.reshape(2 * rows, -1), 2 * rows // SLOT)
    q_far = q_far.reshape(2, rows, -1)
    a_far = send_far(back([q_far], [w_q, w_k, w_v], style="bare"))
    grad_up.append(settle(up_sent[1], up_mine[1]))
    o_sent = send_away(weight_grad([context], d_out_all, 1))
    o_mine = weight_grad([context], d_out_all, 0)
    q_near, sum_near = order.step(attend_back, q, k, v, d_near.reshape(2 * rows, -1), 0, hold=[grad_up[0]])
    q_near = q_near.reshape(2, rows, -1)
    grad_o = settle(o_sent, o_mine)
    a_near = back([q_near], [w_q, w_k, w_v], style="bare")
    a_parts = join_near(a_near, a_far, hold=[y_parts[2]])[:3]
    parts = ((0, 1, 3), (1, 3, 3))
    d_both = [q_near, q_far]
    qkv_sent = [
        send_away(weight_grad(a_all, d_both, 1, spread=spread, cut=parts[0], hold=[grad_up[1]])),
        send_away(weight_grad(a_all, d_both, 1, spread=spread, cut=parts[1], hold=[grad_o])),
    ]
    grad_q = settle(qkv_sent[0], weight_grad(a_all, d_both, 0, spread=spread, cut=parts[0]))
    kv_mine = weight_grad(a_all, d_both, 0, spread=spread, cut=parts[1])
    (y_rows,) = by_rows(functools.partial(join_kernel, 4), [hidden] + y_parts, [bias_down], [BF])
    layer_out = unpack(y_rows, tokens)
    _, d_input, sums1 = by_rows(
        functools.partial(norm_back_kernel, 3),
        a_parts + [x_rows, d_hidden],
        [gain1],
        [BF, BF],
        sums=4,
        hold=[layer_out],
    )
    grad_kv = settle(qkv_sent[1], kv_mine)
    sum_qkv = sum_far + sum_near
    grad_o = grad_o.astype(F32)
    input_grad = unpack(d_input, cotangent)
    grad_down = jnp.concatenate([g.astype(F32) for g in grad_down], axis=1)
    (grad_up,) = return_columns(jnp.concatenate(grad_up, axis=1), member, outer, depth, 1)
    (grad_q,) = return_columns(grad_q, member, outer, depth, 1)
    grad_k, grad_v = return_columns(grad_kv, member, outer, depth, 2)

    whole_sums = [sums1[0], sums1[1], sums2[2], sums2[0], sums2[1], sums2[3]]
    part_sums = [sum_qkv[0, :part_width], sum_qkv[0, 2 * part_width :], sum_inner[0]]
    is_mine = (jnp.arange(TEAM) == member)[None, :, None, None]

    def widen(s):
        blocks = s.reshape(outer, 1, depth, -1)
        return jnp.where(is_mine, blocks, 0.0).reshape(devices, -1)

    table = jnp.concatenate([s.reshape(devices, -1) for s in whole_sums] + [widen(s) for s in part_sums], axis=1)
    small = reduce_small(table, member, me, layer)
    cuts = [small[edges[i] : edges[i + 1]] for i in range(len(vectors))]
    g_gain1, g_shift1, g_bias_o, g_gain2, g_shift2, g_bias_down, g_bias_q, g_bias_v, g_bias_up = cuts
    return (
        layer_out,
        input_grad,
        g_gain1,
        g_shift1,
        grad_q,
        g_bias_q,
        grad_k,
        grad_v,
        g_bias_v,
        grad_o,
        g_bias_o,
        g_gain2,
        g_shift2,
        grad_up,
        g_bias_up,
        grad_down,
        g_bias_down,
    )


def solution(mesh):
    outer = mesh.shape["dp"] // TEAM
    devices = mesh.devices.reshape(outer, TEAM, mesh.shape["fsdp"])
    fine = Mesh(devices, ALL)
    kinds = {"t": P(ALL, None, None), "w": P(ALL, None), "v": P(ALL)}
    vectors = "vvwvwwvwvvvwvwv"
    in_specs = tuple(kinds[c] for c in "ttww" + vectors)
    out_specs = tuple(kinds[c] for c in "tt" + vectors)
    return jax.shard_map(body, mesh=fine, in_specs=in_specs, out_specs=out_specs, check_vma=False)
```

```python
import functools

import jax
import jax.numpy as jnp
from jax import lax
from jax.experimental import pallas as pl
from jax.experimental.pallas import tpu as pltpu
from jax.sharding import Mesh
from jax.sharding import PartitionSpec as P

HD = 64
SLOT = 128
TEAM = 4
TILE = 256
HASTE = 1000
VMEM = 48 * 2**20

EPSILON = 1e-05
MASKED = -1e30
ROOT_HALF = 0.7071067811865476
DENSITY_SCALE = 0.3989422804014327
BF = jnp.bfloat16
F32 = jnp.float32
ALL = ("outer", "team", "fsdp")
SPREAD = ("outer", "fsdp")


def dot(a, b, ca, cb):
    return lax.dot_general(a, b, (((ca,), (cb,)), ((), ())), preferred_element_type=F32)


def team_swap(a, flip):
    return lax.ppermute(a, "team", [(i, i ^ flip) for i in range(TEAM)])


def ring_order(size):
    return list(range(0, size, 2)) + list(range(1, size, 2))[::-1]


def outer_pass(a):
    outer = lax.axis_size("outer")
    order = ring_order(outer)
    return lax.ppermute(a, "outer", [(o, order[(p + 1) % outer]) for p, o in enumerate(order)])


def outer_place(me):
    outer = lax.axis_size("outer")
    order = ring_order(outer)
    place = [0] * outer
    for p, o in enumerate(order):
        place[o] = p
    return jnp.asarray(order, jnp.int32), jnp.asarray(place, jnp.int32)[me]


def outer_halves(a, me):
    outer = lax.axis_size("outer")
    if outer == 2:
        return [a, outer_pass(a)]
    order, place = outer_place(me)
    whole = jnp.zeros((outer,) + a.shape[1:], a.dtype)
    whole = lax.dynamic_update_slice_in_dim(whole, a, me, 0)
    moving = a
    for step in range(1, outer):
        moving = outer_pass(moving)
        whole = lax.dynamic_update_slice_in_dim(whole, moving, order[(place - step) % outer], 0)
    return [whole[: outer // 2], whole[outer // 2 :]]


def outer_scatter(blocks, me):
    outer = lax.axis_size("outer")
    order, place = outer_place(me)
    moving = lax.dynamic_slice_in_dim(blocks, order[(place - 1) % outer], 1, 0)
    for step in range(1, outer):
        moving = outer_pass(moving)
        mine = lax.dynamic_slice_in_dim(blocks, order[(place - 1 - step) % outer], 1, 0)
        moving = (moving.astype(F32) + mine.astype(F32)).astype(BF)
    return moving


def by_team(stacked, member):
    odd = (member & 1) == 1
    high = (member & 2) == 2
    a = [jnp.where(odd, stacked[i ^ 1], stacked[i]) for i in range(4)]
    return [jnp.where(high, a[i ^ 2], a[i]) for i in range(4)]


def deal_columns(shards, member, outer, depth):
    r = shards[0].shape[0]
    parts = [w.reshape(r, outer, TEAM, depth, -1) for w in shards]
    got = []
    for flip in range(TEAM):
        piece = jnp.concatenate(
            [lax.dynamic_index_in_dim(w, member ^ flip, 2, False).reshape(r, -1) for w in parts], axis=1
        )
        got.append(piece if flip == 0 else team_swap(piece, flip))
    return jnp.concatenate(by_team(got, member), axis=0)


def return_columns(block, member, outer, depth, shares):
    r, c = block.shape[0] // TEAM, block.shape[1] // shares
    parts = block.reshape(TEAM, r, shares * c)
    got = []
    for flip in range(TEAM):
        piece = lax.dynamic_index_in_dim(parts, member ^ flip, 0, False)
        got.append(piece if flip == 0 else team_swap(piece, flip))
    got = by_team(got, member)
    result = []
    for i in range(shares):
        cols = jnp.stack([g[:, i * c : (i + 1) * c].reshape(r, outer, depth, -1) for g in got], axis=2)
        result.append(cols.reshape(r, -1).astype(F32))
    return result


def shift_pass(a, axis, step):
    size = lax.axis_size(axis)
    return lax.ppermute(a, axis, [(i, (i + step) % size) for i in range(size)])


def gather_small(vector, member, me, layer):
    depth = lax.axis_size("fsdp")
    outer = lax.axis_size("outer")
    a = vector[None]
    a = jnp.concatenate([a if s == 0 else shift_pass(a, "fsdp", s) for s in range(depth)])
    a = jnp.concatenate([a if s == 0 else shift_pass(a, "outer", s) for s in range(outer)])
    a = jnp.concatenate([a if f == 0 else team_swap(a, f) for f in range(TEAM)])
    index = jnp.arange(TEAM * outer * depth, dtype=jnp.int32)
    flip, step, drop = index // (outer * depth), index // depth % outer, index % depth
    source = ((me - step) % outer * TEAM + (member ^ flip)) * depth + (layer - drop) % depth
    place = (index[:, None] == source[None, :]).astype(BF)
    return dot(place, a, 1, 0)


def reduce_small(table, member, me, layer):
    depth = lax.axis_size("fsdp")
    outer = lax.axis_size("outer")
    blocks = table.reshape(outer, TEAM, depth, -1)
    total = lax.dynamic_index_in_dim(blocks, member, 1, False)
    for flip in range(1, TEAM):
        total = total + team_swap(lax.dynamic_index_in_dim(blocks, member ^ flip, 1, False), flip)
    blocks = total
    total = lax.dynamic_index_in_dim(blocks, me, 0, False)
    for step in range(1, outer):
        total = total + shift_pass(
            lax.dynamic_index_in_dim(blocks, (me + step) % outer, 0, False), "outer", step
        )
    blocks = total
    total = lax.dynamic_index_in_dim(blocks, layer, 0, False)
    for step in range(1, depth):
        total = total + shift_pass(
            lax.dynamic_index_in_dim(blocks, (layer + step) % depth, 0, False), "fsdp", step
        )
    return total


def params():
    return pltpu.CompilerParams(vmem_limit_bytes=VMEM)


def cost(flops, nbytes, exps=0):
    return pl.CostEstimate(
        flops=flops // HASTE, bytes_accessed=nbytes // HASTE, transcendentals=exps // HASTE
    )


def kernel_call(kernel, prefetch, grid, specs, args, out_specs, out_shape, estimate, hold=()):
    count = len(prefetch) + len(args)

    def run(*refs):
        kernel(*refs[:count], *refs[count + len(hold) :])

    return pl.pallas_call(
        run,
        grid_spec=pltpu.PrefetchScalarGridSpec(
            num_scalar_prefetch=len(prefetch),
            grid=grid,
            in_specs=list(specs) + [pl.BlockSpec(memory_space=pl.ANY)] * len(hold),
            out_specs=out_specs,
        ),
        out_shape=out_shape,
        compiler_params=params(),
        cost_estimate=estimate,
    )(*prefetch, *args, *hold)


def pin(value, *hold):
    def run(*refs):
        del refs

    anywhere = pl.BlockSpec(memory_space=pl.ANY)
    return pl.pallas_call(
        run,
        in_specs=[anywhere] * (1 + len(hold)),
        out_specs=anywhere,
        out_shape=jax.ShapeDtypeStruct(value.shape, value.dtype),
        input_output_aliases={0: 0},
        compiler_params=params(),
        cost_estimate=cost(0, 0),
    )(value, *hold)


def still(shape, first=0):
    return pl.BlockSpec(shape, lambda *_: (first,) + (0,) * (len(shape) - 1))


def in_order(block):
    h, z, t, r, n = block.shape
    rows = [block[o, :, i].reshape(z * r, n) for o in range(h) for i in range(t)]
    return jnp.concatenate(rows, axis=0) if len(rows) > 1 else rows[0]


def half_of(start, which, size):
    at = start if which == 0 else 1 - start
    return pl.ds(pl.multiple_of(at * size, size), size)


def forward_kernel(style, count, spread, cuts, per_cut, start_ref, *refs):
    pieces, weights, rest = refs[:count], refs[count : count + 2 * cuts], refs[count + 2 * cuts :]
    start = start_ref[0]
    load = in_order if spread else (lambda b: b.reshape(-1, b.shape[-1]))
    firsts, seconds = load(weights[0][...]), load(weights[1][...])
    for i in range(1, cuts):
        late = pl.program_id(0) >= i * per_cut
        firsts = jnp.where(late, load(weights[2 * i][...]), firsts)
        seconds = jnp.where(late, load(weights[2 * i + 1][...]), seconds)
    size = firsts.shape[0]
    if style == "bare":
        outs = rest
    else:
        bias, outs = rest[0][...], rest[1:]
    at = 0
    for ref in pieces:
        views = [ref] if len(ref.shape) == 2 else [ref.at[i] for i in range(ref.shape[0])]
        for view in views:
            value = dot(view[:, half_of(start, 0, size)], firsts, 1, 0)
            value = value + dot(view[:, half_of(start, 1, size)], seconds, 1, 0)
            if style == "bare":
                outs[at][...] = value.astype(BF)
            elif style == "plain":
                outs[0][at] = (value + bias).astype(BF)
            else:
                value = value + bias
                phi = 0.5 + 0.5 * lax.erf(value * ROOT_HALF)
                outs[0][at] = (value * phi).astype(BF)
                outs[1][at] = (phi + value * DENSITY_SCALE * jnp.exp(-0.5 * value * value)).astype(BF)
            at += 1


def forward_product(pieces, weights, start, bias=None, style="plain", pick=None, rows=512, hold=()):
    whole = len(weights[0]) == 1
    sample = weights[0][0]
    spread = sample.ndim == 5
    paired = sample.ndim == 4
    cuts = len(weights)
    n = sample.shape[-1] * cuts
    tile = min(n // cuts, TILE)
    per_cut = n // cuts // tile
    stack = pieces[0].ndim == 3
    if stack:
        total = pick[1] if pick else pieces[0].shape[0]
        specs = [still((total,) + pieces[0].shape[1:], pick[0] if pick else 0)]
        k = pieces[0].shape[2]
    else:
        total, k = len(pieces), pieces[0].shape[1]
        specs = [still(p.shape) for p in pieces]
    lead = sample.shape[:-1]
    args = list(pieces)
    for i, pair in enumerate(weights):

        def at(j, s, i=i):
            return (0,) * len(lead) + (jnp.clip(j - i * per_cut, 0, per_cut - 1),)

        if paired:
            z, _, b, _ = sample.shape
            specs += [pl.BlockSpec((z, 1, b, tile), lambda j, s, h=h: (0, h, 0, j)) for h in range(2)]
            args += [pair[0], pair[0]]
        elif whole:
            specs += [pl.BlockSpec((lead[0] // 2, tile), lambda j, s, h=h: (h, j)) for h in range(2)]
            args += [pair[0], pair[0]]
        else:
            specs += [pl.BlockSpec(lead + (tile,), at)] * 2
            args += list(pair)
    if style != "bare":
        specs.append(pl.BlockSpec((1, tile), lambda j, s: (0, j)))
        args.append(bias.reshape(1, n))
    if style == "bare":
        out_specs = [pl.BlockSpec((rows, tile), lambda j, s: (0, j))] * total
        out_shape = [jax.ShapeDtypeStruct((rows, n), BF)] * total
    else:
        copies = 2 if style == "gate" else 1
        out_specs = [pl.BlockSpec((total, rows, tile), lambda j, s: (0, 0, j))] * copies
        out_shape = [jax.ShapeDtypeStruct((total, rows, n), BF)] * copies
    return kernel_call(
        functools.partial(forward_kernel, style, len(pieces), spread, cuts, per_cut),
        [start],
        (n // tile,),
        specs,
        args,
        out_specs,
        out_shape,
        cost(2 * total * rows * k * n, 2 * (total * rows * (k + n) + k * n)),
        hold,
    )


def back_kernel(style, count, shares, per_half, start_ref, *refs):
    pieces, weights, rest = refs[:count], refs[count : count + 2 * shares], refs[count + 2 * shares :]
    late = pl.program_id(0) >= per_half
    chosen = []
    for i in range(shares):
        w0, w1 = weights[2 * i][...], weights[2 * i + 1][...]
        if len(w0.shape) == 5:
            w0, w1 = in_order(w0), in_order(w1)
        elif len(w0.shape) == 4:
            w0, w1 = w0[0, 0], w1[0, 0]
        chosen.append(jnp.where(late, w1, w0))
    views = []
    for ref in pieces:
        views += [ref] if len(ref.shape) == 2 else [ref.at[i] for i in range(ref.shape[0])]
    width = chosen[0].shape[1]
    total = None
    for at, view in enumerate(views):
        value = dot(view[:, :width], chosen[0], 1, 1)
        for i in range(1, shares):
            value = value + dot(view[:, i * width : (i + 1) * width], chosen[i], 1, 1)
        if style == "slope":
            low = (value * rest[0][at].astype(F32)).astype(BF)
            rest[1][at] = low
            part = jnp.sum(low.astype(F32), axis=0, keepdims=True)
            total = part if total is None else total + part
        elif style == "plain":
            rest[0][at] = value.astype(BF)
        else:
            rest[at][...] = value.astype(BF)
    if style == "slope":
        rest[2][...] = total


def back_product(pieces, weights, start, style="plain", slope=None, pick=None, rows=512, hold=()):
    shares = len(weights)
    sample = weights[0][0]
    k = sample.shape[-1]
    half_rows = 1
    for d in sample.shape[:-1]:
        half_rows *= d
    whole = len(weights[0]) == 1
    if whole:
        half_rows //= 2
    n = 2 * half_rows
    tile = min(half_rows, TILE)
    per_half = half_rows // tile
    stack = pieces[0].ndim == 3
    if stack:
        total = pick[1] if pick else pieces[0].shape[0]
        specs = [still((total,) + pieces[0].shape[1:], pick[0] if pick else 0)]
    else:
        total = len(pieces)
        specs = [still(p.shape) for p in pieces]
    if sample.ndim == 4:
        tile = sample.shape[2]
        per_half = sample.shape[0]
        block = (1, 1, tile, k)
    elif sample.ndim == 5:
        h, z, t, r, _ = sample.shape
        group = max(1, tile // (z * r))
        tile = group * z * r
        per_half = half_rows // tile
        each = t // group
        block = (1, z, group, r, k)

        def at(j):
            return (j // each, 0, j % each, 0, 0)
    else:
        block = (tile, k)

        def at(j):
            return (j, 0)

    if sample.ndim == 4:
        first = pl.BlockSpec(block, lambda j, s: (jnp.minimum(j, per_half - 1), 0, 0, 0))
        second = pl.BlockSpec(block, lambda j, s: (jnp.maximum(j - per_half, 0), 1, 0, 0))
    else:
        first = pl.BlockSpec(block, lambda j, s: at(jnp.minimum(j, per_half - 1)))
        second = pl.BlockSpec(block, lambda j, s: at(jnp.maximum(j - per_half, 0) + (per_half if whole else 0)))
    args = list(pieces)
    for w in weights:
        specs += [first, second]
        args += [w[0], w[-1]]

    def column(j, s):
        return lax.rem(s[0] * per_half + j, 2 * per_half)

    stacked = pl.BlockSpec((total, rows, tile), lambda j, s: (0, 0, column(j, s)))
    stack_shape = jax.ShapeDtypeStruct((total, rows, n), BF)
    if style == "slope":
        specs.append(stacked)
        args.append(slope)
        out_specs = [stacked, pl.BlockSpec((1, tile), lambda j, s: (0, column(j, s)))]
        out_shape = [stack_shape, jax.ShapeDtypeStruct((1, n), F32)]
    elif style == "plain":
        out_specs, out_shape = [stacked], [stack_shape]
    else:
        out_specs = [pl.BlockSpec((rows, tile), lambda j, s: (0, column(j, s)))] * total
        out_shape = [jax.ShapeDtypeStruct((rows, n), BF)] * total
    return kernel_call(
        functools.partial(back_kernel, style, len(pieces), shares, per_half),
        [start],
        (2 * per_half,),
        specs,
        args,
        out_specs,
        out_shape,
        cost(2 * total * rows * k * n * shares, 2 * (total * rows * (k * shares + n) + k * n)),
        hold,
    )


def weight_kernel(left_count, right_count, start_ref, *refs):
    lefts, rights, out = refs[:left_count], refs[left_count : left_count + right_count], refs[-1]

    def views(group):
        found = []
        for ref in group:
            found += [ref] if len(ref.shape) == 2 else [ref.at[i] for i in range(ref.shape[0])]
        return found

    total = None
    for a, b in zip(views(lefts), views(rights)):
        part = dot(a[...], b[...], 0, 0)
        total = part if total is None else total + part
    low = total.astype(BF)
    if len(out.shape) == 2:
        out[...] = low
    else:
        h, z, t, r, n = out.shape
        for o in range(h):
            for i in range(t):
                base = (o * t + i) * z * r
                out[o, :, i] = low[base : base + z * r].reshape(z, r, n)


def weight_product(left, right, start, which, spread=None, cut=(0, 1, 1), tile=512, hold=()):
    def spec(group, width, index):
        found = []
        for a in group:
            if a.ndim == 2:
                found.append(pl.BlockSpec((a.shape[0], width), lambda j, s: (0, index(j, s))))
            else:
                found.append(pl.BlockSpec(a.shape[:2] + (width,), lambda j, s: (0, 0, index(j, s))))
        return found

    half = left[0].shape[-1] // (1 if which is None else 2)
    share = right[0].shape[-1] // cut[2]
    n = share * (cut[1] - cut[0])
    tile = min(tile, share)
    skip = cut[0] * (share // tile)
    rows = sum(a.shape[0] if a.ndim == 2 else a.shape[0] * a.shape[1] for a in left)
    specs = spec(left, half, lambda j, s: 0 if which is None else s[0] if which == 0 else 1 - s[0])
    specs += spec(right, tile, lambda j, s: j + skip)
    shape = (half, n) if spread is None else spread + (n,)
    block = shape[:-1] + (tile,)
    return kernel_call(
        functools.partial(weight_kernel, len(left), len(right)),
        [start],
        (n // tile,),
        specs,
        [*left, *right],
        pl.BlockSpec(block, lambda j, s: (0,) * (len(block) - 1) + (j,)),
        jax.ShapeDtypeStruct(shape, BF),
        cost(2 * rows * half * n, 2 * (rows * (half + n) + half * n)),
        hold,
    )


def pair_masks():
    lane = lax.broadcasted_iota(jnp.int32, (1, 2 * HD), 1)
    low = jnp.where(lane < HD, 1.0, 0.0).astype(BF)
    high = jnp.where(lane < HD, 0.0, 1.0).astype(BF)
    return low, high


def pair_probs(q_two, k):
    scores = dot(q_two, k, 1, 1) * 0.125
    row = lax.broadcasted_iota(jnp.int32, scores.shape, 0) & (SLOT - 1)
    column = lax.broadcasted_iota(jnp.int32, scores.shape, 1)
    scores = jnp.where(row >= column, scores, MASKED)
    exponent = jnp.exp(scores - jnp.max(scores, axis=-1, keepdims=True))
    return exponent / jnp.sum(exponent, axis=-1, keepdims=True)


def attend_kernel(q_ref, k_ref, v_ref, context_ref):
    low, high = pair_masks()
    for at in range(0, context_ref.shape[1], 2 * HD):
        q, k, v = [ref[:, at : at + 2 * HD] for ref in (q_ref, k_ref, v_ref)]
        probs = pair_probs(jnp.concatenate([q * low, q * high], axis=0), k).astype(BF)
        context = dot(probs[:SLOT], v * low, 1, 0) + dot(probs[SLOT:], v * high, 1, 0)
        context_ref[:, at : at + 2 * HD] = context.astype(BF)


def attend_back_kernel(q_ref, k_ref, v_ref, grad_ref, out_ref, sum_ref):
    part = grad_ref.shape[1]
    low, high = pair_masks()

    @pl.when(pl.program_id(0) == 0)
    def _():
        sum_ref[...] = jnp.zeros_like(sum_ref)

    for at in range(0, part, 2 * HD):
        q, k, v, grad = [ref[:, at : at + 2 * HD] for ref in (q_ref, k_ref, v_ref, grad_ref)]
        q_two = jnp.concatenate([q * low, q * high], axis=0)
        g_two = jnp.concatenate([grad * low, grad * high], axis=0)
        probs = pair_probs(q_two, k)
        d_probs = dot(g_two, v, 1, 1)
        row_dot = jnp.sum(probs * d_probs, axis=-1, keepdims=True)
        d_scores = (probs * (d_probs - row_dot)).astype(BF)
        d_q = dot(d_scores[:SLOT], k * low, 1, 0) + dot(d_scores[SLOT:], k * high, 1, 0)
        d_k = dot(d_scores, q_two, 0, 0)
        d_v = dot(probs.astype(BF), g_two, 0, 0)
        for i, value in enumerate((d_q * 0.125, d_k * 0.125, d_v)):
            where = slice(i * part + at, i * part + at + 2 * HD)
            value = value.astype(BF)
            out_ref[:, where] = value
            sum_ref[:, where] += jnp.sum(value.astype(F32), axis=0, keepdims=True)


def attend(q, k, v, hold=()):
    rows, part = q.shape
    one = pl.BlockSpec((SLOT, part), lambda i: (i, 0))
    return kernel_call(
        attend_kernel,
        [],
        (rows // SLOT,),
        [one] * 3,
        [q, k, v],
        one,
        jax.ShapeDtypeStruct((rows, part), BF),
        cost(32 * rows * SLOT * part, 8 * rows * part, rows * SLOT * part // HD),
        hold,
    )


def attend_back(q, k, v, grad, first, hold=()):
    rows, part = grad.shape
    one = pl.BlockSpec((SLOT, part), lambda i: (i, 0))
    shifted = pl.BlockSpec((SLOT, part), lambda i: (i + first, 0))
    return kernel_call(
        attend_back_kernel,
        [],
        (rows // SLOT,),
        [shifted] * 3 + [one],
        [q, k, v, grad],
        [pl.BlockSpec((SLOT, 3 * part), lambda i: (i, 0)), still((1, 3 * part))],
        [jax.ShapeDtypeStruct((rows, 3 * part), BF), jax.ShapeDtypeStruct((1, 3 * part), F32)],
        cost(80 * rows * SLOT * part, 14 * rows * part, rows * SLOT * part // HD),
        hold,
    )


def normal_of(values):
    centred = values - jnp.mean(values, axis=-1, keepdims=True)
    inverse = lax.rsqrt(jnp.mean(centred * centred, axis=-1, keepdims=True) + EPSILON)
    return centred * inverse, inverse


def rows_of(refs):
    total = refs[0][...].astype(F32)
    for ref in refs[1:]:
        total = total + ref[...].astype(F32)
    return total


def norm_kernel(x_ref, gain_ref, shift_ref, out_ref):
    normal, _ = normal_of(x_ref[...].astype(F32))
    out_ref[...] = (normal * gain_ref[...] + shift_ref[...]).astype(BF)


def join_norm_kernel(count, *refs):
    bias, gain, shift, hidden_ref, out_ref = refs[count:]
    hidden = rows_of(refs[:count]) + bias[...]
    hidden_ref[...] = hidden
    normal, _ = normal_of(hidden)
    out_ref[...] = (normal * gain[...] + shift[...]).astype(BF)


def join_kernel(count, *refs):
    refs[count + 1][...] = (rows_of(refs[:count]) + refs[count][...]).astype(BF)


def norm_back_kernel(count, *refs):
    source, carry, gain, grad_ref, low_ref, sums = refs[count:]
    grad = rows_of(refs[:count])
    normal, inverse = normal_of(source[...].astype(F32))
    scaled = grad * gain[...]
    centre = jnp.mean(scaled, axis=-1, keepdims=True)
    projected = jnp.mean(scaled * normal, axis=-1, keepdims=True)
    carried = carry[...].astype(F32)
    result = carried + inverse * (scaled - centre - normal * projected)
    grad_ref[...] = result.astype(grad_ref.dtype)
    low = result.astype(BF)
    low_ref[...] = low

    @pl.when(pl.program_id(0) == 0)
    def _():
        sums[...] = jnp.zeros_like(sums)

    for i, value in enumerate((grad * normal, grad, low.astype(F32), carried)):
        sums[i : i + 1] += jnp.sum(value, axis=0, keepdims=True)


def add_kernel(a_ref, b_ref, out_ref):
    out_ref[...] = (a_ref[...].astype(F32) + b_ref[...].astype(F32)).astype(BF)


def add_low(a, b, hold=()):
    width = a.shape[-1]
    flat = [x.reshape(-1, width) for x in (a, b)]
    rows = flat[0].shape[0]
    step = min(rows, 256)
    one = pl.BlockSpec((step, width), lambda i: (i, 0))
    result = kernel_call(
        add_kernel,
        [],
        (rows // step,),
        [one, one],
        flat,
        one,
        jax.ShapeDtypeStruct((rows, width), BF),
        cost(rows * width, 6 * rows * width),
        hold,
    )
    return result.reshape(a.shape)


def row_call(kernel, blocks, vectors, outs, sums=0, step=128, hold=()):
    rows, width = blocks[0].shape
    one = pl.BlockSpec((step, width), lambda i: (i, 0))
    out_specs = [one] * len(outs)
    out_shape = [jax.ShapeDtypeStruct((rows, width), d) for d in outs]
    if sums:
        out_specs.append(still((sums, width)))
        out_shape.append(jax.ShapeDtypeStruct((sums, width), F32))
    return kernel_call(
        kernel,
        [],
        (rows // step,),
        [one] * len(blocks) + [still((1, width))] * len(vectors),
        [*blocks, *[v.reshape(1, width) for v in vectors]],
        out_specs,
        out_shape,
        cost(20 * rows * width, 16 * rows * width),
        hold,
    )


def body(
    tokens,
    cotangent,
    doc_starts,
    active_len,
    ln1_gain,
    ln1_bias,
    q_weight,
    q_bias,
    k_weight,
    v_weight,
    v_bias,
    o_weight,
    o_bias,
    ln2_gain,
    ln2_bias,
    up_weight,
    up_bias,
    down_weight,
    down_bias,
):
    depth = lax.axis_size("fsdp")
    outer = lax.axis_size("outer")
    devices = outer * TEAM * depth
    member, me = lax.axis_index("team"), lax.axis_index("outer")
    layer = lax.axis_index("fsdp")
    start = (me if outer == 2 else jnp.zeros_like(me)).reshape(1)
    groups, row_len, width = tokens.shape
    docs = doc_starts.shape[1]
    r = q_weight.shape[0]
    part_width = width // TEAM
    rows = groups * docs * SLOT

    zero_bias = jnp.zeros((part_width,), F32)

    def depth_gather(a):
        return lax.all_gather(a, "fsdp", axis=0, tiled=True)

    def columns(a, i, n):
        c = a.shape[1] // n
        return a[:, i * c : (i + 1) * c]

    def stored(block):
        return block.reshape(1, depth, TEAM, r, block.shape[1])

    def flat(block):
        return block[None]

    def both_halves(block, *hold):
        return outer_halves(pin(block, *hold) if hold else block, me)

    def flatten(halves):
        return [h.reshape(-1, h.shape[-1]) for h in halves]

    deal = deal_columns((q_weight, k_weight, v_weight, up_weight), member, outer, depth)
    qkv_deal, up_deal = deal[:, : 3 * part_width], deal[:, 3 * part_width :]
    block_q, block_k, block_v = [stored(depth_gather(columns(qkv_deal, i, 3))) for i in range(3)]
    w_q, w_k = [both_halves(b) for b in (block_q, block_k)]
    block_o = flat(depth_gather(o_weight))

    vectors = (ln1_gain, ln1_bias, o_bias, ln2_gain, ln2_bias, down_bias, q_bias, v_bias, up_bias)
    packed = gather_small(jnp.concatenate(vectors), member, me, layer)
    edges = [0]
    for v in vectors:
        edges.append(edges[-1] + v.shape[0])
    pieces = [packed[:, edges[i] : edges[i + 1]] for i in range(len(vectors))]
    gain1, shift1, bias_o, gain2, shift2, bias_down = [p.reshape(-1) for p in pieces[:6]]

    def member_part(p):
        whole = p.reshape(outer, TEAM, depth, -1)
        return lax.dynamic_index_in_dim(whole, member, 1, False).reshape(-1)

    bias_q, bias_v, bias_up = [member_part(p) for p in pieces[6:]]

    position = jnp.arange(row_len, dtype=jnp.int32)
    offset = jnp.arange(SLOT, dtype=jnp.int32)
    wanted = doc_starts[:, :, None] + offset
    live = offset < active_len[:, :, None]
    chosen = (wanted[..., None] == position) & live[..., None]
    chosen = chosen.reshape(groups, docs * SLOT, row_len)
    select = chosen.astype(BF)
    covered = jnp.any(chosen, axis=1)

    def pack(source):
        picked = jnp.einsum("gst,gtd->gsd", select, source, preferred_element_type=F32)
        return picked.reshape(rows, width).astype(BF)

    def unpack(slot_rows, fallback):
        blocks = slot_rows.reshape(groups, docs * SLOT, width)
        placed = jnp.einsum("gst,gsd->gtd", select, blocks, preferred_element_type=F32).astype(BF)
        return jnp.where(covered[..., None], placed, fallback)

    class Order:
        last = ()

        def step(self, kernel, *args, hold=(), **kw):
            result = kernel(*args, hold=self.last + tuple(hold), **kw)
            self.last = (jax.tree.leaves(result)[-1],)
            return result

    order = Order()

    def begin(weights):
        return jnp.zeros_like(start) if len(weights[0]) == 1 and outer != 2 else start

    def forward(pieces, weights, *rest, **kw):
        return order.step(forward_product, pieces, weights, begin(weights), *rest, rows=rows, **kw)

    def back(pieces, weights, **kw):
        return order.step(back_product, pieces, weights, begin(weights), rows=rows, **kw)

    def weight_grad(left, right, which, **kw):
        return order.step(weight_product, left, right, start, which, **kw)

    def by_rows(kernel, blocks, *args, **kw):
        return order.step(row_call, kernel, blocks, *args, **kw)

    def add(a, b, **kw):
        return order.step(add_low, a, b, **kw)

    def team_gather(own, *hold):
        across = team_swap(own, 2)
        if hold:
            across = pin(across, *hold)
        return [own, across, team_swap(own, 1), team_swap(across, 1)]

    def send_far(parts):
        return [team_swap(p, 1) for p in parts]

    def join_near(near, far, **kw):
        across = add(near[1], far[1], **kw)
        return [near[0], far[0], team_swap(across, 2), across]

    x_rows = pack(tokens)
    (a_own,) = by_rows(norm_kernel, [x_rows], [gain1, shift1], [BF])
    a_own = pin(a_own, block_o)
    a_across = team_swap(a_own, 2)
    w_o = flatten(both_halves(block_o))
    g_rows = pack(cotangent)
    a_across = pin(a_across, w_q[1], w_o[1], g_rows)
    a_all = [a_own, a_across, team_swap(a_own, 1), team_swap(a_across, 1)]
    block_up = [stored(depth_gather(columns(up_deal, i, 2))) for i in range(2)]
    g_all = team_gather(pin(g_rows, a_all[1]))

    wide = TEAM * rows
    q = forward(a_all, [w_q], bias_q)[0]
    k = forward(a_all, [w_k], zero_bias)[0]
    w_v = both_halves(block_v, q)
    v = forward(a_all, [w_v], bias_v)[0]
    q, k, v = [s.reshape(wide, part_width) for s in (q, k, v)]
    context = order.step(attend, q, k, v, hold=[g_all[1]]).reshape(TEAM, rows, part_width)
    if outer == 2:
        down_pair = jnp.stack([down_weight, outer_pass(pin(down_weight, k))])[None]
        w_down = [[depth_gather(pin(down_pair, context))]]
    else:
        w_down = [[lax.all_gather(down_weight, SPREAD, axis=0, tiled=True)]]
    o_far = send_far(forward([context], [w_o], style="bare", pick=(1, 2)))
    o_near = forward([context], [w_o], style="bare", pick=(0, 2))
    w_up = [both_halves(block_up[0], context)]
    *o_parts, o_across = join_near(o_near, o_far)
    hidden, b_own = by_rows(
        functools.partial(join_norm_kernel, 4),
        [x_rows] + o_parts,
        [bias_o, gain2, shift2],
        [F32, BF],
        hold=[w_up[0][1]],
    )
    w_up.append(both_halves(block_up[1], b_own))
    b_all = team_gather(b_own, w_up[1][1])

    active, slope = forward(b_all, w_up, bias_up, style="gate")

    def depth_scatter(a):
        return lax.psum_scatter(a, "fsdp", scatter_dimension=0, tiled=True)

    def send_away(away, *hold):
        if outer != 2:
            return away
        return outer_pass(pin(away, *hold) if hold else away)

    def settle(sent, mine, **kw):
        c = mine.shape[-1]
        if outer == 2:
            total = add(sent, mine, **kw)
        else:
            both = jnp.concatenate([mine.reshape(outer // 2, -1, c), sent.reshape(outer // 2, -1, c)])
            total = outer_scatter(both, me)
        return depth_scatter(total.reshape(-1, c))

    spread = (outer // 2, depth, TEAM, r)

    def settle_whole(grad):
        return lax.psum_scatter(grad, SPREAD, scatter_dimension=0, tiled=True)

    grad_down = [settle_whole(weight_grad([active], g_all, None, cut=(0, 1, 2)))]
    d_inner, sum_inner = back(g_all, w_down, style="slope", slope=slope)
    n_far = send_far(back([d_inner], w_up, style="bare", pick=(1, 2)))
    n_near = back([d_inner], w_up, style="bare", pick=(0, 2))
    n_parts = join_near(n_near, n_far)[:3]
    up_sent = [
        send_away(weight_grad(b_all, [d_inner], 1, spread=spread, cut=(i, i + 1, 2))) for i in range(2)
    ]
    down_late = weight_grad([active], g_all, None, cut=(1, 2, 2))
    d_hidden, d_out, sums2 = by_rows(
        functools.partial(norm_back_kernel, 3), n_parts + [hidden, g_rows], [gain2], [F32, BF], sums=4
    )
    grad_down.append(settle_whole(pin(down_late, d_out)))
    y_far = send_far(forward([active], w_down, style="bare", pick=(1, 2), hold=[grad_down[0]]))
    y_near = forward([active], w_down, style="bare", pick=(0, 2))
    up_mine = [weight_grad(b_all, [d_inner], 0, spread=spread, cut=(i, i + 1, 2)) for i in range(2)]
    d_out_all = team_gather(d_out, up_sent[0], up_mine[1])

    (d_near,) = back(d_out_all[:2], [w_o])
    (d_far,) = back(d_out_all[2:], [w_o])
    grad_up = [settle(up_sent[0], up_mine[0])]
    *y_parts, y_across = join_near(y_near, y_far)
    q_far, sum_far = order.step(attend_back, q, k, v, d_far.reshape(2 * rows, -1), 2 * rows // SLOT)
    q_far = q_far.reshape(2, rows, -1)
    a_far = send_far(back([q_far], [w_q, w_k, w_v], style="bare"))
    grad_up.append(settle(up_sent[1], up_mine[1]))
    o_sent = send_away(weight_grad([context], d_out_all, 1))
    o_mine = weight_grad([context], d_out_all, 0)
    q_near, sum_near = order.step(attend_back, q, k, v, d_near.reshape(2 * rows, -1), 0, hold=[grad_down[1]])
    q_near = q_near.reshape(2, rows, -1)
    grad_o = settle(o_sent, o_mine)
    a_near = back([q_near], [w_q, w_k, w_v], style="bare")
    a_parts = join_near(a_near, a_far, hold=[y_parts[2], grad_up[0]])[:3]
    parts = ((0, 1, 3), (1, 3, 3))
    d_both = [q_near, q_far]
    qkv_sent = [
        send_away(weight_grad(a_all, d_both, 1, spread=spread, cut=parts[0])),
        send_away(weight_grad(a_all, d_both, 1, spread=spread, cut=parts[1], hold=[grad_up[1]])),
    ]
    grad_q = settle(qkv_sent[0], weight_grad(a_all, d_both, 0, spread=spread, cut=parts[0]))
    kv_mine = weight_grad(a_all, d_both, 0, spread=spread, cut=parts[1], hold=[grad_o])
    (y_rows,) = by_rows(functools.partial(join_kernel, 4), [hidden] + y_parts, [bias_down], [BF])
    layer_out = unpack(y_rows, tokens)
    _, d_input, sums1 = by_rows(
        functools.partial(norm_back_kernel, 3),
        a_parts + [x_rows, d_hidden],
        [gain1],
        [BF, BF],
        sums=4,
        hold=[layer_out],
    )
    grad_kv = settle(qkv_sent[1], kv_mine)
    sum_qkv = sum_far + sum_near
    grad_o = grad_o.astype(F32)
    input_grad = unpack(d_input, cotangent)
    grad_down = jnp.concatenate([g.astype(F32) for g in grad_down], axis=1)
    (grad_up,) = return_columns(jnp.concatenate(grad_up, axis=1), member, outer, depth, 1)
    (grad_q,) = return_columns(grad_q, member, outer, depth, 1)
    grad_k, grad_v = return_columns(grad_kv, member, outer, depth, 2)

    whole_sums = [sums1[0], sums1[1], sums2[2], sums2[0], sums2[1], sums2[3]]
    part_sums = [sum_qkv[0, :part_width], sum_qkv[0, 2 * part_width :], sum_inner[0]]
    is_mine = (jnp.arange(TEAM) == member)[None, :, None, None]

    def widen(s):
        blocks = s.reshape(outer, 1, depth, -1)
        return jnp.where(is_mine, blocks, 0.0).reshape(devices, -1)

    table = jnp.concatenate([s.reshape(devices, -1) for s in whole_sums] + [widen(s) for s in part_sums], axis=1)
    small = reduce_small(table, member, me, layer)
    cuts = [small[edges[i] : edges[i + 1]] for i in range(len(vectors))]
    g_gain1, g_shift1, g_bias_o, g_gain2, g_shift2, g_bias_down, g_bias_q, g_bias_v, g_bias_up = cuts
    return (
        layer_out,
        input_grad,
        g_gain1,
        g_shift1,
        grad_q,
        g_bias_q,
        grad_k,
        grad_v,
        g_bias_v,
        grad_o,
        g_bias_o,
        g_gain2,
        g_shift2,
        grad_up,
        g_bias_up,
        grad_down,
        g_bias_down,
    )


def solution(mesh):
    outer = mesh.shape["dp"] // TEAM
    devices = mesh.devices.reshape(outer, TEAM, mesh.shape["fsdp"])
    fine = Mesh(devices, ALL)
    kinds = {"t": P(ALL, None, None), "w": P(ALL, None), "v": P(ALL)}
    vectors = "vvwvwwvwvvvwvwv"
    in_specs = tuple(kinds[c] for c in "ttww" + vectors)
    out_specs = tuple(kinds[c] for c in "tt" + vectors)
    return jax.shard_map(body, mesh=fine, in_specs=in_specs, out_specs=out_specs, check_vma=False)
```

```python
import functools

import jax
import jax.numpy as jnp
from jax import lax
from jax.experimental import pallas as pl
from jax.experimental.pallas import tpu as pltpu
from jax.sharding import Mesh
from jax.sharding import PartitionSpec as P

HD = 64
SLOT = 128
TEAM = 4
TILE = 256
HASTE = 1000
VMEM = 48 * 2**20

EPSILON = 1e-05
MASKED = -1e30
ROOT_HALF = 0.7071067811865476
DENSITY_SCALE = 0.3989422804014327
BF = jnp.bfloat16
F32 = jnp.float32
ALL = ("outer", "team", "fsdp")
SPREAD = ("outer", "fsdp")


def dot(a, b, ca, cb):
    return lax.dot_general(a, b, (((ca,), (cb,)), ((), ())), preferred_element_type=F32)


def team_swap(a, flip):
    return lax.ppermute(a, "team", [(i, i ^ flip) for i in range(TEAM)])


def ring_order(size):
    return list(range(0, size, 2)) + list(range(1, size, 2))[::-1]


def outer_pass(a):
    outer = lax.axis_size("outer")
    order = ring_order(outer)
    return lax.ppermute(a, "outer", [(o, order[(p + 1) % outer]) for p, o in enumerate(order)])


def outer_place(me):
    outer = lax.axis_size("outer")
    order = ring_order(outer)
    place = [0] * outer
    for p, o in enumerate(order):
        place[o] = p
    return jnp.asarray(order, jnp.int32), jnp.asarray(place, jnp.int32)[me]


def outer_halves(a, me):
    outer = lax.axis_size("outer")
    if outer == 2:
        return [a, outer_pass(a)]
    order, place = outer_place(me)
    whole = jnp.zeros((outer,) + a.shape[1:], a.dtype)
    whole = lax.dynamic_update_slice_in_dim(whole, a, me, 0)
    moving = a
    for step in range(1, outer):
        moving = outer_pass(moving)
        whole = lax.dynamic_update_slice_in_dim(whole, moving, order[(place - step) % outer], 0)
    return [whole[: outer // 2], whole[outer // 2 :]]


def outer_scatter(blocks, me):
    outer = lax.axis_size("outer")
    order, place = outer_place(me)
    moving = lax.dynamic_slice_in_dim(blocks, order[(place - 1) % outer], 1, 0)
    for step in range(1, outer):
        moving = outer_pass(moving)
        mine = lax.dynamic_slice_in_dim(blocks, order[(place - 1 - step) % outer], 1, 0)
        moving = (moving.astype(F32) + mine.astype(F32)).astype(BF)
    return moving


def by_team(stacked, member):
    odd = (member & 1) == 1
    high = (member & 2) == 2
    a = [jnp.where(odd, stacked[i ^ 1], stacked[i]) for i in range(4)]
    return [jnp.where(high, a[i ^ 2], a[i]) for i in range(4)]


def deal_columns(shards, member, outer, depth):
    r = shards[0].shape[0]
    parts = [w.reshape(r, outer, TEAM, depth, -1) for w in shards]
    got = []
    for flip in range(TEAM):
        piece = jnp.concatenate(
            [lax.dynamic_index_in_dim(w, member ^ flip, 2, False).reshape(r, -1) for w in parts], axis=1
        )
        got.append(piece if flip == 0 else team_swap(piece, flip))
    return jnp.concatenate(by_team(got, member), axis=0)


def return_columns(block, member, outer, depth, shares):
    r, c = block.shape[0] // TEAM, block.shape[1] // shares
    parts = block.reshape(TEAM, r, shares * c)
    got = []
    for flip in range(TEAM):
        piece = lax.dynamic_index_in_dim(parts, member ^ flip, 0, False)
        got.append(piece if flip == 0 else team_swap(piece, flip))
    got = by_team(got, member)
    result = []
    for i in range(shares):
        cols = jnp.stack([g[:, i * c : (i + 1) * c].reshape(r, outer, depth, -1) for g in got], axis=2)
        result.append(cols.reshape(r, -1).astype(F32))
    return result


def shift_pass(a, axis, step):
    size = lax.axis_size(axis)
    return lax.ppermute(a, axis, [(i, (i + step) % size) for i in range(size)])


def gather_small(vector, member, me, layer):
    depth = lax.axis_size("fsdp")
    outer = lax.axis_size("outer")
    a = vector[None]
    a = jnp.concatenate([a if s == 0 else shift_pass(a, "fsdp", s) for s in range(depth)])
    a = jnp.concatenate([a if s == 0 else shift_pass(a, "outer", s) for s in range(outer)])
    a = jnp.concatenate([a if f == 0 else team_swap(a, f) for f in range(TEAM)])
    index = jnp.arange(TEAM * outer * depth, dtype=jnp.int32)
    flip, step, drop = index // (outer * depth), index // depth % outer, index % depth
    source = ((me - step) % outer * TEAM + (member ^ flip)) * depth + (layer - drop) % depth
    place = (index[:, None] == source[None, :]).astype(BF)
    return dot(place, a, 1, 0)


def reduce_small(table, member, me, layer):
    depth = lax.axis_size("fsdp")
    outer = lax.axis_size("outer")
    blocks = table.reshape(outer, TEAM, depth, -1)
    total = lax.dynamic_index_in_dim(blocks, member, 1, False)
    for flip in range(1, TEAM):
        total = total + team_swap(lax.dynamic_index_in_dim(blocks, member ^ flip, 1, False), flip)
    blocks = total
    total = lax.dynamic_index_in_dim(blocks, me, 0, False)
    for step in range(1, outer):
        total = total + shift_pass(
            lax.dynamic_index_in_dim(blocks, (me + step) % outer, 0, False), "outer", step
        )
    blocks = total
    total = lax.dynamic_index_in_dim(blocks, layer, 0, False)
    for step in range(1, depth):
        total = total + shift_pass(
            lax.dynamic_index_in_dim(blocks, (layer + step) % depth, 0, False), "fsdp", step
        )
    return total


def params():
    return pltpu.CompilerParams(vmem_limit_bytes=VMEM)


def cost(flops, nbytes, exps=0):
    return pl.CostEstimate(
        flops=flops // HASTE, bytes_accessed=nbytes // HASTE, transcendentals=exps // HASTE
    )


def kernel_call(kernel, prefetch, grid, specs, args, out_specs, out_shape, estimate, hold=()):
    count = len(prefetch) + len(args)

    def run(*refs):
        kernel(*refs[:count], *refs[count + len(hold) :])

    return pl.pallas_call(
        run,
        grid_spec=pltpu.PrefetchScalarGridSpec(
            num_scalar_prefetch=len(prefetch),
            grid=grid,
            in_specs=list(specs) + [pl.BlockSpec(memory_space=pl.ANY)] * len(hold),
            out_specs=out_specs,
        ),
        out_shape=out_shape,
        compiler_params=params(),
        cost_estimate=estimate,
    )(*prefetch, *args, *hold)


def pin(value, *hold):
    def run(*refs):
        del refs

    anywhere = pl.BlockSpec(memory_space=pl.ANY)
    return pl.pallas_call(
        run,
        in_specs=[anywhere] * (1 + len(hold)),
        out_specs=anywhere,
        out_shape=jax.ShapeDtypeStruct(value.shape, value.dtype),
        input_output_aliases={0: 0},
        compiler_params=params(),
        cost_estimate=cost(0, 0),
    )(value, *hold)


def still(shape, first=0):
    return pl.BlockSpec(shape, lambda *_: (first,) + (0,) * (len(shape) - 1))


def in_order(block):
    h, z, t, r, n = block.shape
    rows = [block[o, :, i].reshape(z * r, n) for o in range(h) for i in range(t)]
    return jnp.concatenate(rows, axis=0) if len(rows) > 1 else rows[0]


def half_of(start, which, size):
    at = start if which == 0 else 1 - start
    return pl.ds(pl.multiple_of(at * size, size), size)


def forward_kernel(style, count, spread, cuts, per_cut, start_ref, *refs):
    pieces, weights, rest = refs[:count], refs[count : count + 2 * cuts], refs[count + 2 * cuts :]
    start = start_ref[0]
    load = in_order if spread else (lambda b: b.reshape(-1, b.shape[-1]))
    firsts, seconds = load(weights[0][...]), load(weights[1][...])
    for i in range(1, cuts):
        late = pl.program_id(0) >= i * per_cut
        firsts = jnp.where(late, load(weights[2 * i][...]), firsts)
        seconds = jnp.where(late, load(weights[2 * i + 1][...]), seconds)
    size = firsts.shape[0]
    if style == "bare":
        outs = rest
    else:
        bias, outs = rest[0][...], rest[1:]
    at = 0
    for ref in pieces:
        views = [ref] if len(ref.shape) == 2 else [ref.at[i] for i in range(ref.shape[0])]
        for view in views:
            value = dot(view[:, half_of(start, 0, size)], firsts, 1, 0)
            value = value + dot(view[:, half_of(start, 1, size)], seconds, 1, 0)
            if style == "bare":
                outs[at][...] = value.astype(BF)
            elif style == "plain":
                outs[0][at] = (value + bias).astype(BF)
            else:
                value = value + bias
                phi = 0.5 + 0.5 * lax.erf(value * ROOT_HALF)
                outs[0][at] = (value * phi).astype(BF)
                outs[1][at] = (phi + value * DENSITY_SCALE * jnp.exp(-0.5 * value * value)).astype(BF)
            at += 1


def forward_product(pieces, weights, start, bias=None, style="plain", pick=None, rows=512, hold=()):
    whole = len(weights[0]) == 1
    sample = weights[0][0]
    spread = sample.ndim == 5
    paired = sample.ndim == 4
    cuts = len(weights)
    n = sample.shape[-1] * cuts
    tile = min(n // cuts, TILE)
    per_cut = n // cuts // tile
    stack = pieces[0].ndim == 3
    if stack:
        total = pick[1] if pick else pieces[0].shape[0]
        specs = [still((total,) + pieces[0].shape[1:], pick[0] if pick else 0)]
        k = pieces[0].shape[2]
    else:
        total, k = len(pieces), pieces[0].shape[1]
        specs = [still(p.shape) for p in pieces]
    lead = sample.shape[:-1]
    args = list(pieces)
    for i, pair in enumerate(weights):

        def at(j, s, i=i):
            return (0,) * len(lead) + (jnp.clip(j - i * per_cut, 0, per_cut - 1),)

        if paired:
            z, _, b, _ = sample.shape
            specs += [pl.BlockSpec((z, 1, b, tile), lambda j, s, h=h: (0, h, 0, j)) for h in range(2)]
            args += [pair[0], pair[0]]
        elif whole:
            specs += [pl.BlockSpec((lead[0] // 2, tile), lambda j, s, h=h: (h, j)) for h in range(2)]
            args += [pair[0], pair[0]]
        else:
            specs += [pl.BlockSpec(lead + (tile,), at)] * 2
            args += list(pair)
    if style != "bare":
        specs.append(pl.BlockSpec((1, tile), lambda j, s: (0, j)))
        args.append(bias.reshape(1, n))
    if style == "bare":
        out_specs = [pl.BlockSpec((rows, tile), lambda j, s: (0, j))] * total
        out_shape = [jax.ShapeDtypeStruct((rows, n), BF)] * total
    else:
        copies = 2 if style == "gate" else 1
        out_specs = [pl.BlockSpec((total, rows, tile), lambda j, s: (0, 0, j))] * copies
        out_shape = [jax.ShapeDtypeStruct((total, rows, n), BF)] * copies
    return kernel_call(
        functools.partial(forward_kernel, style, len(pieces), spread, cuts, per_cut),
        [start],
        (n // tile,),
        specs,
        args,
        out_specs,
        out_shape,
        cost(2 * total * rows * k * n, 2 * (total * rows * (k + n) + k * n)),
        hold,
    )


def back_kernel(style, count, shares, per_half, start_ref, *refs):
    pieces, weights, rest = refs[:count], refs[count : count + 2 * shares], refs[count + 2 * shares :]
    late = pl.program_id(0) >= per_half
    chosen = []
    for i in range(shares):
        w0, w1 = weights[2 * i][...], weights[2 * i + 1][...]
        if len(w0.shape) == 5:
            w0, w1 = in_order(w0), in_order(w1)
        elif len(w0.shape) == 4:
            w0, w1 = w0[0, 0], w1[0, 0]
        chosen.append(jnp.where(late, w1, w0))
    views = []
    for ref in pieces:
        views += [ref] if len(ref.shape) == 2 else [ref.at[i] for i in range(ref.shape[0])]
    width = chosen[0].shape[1]
    total = None
    for at, view in enumerate(views):
        value = dot(view[:, :width], chosen[0], 1, 1)
        for i in range(1, shares):
            value = value + dot(view[:, i * width : (i + 1) * width], chosen[i], 1, 1)
        if style == "slope":
            low = (value * rest[0][at].astype(F32)).astype(BF)
            rest[1][at] = low
            part = jnp.sum(low.astype(F32), axis=0, keepdims=True)
            total = part if total is None else total + part
        elif style == "plain":
            rest[0][at] = value.astype(BF)
        else:
            rest[at][...] = value.astype(BF)
    if style == "slope":
        rest[2][...] = total


def back_product(pieces, weights, start, style="plain", slope=None, pick=None, rows=512, hold=()):
    shares = len(weights)
    sample = weights[0][0]
    k = sample.shape[-1]
    half_rows = 1
    for d in sample.shape[:-1]:
        half_rows *= d
    whole = len(weights[0]) == 1
    if whole:
        half_rows //= 2
    n = 2 * half_rows
    tile = min(half_rows, TILE)
    per_half = half_rows // tile
    stack = pieces[0].ndim == 3
    if stack:
        total = pick[1] if pick else pieces[0].shape[0]
        specs = [still((total,) + pieces[0].shape[1:], pick[0] if pick else 0)]
    else:
        total = len(pieces)
        specs = [still(p.shape) for p in pieces]
    if sample.ndim == 4:
        tile = sample.shape[2]
        per_half = sample.shape[0]
        block = (1, 1, tile, k)
    elif sample.ndim == 5:
        h, z, t, r, _ = sample.shape
        group = max(1, tile // (z * r))
        tile = group * z * r
        per_half = half_rows // tile
        each = t // group
        block = (1, z, group, r, k)

        def at(j):
            return (j // each, 0, j % each, 0, 0)
    else:
        block = (tile, k)

        def at(j):
            return (j, 0)

    if sample.ndim == 4:
        first = pl.BlockSpec(block, lambda j, s: (jnp.minimum(j, per_half - 1), 0, 0, 0))
        second = pl.BlockSpec(block, lambda j, s: (jnp.maximum(j - per_half, 0), 1, 0, 0))
    else:
        first = pl.BlockSpec(block, lambda j, s: at(jnp.minimum(j, per_half - 1)))
        second = pl.BlockSpec(block, lambda j, s: at(jnp.maximum(j - per_half, 0) + (per_half if whole else 0)))
    args = list(pieces)
    for w in weights:
        specs += [first, second]
        args += [w[0], w[-1]]

    def column(j, s):
        return lax.rem(s[0] * per_half + j, 2 * per_half)

    stacked = pl.BlockSpec((total, rows, tile), lambda j, s: (0, 0, column(j, s)))
    stack_shape = jax.ShapeDtypeStruct((total, rows, n), BF)
    if style == "slope":
        specs.append(stacked)
        args.append(slope)
        out_specs = [stacked, pl.BlockSpec((1, tile), lambda j, s: (0, column(j, s)))]
        out_shape = [stack_shape, jax.ShapeDtypeStruct((1, n), F32)]
    elif style == "plain":
        out_specs, out_shape = [stacked], [stack_shape]
    else:
        out_specs = [pl.BlockSpec((rows, tile), lambda j, s: (0, column(j, s)))] * total
        out_shape = [jax.ShapeDtypeStruct((rows, n), BF)] * total
    return kernel_call(
        functools.partial(back_kernel, style, len(pieces), shares, per_half),
        [start],
        (2 * per_half,),
        specs,
        args,
        out_specs,
        out_shape,
        cost(2 * total * rows * k * n * shares, 2 * (total * rows * (k * shares + n) + k * n)),
        hold,
    )


def weight_kernel(left_count, right_count, start_ref, *refs):
    lefts, rights, out = refs[:left_count], refs[left_count : left_count + right_count], refs[-1]

    def views(group):
        found = []
        for ref in group:
            found += [ref] if len(ref.shape) == 2 else [ref.at[i] for i in range(ref.shape[0])]
        return found

    total = None
    for a, b in zip(views(lefts), views(rights)):
        part = dot(a[...], b[...], 0, 0)
        total = part if total is None else total + part
    low = total.astype(BF)
    if len(out.shape) == 2:
        out[...] = low
    else:
        h, z, t, r, n = out.shape
        for o in range(h):
            for i in range(t):
                base = (o * t + i) * z * r
                out[o, :, i] = low[base : base + z * r].reshape(z, r, n)


def weight_product(left, right, start, which, spread=None, cut=(0, 1, 1), tile=512, hold=()):
    def spec(group, width, index):
        found = []
        for a in group:
            if a.ndim == 2:
                found.append(pl.BlockSpec((a.shape[0], width), lambda j, s: (0, index(j, s))))
            else:
                found.append(pl.BlockSpec(a.shape[:2] + (width,), lambda j, s: (0, 0, index(j, s))))
        return found

    half = left[0].shape[-1] // (1 if which is None else 2)
    share = right[0].shape[-1] // cut[2]
    n = share * (cut[1] - cut[0])
    tile = min(tile, share)
    skip = cut[0] * (share // tile)
    rows = sum(a.shape[0] if a.ndim == 2 else a.shape[0] * a.shape[1] for a in left)
    specs = spec(left, half, lambda j, s: 0 if which is None else s[0] if which == 0 else 1 - s[0])
    specs += spec(right, tile, lambda j, s: j + skip)
    shape = (half, n) if spread is None else spread + (n,)
    block = shape[:-1] + (tile,)
    return kernel_call(
        functools.partial(weight_kernel, len(left), len(right)),
        [start],
        (n // tile,),
        specs,
        [*left, *right],
        pl.BlockSpec(block, lambda j, s: (0,) * (len(block) - 1) + (j,)),
        jax.ShapeDtypeStruct(shape, BF),
        cost(2 * rows * half * n, 2 * (rows * (half + n) + half * n)),
        hold,
    )


def pair_masks():
    lane = lax.broadcasted_iota(jnp.int32, (1, 2 * HD), 1)
    low = jnp.where(lane < HD, 1.0, 0.0).astype(BF)
    high = jnp.where(lane < HD, 0.0, 1.0).astype(BF)
    return low, high


def pair_probs(q_two, k):
    scores = dot(q_two, k, 1, 1) * 0.125
    row = lax.broadcasted_iota(jnp.int32, scores.shape, 0) & (SLOT - 1)
    column = lax.broadcasted_iota(jnp.int32, scores.shape, 1)
    scores = jnp.where(row >= column, scores, MASKED)
    exponent = jnp.exp(scores - jnp.max(scores, axis=-1, keepdims=True))
    return exponent / jnp.sum(exponent, axis=-1, keepdims=True)


def attend_kernel(q_ref, k_ref, v_ref, context_ref):
    low, high = pair_masks()
    for at in range(0, context_ref.shape[1], 2 * HD):
        q, k, v = [ref[:, at : at + 2 * HD] for ref in (q_ref, k_ref, v_ref)]
        probs = pair_probs(jnp.concatenate([q * low, q * high], axis=0), k).astype(BF)
        context = dot(probs[:SLOT], v * low, 1, 0) + dot(probs[SLOT:], v * high, 1, 0)
        context_ref[:, at : at + 2 * HD] = context.astype(BF)


def attend_back_kernel(q_ref, k_ref, v_ref, grad_ref, out_ref, sum_ref):
    part = grad_ref.shape[1]
    low, high = pair_masks()

    @pl.when(pl.program_id(0) == 0)
    def _():
        sum_ref[...] = jnp.zeros_like(sum_ref)

    for at in range(0, part, 2 * HD):
        q, k, v, grad = [ref[:, at : at + 2 * HD] for ref in (q_ref, k_ref, v_ref, grad_ref)]
        q_two = jnp.concatenate([q * low, q * high], axis=0)
        g_two = jnp.concatenate([grad * low, grad * high], axis=0)
        probs = pair_probs(q_two, k)
        d_probs = dot(g_two, v, 1, 1)
        row_dot = jnp.sum(probs * d_probs, axis=-1, keepdims=True)
        d_scores = (probs * (d_probs - row_dot)).astype(BF)
        d_q = dot(d_scores[:SLOT], k * low, 1, 0) + dot(d_scores[SLOT:], k * high, 1, 0)
        d_k = dot(d_scores, q_two, 0, 0)
        d_v = dot(probs.astype(BF), g_two, 0, 0)
        for i, value in enumerate((d_q * 0.125, d_k * 0.125, d_v)):
            where = slice(i * part + at, i * part + at + 2 * HD)
            value = value.astype(BF)
            out_ref[:, where] = value
            sum_ref[:, where] += jnp.sum(value.astype(F32), axis=0, keepdims=True)


def attend(q, k, v, hold=()):
    rows, part = q.shape
    one = pl.BlockSpec((SLOT, part), lambda i: (i, 0))
    return kernel_call(
        attend_kernel,
        [],
        (rows // SLOT,),
        [one] * 3,
        [q, k, v],
        one,
        jax.ShapeDtypeStruct((rows, part), BF),
        cost(32 * rows * SLOT * part, 8 * rows * part, rows * SLOT * part // HD),
        hold,
    )


def attend_back(q, k, v, grad, first, hold=()):
    rows, part = grad.shape
    one = pl.BlockSpec((SLOT, part), lambda i: (i, 0))
    shifted = pl.BlockSpec((SLOT, part), lambda i: (i + first, 0))
    return kernel_call(
        attend_back_kernel,
        [],
        (rows // SLOT,),
        [shifted] * 3 + [one],
        [q, k, v, grad],
        [pl.BlockSpec((SLOT, 3 * part), lambda i: (i, 0)), still((1, 3 * part))],
        [jax.ShapeDtypeStruct((rows, 3 * part), BF), jax.ShapeDtypeStruct((1, 3 * part), F32)],
        cost(80 * rows * SLOT * part, 14 * rows * part, rows * SLOT * part // HD),
        hold,
    )


def normal_of(values):
    centred = values - jnp.mean(values, axis=-1, keepdims=True)
    inverse = lax.rsqrt(jnp.mean(centred * centred, axis=-1, keepdims=True) + EPSILON)
    return centred * inverse, inverse


def rows_of(refs):
    total = refs[0][...].astype(F32)
    for ref in refs[1:]:
        total = total + ref[...].astype(F32)
    return total


def norm_kernel(x_ref, gain_ref, shift_ref, out_ref):
    normal, _ = normal_of(x_ref[...].astype(F32))
    out_ref[...] = (normal * gain_ref[...] + shift_ref[...]).astype(BF)


def join_norm_kernel(count, *refs):
    bias, gain, shift, hidden_ref, out_ref = refs[count:]
    hidden = rows_of(refs[:count]) + bias[...]
    hidden_ref[...] = hidden
    normal, _ = normal_of(hidden)
    out_ref[...] = (normal * gain[...] + shift[...]).astype(BF)


def join_kernel(count, *refs):
    refs[count + 1][...] = (rows_of(refs[:count]) + refs[count][...]).astype(BF)


def norm_back_kernel(count, *refs):
    source, carry, gain, grad_ref, low_ref, sums = refs[count:]
    grad = rows_of(refs[:count])
    normal, inverse = normal_of(source[...].astype(F32))
    scaled = grad * gain[...]
    centre = jnp.mean(scaled, axis=-1, keepdims=True)
    projected = jnp.mean(scaled * normal, axis=-1, keepdims=True)
    carried = carry[...].astype(F32)
    result = carried + inverse * (scaled - centre - normal * projected)
    grad_ref[...] = result.astype(grad_ref.dtype)
    low = result.astype(BF)
    low_ref[...] = low

    @pl.when(pl.program_id(0) == 0)
    def _():
        sums[...] = jnp.zeros_like(sums)

    for i, value in enumerate((grad * normal, grad, low.astype(F32), carried)):
        sums[i : i + 1] += jnp.sum(value, axis=0, keepdims=True)


def add_kernel(a_ref, b_ref, out_ref):
    out_ref[...] = (a_ref[...].astype(F32) + b_ref[...].astype(F32)).astype(BF)


def add_low(a, b, hold=()):
    width = a.shape[-1]
    flat = [x.reshape(-1, width) for x in (a, b)]
    rows = flat[0].shape[0]
    step = min(rows, 256)
    one = pl.BlockSpec((step, width), lambda i: (i, 0))
    result = kernel_call(
        add_kernel,
        [],
        (rows // step,),
        [one, one],
        flat,
        one,
        jax.ShapeDtypeStruct((rows, width), BF),
        cost(rows * width, 6 * rows * width),
        hold,
    )
    return result.reshape(a.shape)


def row_call(kernel, blocks, vectors, outs, sums=0, step=128, hold=()):
    rows, width = blocks[0].shape
    one = pl.BlockSpec((step, width), lambda i: (i, 0))
    out_specs = [one] * len(outs)
    out_shape = [jax.ShapeDtypeStruct((rows, width), d) for d in outs]
    if sums:
        out_specs.append(still((sums, width)))
        out_shape.append(jax.ShapeDtypeStruct((sums, width), F32))
    return kernel_call(
        kernel,
        [],
        (rows // step,),
        [one] * len(blocks) + [still((1, width))] * len(vectors),
        [*blocks, *[v.reshape(1, width) for v in vectors]],
        out_specs,
        out_shape,
        cost(20 * rows * width, 16 * rows * width),
        hold,
    )


def body(
    tokens,
    cotangent,
    doc_starts,
    active_len,
    ln1_gain,
    ln1_bias,
    q_weight,
    q_bias,
    k_weight,
    v_weight,
    v_bias,
    o_weight,
    o_bias,
    ln2_gain,
    ln2_bias,
    up_weight,
    up_bias,
    down_weight,
    down_bias,
):
    depth = lax.axis_size("fsdp")
    outer = lax.axis_size("outer")
    devices = outer * TEAM * depth
    member, me = lax.axis_index("team"), lax.axis_index("outer")
    layer = lax.axis_index("fsdp")
    start = (me if outer == 2 else jnp.zeros_like(me)).reshape(1)
    groups, row_len, width = tokens.shape
    docs = doc_starts.shape[1]
    r = q_weight.shape[0]
    part_width = width // TEAM
    rows = groups * docs * SLOT

    zero_bias = jnp.zeros((part_width,), F32)

    def depth_gather(a):
        return lax.all_gather(a, "fsdp", axis=0, tiled=True)

    def columns(a, i, n):
        c = a.shape[1] // n
        return a[:, i * c : (i + 1) * c]

    def stored(block):
        return block.reshape(1, depth, TEAM, r, block.shape[1])

    def flat(block):
        return block[None]

    def both_halves(block, *hold):
        return outer_halves(pin(block, *hold) if hold else block, me)

    def flatten(halves):
        return [h.reshape(-1, h.shape[-1]) for h in halves]

    deal = deal_columns((q_weight, k_weight, v_weight, up_weight), member, outer, depth)
    qkv_deal, up_deal = deal[:, : 3 * part_width], deal[:, 3 * part_width :]
    block_q, block_k, block_v = [stored(depth_gather(columns(qkv_deal, i, 3))) for i in range(3)]
    w_q, w_k = [both_halves(b) for b in (block_q, block_k)]
    block_o = flat(depth_gather(o_weight))

    vectors = (ln1_gain, ln1_bias, o_bias, ln2_gain, ln2_bias, down_bias, q_bias, v_bias, up_bias)
    packed = gather_small(jnp.concatenate(vectors), member, me, layer)
    edges = [0]
    for v in vectors:
        edges.append(edges[-1] + v.shape[0])
    pieces = [packed[:, edges[i] : edges[i + 1]] for i in range(len(vectors))]
    gain1, shift1, bias_o, gain2, shift2, bias_down = [p.reshape(-1) for p in pieces[:6]]

    def member_part(p):
        whole = p.reshape(outer, TEAM, depth, -1)
        return lax.dynamic_index_in_dim(whole, member, 1, False).reshape(-1)

    bias_q, bias_v, bias_up = [member_part(p) for p in pieces[6:]]

    position = jnp.arange(row_len, dtype=jnp.int32)
    offset = jnp.arange(SLOT, dtype=jnp.int32)
    wanted = doc_starts[:, :, None] + offset
    live = offset < active_len[:, :, None]
    chosen = (wanted[..., None] == position) & live[..., None]
    chosen = chosen.reshape(groups, docs * SLOT, row_len)
    select = chosen.astype(BF)
    covered = jnp.any(chosen, axis=1)

    def pack(source):
        picked = jnp.einsum("gst,gtd->gsd", select, source, preferred_element_type=F32)
        return picked.reshape(rows, width).astype(BF)

    def unpack(slot_rows, fallback):
        blocks = slot_rows.reshape(groups, docs * SLOT, width)
        placed = jnp.einsum("gst,gsd->gtd", select, blocks, preferred_element_type=F32).astype(BF)
        return jnp.where(covered[..., None], placed, fallback)

    class Order:
        last = ()

        def step(self, kernel, *args, hold=(), **kw):
            result = kernel(*args, hold=self.last + tuple(hold), **kw)
            self.last = (jax.tree.leaves(result)[-1],)
            return result

    order = Order()

    def begin(weights):
        return jnp.zeros_like(start) if len(weights[0]) == 1 and outer != 2 else start

    def forward(pieces, weights, *rest, **kw):
        return order.step(forward_product, pieces, weights, begin(weights), *rest, rows=rows, **kw)

    def back(pieces, weights, **kw):
        return order.step(back_product, pieces, weights, begin(weights), rows=rows, **kw)

    def weight_grad(left, right, which, **kw):
        return order.step(weight_product, left, right, start, which, **kw)

    def by_rows(kernel, blocks, *args, **kw):
        return order.step(row_call, kernel, blocks, *args, **kw)

    def add(a, b, **kw):
        return order.step(add_low, a, b, **kw)

    def team_gather(own, *hold):
        across = team_swap(own, 2)
        if hold:
            across = pin(across, *hold)
        return [own, across, team_swap(own, 1), team_swap(across, 1)]

    def send_far(parts):
        return [team_swap(p, 1) for p in parts]

    def join_near(near, far, **kw):
        across = add(near[1], far[1], **kw)
        return [near[0], far[0], team_swap(across, 2), across]

    x_rows = pack(tokens)
    (a_own,) = by_rows(norm_kernel, [x_rows], [gain1, shift1], [BF])
    a_own = pin(a_own, block_o)
    a_across = team_swap(a_own, 2)
    w_o = flatten(both_halves(block_o))
    g_rows = pack(cotangent)
    a_across = pin(a_across, w_q[1], w_o[1], g_rows)
    a_all = [a_own, a_across, team_swap(a_own, 1), team_swap(a_across, 1)]
    block_up = [stored(depth_gather(columns(up_deal, i, 2))) for i in range(2)]
    g_all = team_gather(pin(g_rows, a_all[1]))

    wide = TEAM * rows
    q = forward(a_all, [w_q], bias_q)[0]
    k = forward(a_all, [w_k], zero_bias)[0]
    w_v = both_halves(block_v, q)
    v = forward(a_all, [w_v], bias_v)[0]
    q, k, v = [s.reshape(wide, part_width) for s in (q, k, v)]
    context = order.step(attend, q, k, v, hold=[g_all[1]]).reshape(TEAM, rows, part_width)
    if outer == 2:
        down_pair = jnp.stack([down_weight, outer_pass(pin(down_weight, k))])[None]
        w_down = [[depth_gather(pin(down_pair, context))]]
    else:
        w_down = [[lax.all_gather(down_weight, SPREAD, axis=0, tiled=True)]]
    o_far = send_far(forward([context], [w_o], style="bare", pick=(1, 2)))
    o_near = forward([context], [w_o], style="bare", pick=(0, 2))
    w_up = [both_halves(block_up[0], context)]
    *o_parts, o_across = join_near(o_near, o_far)
    hidden, b_own = by_rows(
        functools.partial(join_norm_kernel, 4),
        [x_rows] + o_parts,
        [bias_o, gain2, shift2],
        [F32, BF],
        hold=[w_up[0][1]],
    )
    w_up.append(both_halves(block_up[1], b_own))
    b_all = team_gather(b_own, w_up[1][1])

    active, slope = forward(b_all, w_up, bias_up, style="gate")

    def depth_scatter(a):
        return lax.psum_scatter(a, "fsdp", scatter_dimension=0, tiled=True)

    def send_away(away, *hold):
        if outer != 2:
            return away
        return outer_pass(pin(away, *hold) if hold else away)

    def settle(sent, mine, **kw):
        c = mine.shape[-1]
        if outer == 2:
            total = add(sent, mine, **kw)
        else:
            both = jnp.concatenate([mine.reshape(outer // 2, -1, c), sent.reshape(outer // 2, -1, c)])
            total = outer_scatter(both, me)
        return depth_scatter(total.reshape(-1, c))

    spread = (outer // 2, depth, TEAM, r)

    def settle_whole(grad):
        return lax.psum_scatter(grad, SPREAD, scatter_dimension=0, tiled=True)

    grad_down = [settle_whole(weight_grad([active], g_all, None, cut=(0, 1, 2)))]
    grad_down.append(settle_whole(weight_grad([active], g_all, None, cut=(1, 2, 2))))
    d_inner, sum_inner = back(g_all, w_down, style="slope", slope=slope)
    n_far = send_far(back([d_inner], w_up, style="bare", pick=(1, 2)))
    n_near = back([d_inner], w_up, style="bare", pick=(0, 2))
    n_parts = join_near(n_near, n_far)[:3]
    up_sent = [
        send_away(weight_grad(b_all, [d_inner], 1, spread=spread, cut=(i, i + 1, 2))) for i in range(2)
    ]
    up_mine = [weight_grad(b_all, [d_inner], 0, spread=spread, cut=(i, i + 1, 2)) for i in range(2)]
    d_hidden, d_out, sums2 = by_rows(
        functools.partial(norm_back_kernel, 3), n_parts + [hidden, g_rows], [gain2], [F32, BF], sums=4
    )
    y_far = send_far(forward([active], w_down, style="bare", pick=(1, 2), hold=[grad_down[0]]))
    y_near = forward([active], w_down, style="bare", pick=(0, 2))
    d_out_all = team_gather(d_out, up_sent[0], y_near[1])

    (d_near,) = back(d_out_all[:2], [w_o])
    (d_far,) = back(d_out_all[2:], [w_o])
    grad_up = [settle(up_sent[0], up_mine[0], hold=[grad_down[1]])]
    *y_parts, y_across = join_near(y_near, y_far)
    q_far, sum_far = order.step(attend_back, q, k, v, d_far.reshape(2 * rows, -1), 2 * rows // SLOT)
    q_far = q_far.reshape(2, rows, -1)
    a_far = send_far(back([q_far], [w_q, w_k, w_v], style="bare"))
    grad_up.append(settle(up_sent[1], up_mine[1]))
    o_sent = send_away(weight_grad([context], d_out_all, 1))
    o_mine = weight_grad([context], d_out_all, 0)
    q_near, sum_near = order.step(attend_back, q, k, v, d_near.reshape(2 * rows, -1), 0, hold=[grad_up[0]])
    q_near = q_near.reshape(2, rows, -1)
    grad_o = settle(o_sent, o_mine)
    a_near = back([q_near], [w_q, w_k, w_v], style="bare")
    a_parts = join_near(a_near, a_far, hold=[y_parts[2]])[:3]
    parts = ((0, 1, 3), (1, 3, 3))
    d_both = [q_near, q_far]
    qkv_sent = [
        send_away(weight_grad(a_all, d_both, 1, spread=spread, cut=parts[0], hold=[grad_up[1]])),
        send_away(weight_grad(a_all, d_both, 1, spread=spread, cut=parts[1], hold=[grad_o])),
    ]
    grad_q = settle(qkv_sent[0], weight_grad(a_all, d_both, 0, spread=spread, cut=parts[0]))
    kv_mine = weight_grad(a_all, d_both, 0, spread=spread, cut=parts[1])
    (y_rows,) = by_rows(functools.partial(join_kernel, 4), [hidden] + y_parts, [bias_down], [BF])
    layer_out = unpack(y_rows, tokens)
    _, d_input, sums1 = by_rows(
        functools.partial(norm_back_kernel, 3),
        a_parts + [x_rows, d_hidden],
        [gain1],
        [BF, BF],
        sums=4,
        hold=[layer_out],
    )
    grad_kv = settle(qkv_sent[1], kv_mine)
    sum_qkv = sum_far + sum_near
    grad_o = grad_o.astype(F32)
    input_grad = unpack(d_input, cotangent)
    grad_down = jnp.concatenate([g.astype(F32) for g in grad_down], axis=1)
    (grad_up,) = return_columns(jnp.concatenate(grad_up, axis=1), member, outer, depth, 1)
    (grad_q,) = return_columns(grad_q, member, outer, depth, 1)
    grad_k, grad_v = return_columns(grad_kv, member, outer, depth, 2)

    whole_sums = [sums1[0], sums1[1], sums2[2], sums2[0], sums2[1], sums2[3]]
    part_sums = [sum_qkv[0, :part_width], sum_qkv[0, 2 * part_width :], sum_inner[0]]
    is_mine = (jnp.arange(TEAM) == member)[None, :, None, None]

    def widen(s):
        blocks = s.reshape(outer, 1, depth, -1)
        return jnp.where(is_mine, blocks, 0.0).reshape(devices, -1)

    table = jnp.concatenate([s.reshape(devices, -1) for s in whole_sums] + [widen(s) for s in part_sums], axis=1)
    small = reduce_small(table, member, me, layer)
    cuts = [small[edges[i] : edges[i + 1]] for i in range(len(vectors))]
    g_gain1, g_shift1, g_bias_o, g_gain2, g_shift2, g_bias_down, g_bias_q, g_bias_v, g_bias_up = cuts
    return (
        layer_out,
        input_grad,
        g_gain1,
        g_shift1,
        grad_q,
        g_bias_q,
        grad_k,
        grad_v,
        g_bias_v,
        grad_o,
        g_bias_o,
        g_gain2,
        g_shift2,
        grad_up,
        g_bias_up,
        grad_down,
        g_bias_down,
    )


def solution(mesh):
    outer = mesh.shape["dp"] // TEAM
    devices = mesh.devices.reshape(outer, TEAM, mesh.shape["fsdp"])
    fine = Mesh(devices, ALL)
    kinds = {"t": P(ALL, None, None), "w": P(ALL, None), "v": P(ALL)}
    vectors = "vvwvwwvwvvvwvwv"
    in_specs = tuple(kinds[c] for c in "ttww" + vectors)
    out_specs = tuple(kinds[c] for c in "tt" + vectors)
    return jax.shard_map(body, mesh=fine, in_specs=in_specs, out_specs=out_specs, check_vma=False)
```

```python
import functools

import jax
import jax.numpy as jnp
from jax import lax
from jax.experimental import pallas as pl
from jax.experimental.pallas import tpu as pltpu
from jax.sharding import Mesh
from jax.sharding import PartitionSpec as P

HD = 64
SLOT = 128
TEAM = 4
TILE = 256
HASTE = 1000
VMEM = 48 * 2**20

EPSILON = 1e-05
MASKED = -1e30
ROOT_HALF = 0.7071067811865476
DENSITY_SCALE = 0.3989422804014327
BF = jnp.bfloat16
F32 = jnp.float32
ALL = ("outer", "team", "fsdp")
SPREAD = ("outer", "fsdp")


def dot(a, b, ca, cb):
    return lax.dot_general(a, b, (((ca,), (cb,)), ((), ())), preferred_element_type=F32)


def team_swap(a, flip):
    return lax.ppermute(a, "team", [(i, i ^ flip) for i in range(TEAM)])


def ring_order(size):
    return list(range(0, size, 2)) + list(range(1, size, 2))[::-1]


def outer_pass(a):
    outer = lax.axis_size("outer")
    order = ring_order(outer)
    return lax.ppermute(a, "outer", [(o, order[(p + 1) % outer]) for p, o in enumerate(order)])


def outer_place(me):
    outer = lax.axis_size("outer")
    order = ring_order(outer)
    place = [0] * outer
    for p, o in enumerate(order):
        place[o] = p
    return jnp.asarray(order, jnp.int32), jnp.asarray(place, jnp.int32)[me]


def outer_halves(a, me):
    outer = lax.axis_size("outer")
    if outer == 2:
        return [a, outer_pass(a)]
    order, place = outer_place(me)
    whole = jnp.zeros((outer,) + a.shape[1:], a.dtype)
    whole = lax.dynamic_update_slice_in_dim(whole, a, me, 0)
    moving = a
    for step in range(1, outer):
        moving = outer_pass(moving)
        whole = lax.dynamic_update_slice_in_dim(whole, moving, order[(place - step) % outer], 0)
    return [whole[: outer // 2], whole[outer // 2 :]]


def outer_scatter(blocks, me):
    outer = lax.axis_size("outer")
    order, place = outer_place(me)
    moving = lax.dynamic_slice_in_dim(blocks, order[(place - 1) % outer], 1, 0)
    for step in range(1, outer):
        moving = outer_pass(moving)
        mine = lax.dynamic_slice_in_dim(blocks, order[(place - 1 - step) % outer], 1, 0)
        moving = (moving.astype(F32) + mine.astype(F32)).astype(BF)
    return moving


def by_team(stacked, member):
    odd = (member & 1) == 1
    high = (member & 2) == 2
    a = [jnp.where(odd, stacked[i ^ 1], stacked[i]) for i in range(4)]
    return [jnp.where(high, a[i ^ 2], a[i]) for i in range(4)]


def deal_columns(shards, member, outer, depth):
    r = shards[0].shape[0]
    parts = [w.reshape(r, outer, TEAM, depth, -1) for w in shards]
    got = []
    for flip in range(TEAM):
        piece = jnp.concatenate(
            [lax.dynamic_index_in_dim(w, member ^ flip, 2, False).reshape(r, -1) for w in parts], axis=1
        )
        got.append(piece if flip == 0 else team_swap(piece, flip))
    return jnp.concatenate(by_team(got, member), axis=0)


def return_columns(block, member, outer, depth, shares):
    r, c = block.shape[0] // TEAM, block.shape[1] // shares
    parts = block.reshape(TEAM, r, shares * c)
    got = []
    for flip in range(TEAM):
        piece = lax.dynamic_index_in_dim(parts, member ^ flip, 0, False)
        got.append(piece if flip == 0 else team_swap(piece, flip))
    got = by_team(got, member)
    result = []
    for i in range(shares):
        cols = jnp.stack([g[:, i * c : (i + 1) * c].reshape(r, outer, depth, -1) for g in got], axis=2)
        result.append(cols.reshape(r, -1).astype(F32))
    return result


def shift_pass(a, axis, step):
    size = lax.axis_size(axis)
    return lax.ppermute(a, axis, [(i, (i + step) % size) for i in range(size)])


def gather_small(vector, member, me, layer):
    depth = lax.axis_size("fsdp")
    outer = lax.axis_size("outer")
    a = vector[None]
    a = jnp.concatenate([a if s == 0 else shift_pass(a, "fsdp", s) for s in range(depth)])
    a = jnp.concatenate([a if s == 0 else shift_pass(a, "outer", s) for s in range(outer)])
    a = jnp.concatenate([a if f == 0 else team_swap(a, f) for f in range(TEAM)])
    index = jnp.arange(TEAM * outer * depth, dtype=jnp.int32)
    flip, step, drop = index // (outer * depth), index // depth % outer, index % depth
    source = ((me - step) % outer * TEAM + (member ^ flip)) * depth + (layer - drop) % depth
    place = (index[:, None] == source[None, :]).astype(BF)
    return dot(place, a, 1, 0)


def reduce_small(table, member, me, layer):
    depth = lax.axis_size("fsdp")
    outer = lax.axis_size("outer")
    blocks = table.reshape(outer, TEAM, depth, -1)
    total = lax.dynamic_index_in_dim(blocks, member, 1, False)
    for flip in range(1, TEAM):
        total = total + team_swap(lax.dynamic_index_in_dim(blocks, member ^ flip, 1, False), flip)
    blocks = total
    total = lax.dynamic_index_in_dim(blocks, me, 0, False)
    for step in range(1, outer):
        total = total + shift_pass(
            lax.dynamic_index_in_dim(blocks, (me + step) % outer, 0, False), "outer", step
        )
    blocks = total
    total = lax.dynamic_index_in_dim(blocks, layer, 0, False)
    for step in range(1, depth):
        total = total + shift_pass(
            lax.dynamic_index_in_dim(blocks, (layer + step) % depth, 0, False), "fsdp", step
        )
    return total


def params():
    return pltpu.CompilerParams(vmem_limit_bytes=VMEM)


def cost(flops, nbytes, exps=0):
    return pl.CostEstimate(
        flops=flops // HASTE, bytes_accessed=nbytes // HASTE, transcendentals=exps // HASTE
    )


def kernel_call(kernel, prefetch, grid, specs, args, out_specs, out_shape, estimate, hold=()):
    count = len(prefetch) + len(args)

    def run(*refs):
        kernel(*refs[:count], *refs[count + len(hold) :])

    return pl.pallas_call(
        run,
        grid_spec=pltpu.PrefetchScalarGridSpec(
            num_scalar_prefetch=len(prefetch),
            grid=grid,
            in_specs=list(specs) + [pl.BlockSpec(memory_space=pl.ANY)] * len(hold),
            out_specs=out_specs,
        ),
        out_shape=out_shape,
        compiler_params=params(),
        cost_estimate=estimate,
    )(*prefetch, *args, *hold)


def pin(value, *hold):
    def run(*refs):
        del refs

    anywhere = pl.BlockSpec(memory_space=pl.ANY)
    return pl.pallas_call(
        run,
        in_specs=[anywhere] * (1 + len(hold)),
        out_specs=anywhere,
        out_shape=jax.ShapeDtypeStruct(value.shape, value.dtype),
        input_output_aliases={0: 0},
        compiler_params=params(),
        cost_estimate=cost(0, 0),
    )(value, *hold)


def still(shape, first=0):
    return pl.BlockSpec(shape, lambda *_: (first,) + (0,) * (len(shape) - 1))


def in_order(block):
    h, z, t, r, n = block.shape
    rows = [block[o, :, i].reshape(z * r, n) for o in range(h) for i in range(t)]
    return jnp.concatenate(rows, axis=0) if len(rows) > 1 else rows[0]


def half_of(start, which, size):
    at = start if which == 0 else 1 - start
    return pl.ds(pl.multiple_of(at * size, size), size)


def forward_kernel(style, count, spread, cuts, per_cut, start_ref, *refs):
    pieces, weights, rest = refs[:count], refs[count : count + 2 * cuts], refs[count + 2 * cuts :]
    start = start_ref[0]
    load = in_order if spread else (lambda b: b.reshape(-1, b.shape[-1]))
    firsts, seconds = load(weights[0][...]), load(weights[1][...])
    for i in range(1, cuts):
        late = pl.program_id(0) >= i * per_cut
        firsts = jnp.where(late, load(weights[2 * i][...]), firsts)
        seconds = jnp.where(late, load(weights[2 * i + 1][...]), seconds)
    size = firsts.shape[0]
    if style == "bare":
        outs = rest
    else:
        bias, outs = rest[0][...], rest[1:]
    at = 0
    for ref in pieces:
        views = [ref] if len(ref.shape) == 2 else [ref.at[i] for i in range(ref.shape[0])]
        for view in views:
            value = dot(view[:, half_of(start, 0, size)], firsts, 1, 0)
            value = value + dot(view[:, half_of(start, 1, size)], seconds, 1, 0)
            if style == "bare":
                outs[at][...] = value.astype(BF)
            elif style == "plain":
                outs[0][at] = (value + bias).astype(BF)
            else:
                value = value + bias
                phi = 0.5 + 0.5 * lax.erf(value * ROOT_HALF)
                outs[0][at] = (value * phi).astype(BF)
                outs[1][at] = (phi + value * DENSITY_SCALE * jnp.exp(-0.5 * value * value)).astype(BF)
            at += 1


def forward_product(pieces, weights, start, bias=None, style="plain", pick=None, rows=512, hold=()):
    whole = len(weights[0]) == 1
    sample = weights[0][0]
    spread = sample.ndim == 5
    paired = sample.ndim == 4
    cuts = len(weights)
    n = sample.shape[-1] * cuts
    tile = min(n // cuts, TILE)
    per_cut = n // cuts // tile
    stack = pieces[0].ndim == 3
    if stack:
        total = pick[1] if pick else pieces[0].shape[0]
        specs = [still((total,) + pieces[0].shape[1:], pick[0] if pick else 0)]
        k = pieces[0].shape[2]
    else:
        total, k = len(pieces), pieces[0].shape[1]
        specs = [still(p.shape) for p in pieces]
    lead = sample.shape[:-1]
    args = list(pieces)
    for i, pair in enumerate(weights):

        def at(j, s, i=i):
            return (0,) * len(lead) + (jnp.clip(j - i * per_cut, 0, per_cut - 1),)

        if paired:
            z, _, b, _ = sample.shape
            specs += [pl.BlockSpec((z, 1, b, tile), lambda j, s, h=h: (0, h, 0, j)) for h in range(2)]
            args += [pair[0], pair[0]]
        elif whole:
            specs += [pl.BlockSpec((lead[0] // 2, tile), lambda j, s, h=h: (h, j)) for h in range(2)]
            args += [pair[0], pair[0]]
        else:
            specs += [pl.BlockSpec(lead + (tile,), at)] * 2
            args += list(pair)
    if style != "bare":
        specs.append(pl.BlockSpec((1, tile), lambda j, s: (0, j)))
        args.append(bias.reshape(1, n))
    if style == "bare":
        out_specs = [pl.BlockSpec((rows, tile), lambda j, s: (0, j))] * total
        out_shape = [jax.ShapeDtypeStruct((rows, n), BF)] * total
    else:
        copies = 2 if style == "gate" else 1
        out_specs = [pl.BlockSpec((total, rows, tile), lambda j, s: (0, 0, j))] * copies
        out_shape = [jax.ShapeDtypeStruct((total, rows, n), BF)] * copies
    return kernel_call(
        functools.partial(forward_kernel, style, len(pieces), spread, cuts, per_cut),
        [start],
        (n // tile,),
        specs,
        args,
        out_specs,
        out_shape,
        cost(2 * total * rows * k * n, 2 * (total * rows * (k + n) + k * n)),
        hold,
    )


def back_kernel(style, count, shares, per_half, start_ref, *refs):
    pieces, weights, rest = refs[:count], refs[count : count + 2 * shares], refs[count + 2 * shares :]
    late = pl.program_id(0) >= per_half
    chosen = []
    for i in range(shares):
        w0, w1 = weights[2 * i][...], weights[2 * i + 1][...]
        if len(w0.shape) == 5:
            w0, w1 = in_order(w0), in_order(w1)
        elif len(w0.shape) == 4:
            w0, w1 = w0[0, 0], w1[0, 0]
        chosen.append(jnp.where(late, w1, w0))
    views = []
    for ref in pieces:
        views += [ref] if len(ref.shape) == 2 else [ref.at[i] for i in range(ref.shape[0])]
    width = chosen[0].shape[1]
    total = None
    for at, view in enumerate(views):
        value = dot(view[:, :width], chosen[0], 1, 1)
        for i in range(1, shares):
            value = value + dot(view[:, i * width : (i + 1) * width], chosen[i], 1, 1)
        if style == "slope":
            low = (value * rest[0][at].astype(F32)).astype(BF)
            rest[1][at] = low
            part = jnp.sum(low.astype(F32), axis=0, keepdims=True)
            total = part if total is None else total + part
        elif style == "plain":
            rest[0][at] = value.astype(BF)
        else:
            rest[at][...] = value.astype(BF)
    if style == "slope":
        rest[2][...] = total


def back_product(pieces, weights, start, style="plain", slope=None, pick=None, rows=512, hold=()):
    shares = len(weights)
    sample = weights[0][0]
    k = sample.shape[-1]
    half_rows = 1
    for d in sample.shape[:-1]:
        half_rows *= d
    whole = len(weights[0]) == 1
    if whole:
        half_rows //= 2
    n = 2 * half_rows
    tile = min(half_rows, TILE)
    per_half = half_rows // tile
    stack = pieces[0].ndim == 3
    if stack:
        total = pick[1] if pick else pieces[0].shape[0]
        specs = [still((total,) + pieces[0].shape[1:], pick[0] if pick else 0)]
    else:
        total = len(pieces)
        specs = [still(p.shape) for p in pieces]
    if sample.ndim == 4:
        tile = sample.shape[2]
        per_half = sample.shape[0]
        block = (1, 1, tile, k)
    elif sample.ndim == 5:
        h, z, t, r, _ = sample.shape
        group = max(1, tile // (z * r))
        tile = group * z * r
        per_half = half_rows // tile
        each = t // group
        block = (1, z, group, r, k)

        def at(j):
            return (j // each, 0, j % each, 0, 0)
    else:
        block = (tile, k)

        def at(j):
            return (j, 0)

    if sample.ndim == 4:
        first = pl.BlockSpec(block, lambda j, s: (jnp.minimum(j, per_half - 1), 0, 0, 0))
        second = pl.BlockSpec(block, lambda j, s: (jnp.maximum(j - per_half, 0), 1, 0, 0))
    else:
        first = pl.BlockSpec(block, lambda j, s: at(jnp.minimum(j, per_half - 1)))
        second = pl.BlockSpec(block, lambda j, s: at(jnp.maximum(j - per_half, 0) + (per_half if whole else 0)))
    args = list(pieces)
    for w in weights:
        specs += [first, second]
        args += [w[0], w[-1]]

    def column(j, s):
        return lax.rem(s[0] * per_half + j, 2 * per_half)

    stacked = pl.BlockSpec((total, rows, tile), lambda j, s: (0, 0, column(j, s)))
    stack_shape = jax.ShapeDtypeStruct((total, rows, n), BF)
    if style == "slope":
        specs.append(stacked)
        args.append(slope)
        out_specs = [stacked, pl.BlockSpec((1, tile), lambda j, s: (0, column(j, s)))]
        out_shape = [stack_shape, jax.ShapeDtypeStruct((1, n), F32)]
    elif style == "plain":
        out_specs, out_shape = [stacked], [stack_shape]
    else:
        out_specs = [pl.BlockSpec((rows, tile), lambda j, s: (0, column(j, s)))] * total
        out_shape = [jax.ShapeDtypeStruct((rows, n), BF)] * total
    return kernel_call(
        functools.partial(back_kernel, style, len(pieces), shares, per_half),
        [start],
        (2 * per_half,),
        specs,
        args,
        out_specs,
        out_shape,
        cost(2 * total * rows * k * n * shares, 2 * (total * rows * (k * shares + n) + k * n)),
        hold,
    )


def weight_kernel(left_count, right_count, start_ref, *refs):
    lefts, rights, out = refs[:left_count], refs[left_count : left_count + right_count], refs[-1]

    def views(group):
        found = []
        for ref in group:
            found += [ref] if len(ref.shape) == 2 else [ref.at[i] for i in range(ref.shape[0])]
        return found

    total = None
    for a, b in zip(views(lefts), views(rights)):
        part = dot(a[...], b[...], 0, 0)
        total = part if total is None else total + part
    low = total.astype(BF)
    if len(out.shape) == 2:
        out[...] = low
    else:
        h, z, t, r, n = out.shape
        for o in range(h):
            for i in range(t):
                base = (o * t + i) * z * r
                out[o, :, i] = low[base : base + z * r].reshape(z, r, n)


def weight_product(left, right, start, which, spread=None, cut=(0, 1, 1), tile=512, hold=()):
    def spec(group, width, index):
        found = []
        for a in group:
            if a.ndim == 2:
                found.append(pl.BlockSpec((a.shape[0], width), lambda j, s: (0, index(j, s))))
            else:
                found.append(pl.BlockSpec(a.shape[:2] + (width,), lambda j, s: (0, 0, index(j, s))))
        return found

    half = left[0].shape[-1] // (1 if which is None else 2)
    share = right[0].shape[-1] // cut[2]
    n = share * (cut[1] - cut[0])
    tile = min(tile, share)
    skip = cut[0] * (share // tile)
    rows = sum(a.shape[0] if a.ndim == 2 else a.shape[0] * a.shape[1] for a in left)
    specs = spec(left, half, lambda j, s: 0 if which is None else s[0] if which == 0 else 1 - s[0])
    specs += spec(right, tile, lambda j, s: j + skip)
    shape = (half, n) if spread is None else spread + (n,)
    block = shape[:-1] + (tile,)
    return kernel_call(
        functools.partial(weight_kernel, len(left), len(right)),
        [start],
        (n // tile,),
        specs,
        [*left, *right],
        pl.BlockSpec(block, lambda j, s: (0,) * (len(block) - 1) + (j,)),
        jax.ShapeDtypeStruct(shape, BF),
        cost(2 * rows * half * n, 2 * (rows * (half + n) + half * n)),
        hold,
    )


def pair_masks():
    lane = lax.broadcasted_iota(jnp.int32, (1, 2 * HD), 1)
    low = jnp.where(lane < HD, 1.0, 0.0).astype(BF)
    high = jnp.where(lane < HD, 0.0, 1.0).astype(BF)
    return low, high


def pair_probs(q_two, k):
    scores = dot(q_two, k, 1, 1) * 0.125
    row = lax.broadcasted_iota(jnp.int32, scores.shape, 0) & (SLOT - 1)
    column = lax.broadcasted_iota(jnp.int32, scores.shape, 1)
    scores = jnp.where(row >= column, scores, MASKED)
    exponent = jnp.exp(scores - jnp.max(scores, axis=-1, keepdims=True))
    return exponent / jnp.sum(exponent, axis=-1, keepdims=True)


def attend_kernel(q_ref, k_ref, v_ref, context_ref):
    low, high = pair_masks()
    for at in range(0, context_ref.shape[1], 2 * HD):
        q, k, v = [ref[:, at : at + 2 * HD] for ref in (q_ref, k_ref, v_ref)]
        probs = pair_probs(jnp.concatenate([q * low, q * high], axis=0), k).astype(BF)
        context = dot(probs[:SLOT], v * low, 1, 0) + dot(probs[SLOT:], v * high, 1, 0)
        context_ref[:, at : at + 2 * HD] = context.astype(BF)


def attend_back_kernel(q_ref, k_ref, v_ref, grad_ref, out_ref, sum_ref):
    part = grad_ref.shape[1]
    low, high = pair_masks()

    @pl.when(pl.program_id(0) == 0)
    def _():
        sum_ref[...] = jnp.zeros_like(sum_ref)

    for at in range(0, part, 2 * HD):
        q, k, v, grad = [ref[:, at : at + 2 * HD] for ref in (q_ref, k_ref, v_ref, grad_ref)]
        q_two = jnp.concatenate([q * low, q * high], axis=0)
        g_two = jnp.concatenate([grad * low, grad * high], axis=0)
        probs = pair_probs(q_two, k)
        d_probs = dot(g_two, v, 1, 1)
        row_dot = jnp.sum(probs * d_probs, axis=-1, keepdims=True)
        d_scores = (probs * (d_probs - row_dot)).astype(BF)
        d_q = dot(d_scores[:SLOT], k * low, 1, 0) + dot(d_scores[SLOT:], k * high, 1, 0)
        d_k = dot(d_scores, q_two, 0, 0)
        d_v = dot(probs.astype(BF), g_two, 0, 0)
        for i, value in enumerate((d_q * 0.125, d_k * 0.125, d_v)):
            where = slice(i * part + at, i * part + at + 2 * HD)
            value = value.astype(BF)
            out_ref[:, where] = value
            sum_ref[:, where] += jnp.sum(value.astype(F32), axis=0, keepdims=True)


def attend(q, k, v, hold=()):
    rows, part = q.shape
    one = pl.BlockSpec((SLOT, part), lambda i: (i, 0))
    return kernel_call(
        attend_kernel,
        [],
        (rows // SLOT,),
        [one] * 3,
        [q, k, v],
        one,
        jax.ShapeDtypeStruct((rows, part), BF),
        cost(32 * rows * SLOT * part, 8 * rows * part, rows * SLOT * part // HD),
        hold,
    )


def attend_back(q, k, v, grad, first, hold=()):
    rows, part = grad.shape
    one = pl.BlockSpec((SLOT, part), lambda i: (i, 0))
    shifted = pl.BlockSpec((SLOT, part), lambda i: (i + first, 0))
    return kernel_call(
        attend_back_kernel,
        [],
        (rows // SLOT,),
        [shifted] * 3 + [one],
        [q, k, v, grad],
        [pl.BlockSpec((SLOT, 3 * part), lambda i: (i, 0)), still((1, 3 * part))],
        [jax.ShapeDtypeStruct((rows, 3 * part), BF), jax.ShapeDtypeStruct((1, 3 * part), F32)],
        cost(80 * rows * SLOT * part, 14 * rows * part, rows * SLOT * part // HD),
        hold,
    )


def normal_of(values):
    centred = values - jnp.mean(values, axis=-1, keepdims=True)
    inverse = lax.rsqrt(jnp.mean(centred * centred, axis=-1, keepdims=True) + EPSILON)
    return centred * inverse, inverse


def rows_of(refs):
    total = refs[0][...].astype(F32)
    for ref in refs[1:]:
        total = total + ref[...].astype(F32)
    return total


def norm_kernel(x_ref, gain_ref, shift_ref, out_ref):
    normal, _ = normal_of(x_ref[...].astype(F32))
    out_ref[...] = (normal * gain_ref[...] + shift_ref[...]).astype(BF)


def join_norm_kernel(count, *refs):
    bias, gain, shift, hidden_ref, out_ref = refs[count:]
    hidden = rows_of(refs[:count]) + bias[...]
    hidden_ref[...] = hidden
    normal, _ = normal_of(hidden)
    out_ref[...] = (normal * gain[...] + shift[...]).astype(BF)


def join_kernel(count, *refs):
    refs[count + 1][...] = (rows_of(refs[:count]) + refs[count][...]).astype(BF)


def norm_back_kernel(count, *refs):
    source, carry, gain, grad_ref, low_ref, sums = refs[count:]
    grad = rows_of(refs[:count])
    normal, inverse = normal_of(source[...].astype(F32))
    scaled = grad * gain[...]
    centre = jnp.mean(scaled, axis=-1, keepdims=True)
    projected = jnp.mean(scaled * normal, axis=-1, keepdims=True)
    carried = carry[...].astype(F32)
    result = carried + inverse * (scaled - centre - normal * projected)
    grad_ref[...] = result.astype(grad_ref.dtype)
    low = result.astype(BF)
    low_ref[...] = low

    @pl.when(pl.program_id(0) == 0)
    def _():
        sums[...] = jnp.zeros_like(sums)

    for i, value in enumerate((grad * normal, grad, low.astype(F32), carried)):
        sums[i : i + 1] += jnp.sum(value, axis=0, keepdims=True)


def add_kernel(a_ref, b_ref, out_ref):
    out_ref[...] = (a_ref[...].astype(F32) + b_ref[...].astype(F32)).astype(BF)


def add_low(a, b, hold=()):
    width = a.shape[-1]
    flat = [x.reshape(-1, width) for x in (a, b)]
    rows = flat[0].shape[0]
    step = min(rows, 256)
    one = pl.BlockSpec((step, width), lambda i: (i, 0))
    result = kernel_call(
        add_kernel,
        [],
        (rows // step,),
        [one, one],
        flat,
        one,
        jax.ShapeDtypeStruct((rows, width), BF),
        cost(rows * width, 6 * rows * width),
        hold,
    )
    return result.reshape(a.shape)


def row_call(kernel, blocks, vectors, outs, sums=0, step=128, hold=()):
    rows, width = blocks[0].shape
    one = pl.BlockSpec((step, width), lambda i: (i, 0))
    out_specs = [one] * len(outs)
    out_shape = [jax.ShapeDtypeStruct((rows, width), d) for d in outs]
    if sums:
        out_specs.append(still((sums, width)))
        out_shape.append(jax.ShapeDtypeStruct((sums, width), F32))
    return kernel_call(
        kernel,
        [],
        (rows // step,),
        [one] * len(blocks) + [still((1, width))] * len(vectors),
        [*blocks, *[v.reshape(1, width) for v in vectors]],
        out_specs,
        out_shape,
        cost(20 * rows * width, 16 * rows * width),
        hold,
    )


def body(
    tokens,
    cotangent,
    doc_starts,
    active_len,
    ln1_gain,
    ln1_bias,
    q_weight,
    q_bias,
    k_weight,
    v_weight,
    v_bias,
    o_weight,
    o_bias,
    ln2_gain,
    ln2_bias,
    up_weight,
    up_bias,
    down_weight,
    down_bias,
):
    depth = lax.axis_size("fsdp")
    outer = lax.axis_size("outer")
    devices = outer * TEAM * depth
    member, me = lax.axis_index("team"), lax.axis_index("outer")
    layer = lax.axis_index("fsdp")
    start = (me if outer == 2 else jnp.zeros_like(me)).reshape(1)
    groups, row_len, width = tokens.shape
    docs = doc_starts.shape[1]
    r = q_weight.shape[0]
    part_width = width // TEAM
    rows = groups * docs * SLOT

    zero_bias = jnp.zeros((part_width,), F32)

    def depth_gather(a):
        return lax.all_gather(a, "fsdp", axis=0, tiled=True)

    def columns(a, i, n):
        c = a.shape[1] // n
        return a[:, i * c : (i + 1) * c]

    def stored(block):
        return block.reshape(1, depth, TEAM, r, block.shape[1])

    def flat(block):
        return block[None]

    def both_halves(block, *hold):
        return outer_halves(pin(block, *hold) if hold else block, me)

    def flatten(halves):
        return [h.reshape(-1, h.shape[-1]) for h in halves]

    deal = deal_columns((q_weight, k_weight, v_weight, up_weight), member, outer, depth)
    qkv_deal, up_deal = deal[:, : 3 * part_width], deal[:, 3 * part_width :]
    block_q, block_k, block_v = [stored(depth_gather(columns(qkv_deal, i, 3))) for i in range(3)]
    w_q, w_k = [both_halves(b) for b in (block_q, block_k)]
    block_o = flat(depth_gather(o_weight))

    vectors = (ln1_gain, ln1_bias, o_bias, ln2_gain, ln2_bias, down_bias, q_bias, v_bias, up_bias)
    packed = gather_small(jnp.concatenate(vectors), member, me, layer)
    edges = [0]
    for v in vectors:
        edges.append(edges[-1] + v.shape[0])
    pieces = [packed[:, edges[i] : edges[i + 1]] for i in range(len(vectors))]
    gain1, shift1, bias_o, gain2, shift2, bias_down = [p.reshape(-1) for p in pieces[:6]]

    def member_part(p):
        whole = p.reshape(outer, TEAM, depth, -1)
        return lax.dynamic_index_in_dim(whole, member, 1, False).reshape(-1)

    bias_q, bias_v, bias_up = [member_part(p) for p in pieces[6:]]

    position = jnp.arange(row_len, dtype=jnp.int32)
    offset = jnp.arange(SLOT, dtype=jnp.int32)
    wanted = doc_starts[:, :, None] + offset
    live = offset < active_len[:, :, None]
    chosen = (wanted[..., None] == position) & live[..., None]
    chosen = chosen.reshape(groups, docs * SLOT, row_len)
    select = chosen.astype(BF)
    covered = jnp.any(chosen, axis=1)

    def pack(source):
        picked = jnp.einsum("gst,gtd->gsd", select, source, preferred_element_type=F32)
        return picked.reshape(rows, width).astype(BF)

    def unpack(slot_rows, fallback):
        blocks = slot_rows.reshape(groups, docs * SLOT, width)
        placed = jnp.einsum("gst,gsd->gtd", select, blocks, preferred_element_type=F32).astype(BF)
        return jnp.where(covered[..., None], placed, fallback)

    class Order:
        last = ()

        def step(self, kernel, *args, hold=(), **kw):
            result = kernel(*args, hold=self.last + tuple(hold), **kw)
            self.last = (jax.tree.leaves(result)[-1],)
            return result

    order = Order()

    def begin(weights):
        return jnp.zeros_like(start) if len(weights[0]) == 1 and outer != 2 else start

    def forward(pieces, weights, *rest, **kw):
        return order.step(forward_product, pieces, weights, begin(weights), *rest, rows=rows, **kw)

    def back(pieces, weights, **kw):
        return order.step(back_product, pieces, weights, begin(weights), rows=rows, **kw)

    def weight_grad(left, right, which, **kw):
        return order.step(weight_product, left, right, start, which, **kw)

    def by_rows(kernel, blocks, *args, **kw):
        return order.step(row_call, kernel, blocks, *args, **kw)

    def add(a, b, **kw):
        return order.step(add_low, a, b, **kw)

    def team_gather(own, *hold):
        across = team_swap(own, 2)
        if hold:
            across = pin(across, *hold)
        return [own, across, team_swap(own, 1), team_swap(across, 1)]

    def send_far(parts):
        return [team_swap(p, 1) for p in parts]

    def join_near(near, far, **kw):
        across = add(near[1], far[1], **kw)
        return [near[0], far[0], team_swap(across, 2), across]

    x_rows = pack(tokens)
    (a_own,) = by_rows(norm_kernel, [x_rows], [gain1, shift1], [BF])
    a_own = pin(a_own, block_o)
    a_across = team_swap(a_own, 2)
    w_o = flatten(both_halves(block_o))
    g_rows = pack(cotangent)
    a_across = pin(a_across, w_q[1], w_o[1], g_rows)
    a_all = [a_own, a_across, team_swap(a_own, 1), team_swap(a_across, 1)]
    block_up = [stored(depth_gather(columns(up_deal, i, 2))) for i in range(2)]
    g_all = team_gather(pin(g_rows, a_all[1]))

    wide = TEAM * rows
    q = forward(a_all, [w_q], bias_q)[0]
    k = forward(a_all, [w_k], zero_bias)[0]
    w_v = both_halves(block_v, q)
    v = forward(a_all, [w_v], bias_v)[0]
    q, k, v = [s.reshape(wide, part_width) for s in (q, k, v)]
    context = order.step(attend, q, k, v, hold=[g_all[1]]).reshape(TEAM, rows, part_width)
    if outer == 2:
        down_pair = jnp.stack([down_weight, outer_pass(pin(down_weight, k))])[None]
        w_down = [[depth_gather(pin(down_pair, context))]]
    else:
        w_down = [[lax.all_gather(down_weight, SPREAD, axis=0, tiled=True)]]
    o_far = send_far(forward([context], [w_o], style="bare", pick=(1, 2)))
    o_near = forward([context], [w_o], style="bare", pick=(0, 2))
    w_up = [both_halves(block_up[0], context)]
    *o_parts, o_across = join_near(o_near, o_far)
    hidden, b_own = by_rows(
        functools.partial(join_norm_kernel, 4),
        [x_rows] + o_parts,
        [bias_o, gain2, shift2],
        [F32, BF],
        hold=[w_up[0][1]],
    )
    w_up.append(both_halves(block_up[1], b_own))
    b_all = team_gather(b_own, w_up[1][1])

    active, slope = forward(b_all, w_up, bias_up, style="gate")

    def depth_scatter(a):
        return lax.psum_scatter(a, "fsdp", scatter_dimension=0, tiled=True)

    def send_away(away, *hold):
        if outer != 2:
            return away
        return outer_pass(pin(away, *hold) if hold else away)

    def settle(sent, mine, **kw):
        c = mine.shape[-1]
        if outer == 2:
            total = add(sent, mine, **kw)
        else:
            both = jnp.concatenate([mine.reshape(outer // 2, -1, c), sent.reshape(outer // 2, -1, c)])
            total = outer_scatter(both, me)
        return depth_scatter(total.reshape(-1, c))

    spread = (outer // 2, depth, TEAM, r)

    def settle_whole(grad):
        return lax.psum_scatter(grad, SPREAD, scatter_dimension=0, tiled=True)

    grad_down = [settle_whole(weight_grad([active], g_all, None, cut=(0, 1, 2)))]
    grad_down.append(settle_whole(weight_grad([active], g_all, None, cut=(1, 2, 2))))
    d_inner, sum_inner = back(g_all, w_down, style="slope", slope=slope)
    n_far = send_far(back([d_inner], w_up, style="bare", pick=(1, 2)))
    n_near = back([d_inner], w_up, style="bare", pick=(0, 2))
    n_parts = join_near(n_near, n_far)[:3]
    up_sent = [
        send_away(weight_grad(b_all, [d_inner], 1, spread=spread, cut=(i, i + 1, 2))) for i in range(2)
    ]
    up_mine = [weight_grad(b_all, [d_inner], 0, spread=spread, cut=(i, i + 1, 2)) for i in range(2)]
    d_hidden, d_out, sums2 = by_rows(
        functools.partial(norm_back_kernel, 3), n_parts + [hidden, g_rows], [gain2], [F32, BF], sums=4
    )
    y_far = send_far(forward([active], w_down, style="bare", pick=(1, 2), hold=[grad_down[0]]))
    y_near = forward([active], w_down, style="bare", pick=(0, 2))
    d_out_all = team_gather(d_out, up_sent[0], y_near[1])

    (d_near,) = back(d_out_all[:2], [w_o])
    (d_far,) = back(d_out_all[2:], [w_o])
    grad_up = [settle(up_sent[0], up_mine[0], hold=[grad_down[1]])]
    *y_parts, y_across = join_near(y_near, y_far)
    q_far, sum_far = order.step(attend_back, q, k, v, d_far.reshape(2 * rows, -1), 2 * rows // SLOT)
    q_far = q_far.reshape(2, rows, -1)
    a_far = send_far(back([q_far], [w_q, w_k, w_v], style="bare"))
    o_sent = send_away(weight_grad([context], d_out_all, 1))
    o_mine = weight_grad([context], d_out_all, 0)
    grad_up.append(settle(up_sent[1], up_mine[1]))
    q_near, sum_near = order.step(attend_back, q, k, v, d_near.reshape(2 * rows, -1), 0, hold=[grad_up[0]])
    q_near = q_near.reshape(2, rows, -1)
    grad_o = settle(o_sent, o_mine)
    a_near = back([q_near], [w_q, w_k, w_v], style="bare")
    a_parts = join_near(a_near, a_far, hold=[y_parts[2]])[:3]
    parts = ((0, 1, 3), (1, 3, 3))
    d_both = [q_near, q_far]
    qkv_sent = [
        send_away(weight_grad(a_all, d_both, 1, spread=spread, cut=parts[0], hold=[grad_up[1]])),
        send_away(weight_grad(a_all, d_both, 1, spread=spread, cut=parts[1], hold=[grad_o])),
    ]
    grad_q = settle(qkv_sent[0], weight_grad(a_all, d_both, 0, spread=spread, cut=parts[0]))
    kv_mine = weight_grad(a_all, d_both, 0, spread=spread, cut=parts[1])
    (y_rows,) = by_rows(functools.partial(join_kernel, 4), [hidden] + y_parts, [bias_down], [BF])
    layer_out = unpack(y_rows, tokens)
    _, d_input, sums1 = by_rows(
        functools.partial(norm_back_kernel, 3),
        a_parts + [x_rows, d_hidden],
        [gain1],
        [BF, BF],
        sums=4,
        hold=[layer_out],
    )
    grad_kv = settle(qkv_sent[1], kv_mine)
    sum_qkv = sum_far + sum_near
    grad_o = grad_o.astype(F32)
    input_grad = unpack(d_input, cotangent)
    grad_down = jnp.concatenate([g.astype(F32) for g in grad_down], axis=1)
    (grad_up,) = return_columns(jnp.concatenate(grad_up, axis=1), member, outer, depth, 1)
    (grad_q,) = return_columns(grad_q, member, outer, depth, 1)
    grad_k, grad_v = return_columns(grad_kv, member, outer, depth, 2)

    whole_sums = [sums1[0], sums1[1], sums2[2], sums2[0], sums2[1], sums2[3]]
    part_sums = [sum_qkv[0, :part_width], sum_qkv[0, 2 * part_width :], sum_inner[0]]
    is_mine = (jnp.arange(TEAM) == member)[None, :, None, None]

    def widen(s):
        blocks = s.reshape(outer, 1, depth, -1)
        return jnp.where(is_mine, blocks, 0.0).reshape(devices, -1)

    table = jnp.concatenate([s.reshape(devices, -1) for s in whole_sums] + [widen(s) for s in part_sums], axis=1)
    small = reduce_small(table, member, me, layer)
    cuts = [small[edges[i] : edges[i + 1]] for i in range(len(vectors))]
    g_gain1, g_shift1, g_bias_o, g_gain2, g_shift2, g_bias_down, g_bias_q, g_bias_v, g_bias_up = cuts
    return (
        layer_out,
        input_grad,
        g_gain1,
        g_shift1,
        grad_q,
        g_bias_q,
        grad_k,
        grad_v,
        g_bias_v,
        grad_o,
        g_bias_o,
        g_gain2,
        g_shift2,
        grad_up,
        g_bias_up,
        grad_down,
        g_bias_down,
    )


def solution(mesh):
    outer = mesh.shape["dp"] // TEAM
    devices = mesh.devices.reshape(outer, TEAM, mesh.shape["fsdp"])
    fine = Mesh(devices, ALL)
    kinds = {"t": P(ALL, None, None), "w": P(ALL, None), "v": P(ALL)}
    vectors = "vvwvwwvwvvvwvwv"
    in_specs = tuple(kinds[c] for c in "ttww" + vectors)
    out_specs = tuple(kinds[c] for c in "tt" + vectors)
    return jax.shard_map(body, mesh=fine, in_specs=in_specs, out_specs=out_specs, check_vma=False)
```
